32 devices in a mesh: ctx: 8 (over z, x), wsh: 4 (over y, core).
Axes of the slice: x: 2, y: 2, z: 4, core: 2. Of those that a mesh axis runs over, the one named last changes fastest.
Arguments:
- inputs: bfloat16 [8, 1024, 768], P('wsh', 'ctx'), may hold values from -6 to 6
- teacher: bfloat16 [8, 1024, 768], P('wsh', 'ctx'), may hold values from -6 to 6
- seq_lengths: int32 [8], P('wsh'), may hold values from 256 to 1024, as said below
- gain_attn: bfloat16 [768], P('wsh'), may hold values from 0.5 to 1.5
- w_query: bfloat16 [768, 768], P('wsh'), may hold values from -0.109375 to 0.109375
- w_key: bfloat16 [768, 768], P('wsh'), may hold values from -0.109375 to 0.109375
- w_value: bfloat16 [768, 768], P('wsh'), may hold values from -0.21875 to 0.21875
- w_out: bfloat16 [768, 768], P('wsh'), may hold values from -2.5 to 2.5
- bias_table: bfloat16 [32, 12], P('wsh'), may hold values from -4 to 4
- gain_ffn: bfloat16 [768], P('wsh'), may hold values from 0.5 to 1.5
- w_inner: bfloat16 [768, 3072], P('wsh'), may hold values from -0.21875 to 0.21875
- w_outer: bfloat16 [3072, 768], P('wsh'), may hold values from -0.109375 to 0.109375
Outputs:
- layer_out: bfloat16 [8, 1024, 768], P('wsh', 'ctx')
- loss_value: float32 [], replicated
- input_grad: float32 [8, 1024, 768], P('wsh', 'ctx')
- gain_attn_grad: float32 [768], P('wsh')
- w_query_grad: float32 [768, 768], P('wsh')
- w_key_grad: float32 [768, 768], P('wsh')
- w_value_grad: float32 [768, 768], P('wsh')
- w_out_grad: float32 [768, 768], P('wsh')
- bias_table_grad: float32 [32, 12], P('wsh')
- gain_ffn_grad: float32 [768], P('wsh')
- w_inner_grad: float32 [768, 3072], P('wsh')
- w_outer_grad: float32 [3072, 768], P('wsh')
The draws below stay inside these ranges and needn't reach their ends.
Inputs may be any that keep to these rules, and one draw needn't show every extreme that they name: `seq_lengths`: in each aligned group of 2 sequences exactly one, chosen by the seed, has all 1024 tokens valid; every other sequence has fewer.
All inputs are finite; a program needn't handle non-finite values.
Results may differ from the reference program's by a relative error of at most 0.017.
Values may be sent and summed in bfloat16 or wider, within the bound.
No kernel may reach another device: no remote copies, remote signals or barrier semaphores. Data moves between devices by JAX's collectives and lax.ppermute only.
A program may use at most 128 MiB of HBM per device.

```python
import math
import jax
import jax.numpy as jnp
from jax import lax

D = 768
H = 12
DH = 64
FF = 3072
BUCKETS = 32
SEQ_DEV = 2
NSEQ = 8
LENGTH = 1024
TOKENS = 8192


def draw_seq_lengths(key, part):
    short_key = jax.random.fold_in(key, 11)
    pick_key = jax.random.fold_in(key, 23)
    lengths = jax.random.randint(short_key, (NSEQ,), LENGTH // 4, LENGTH)
    groups = NSEQ // SEQ_DEV
    chosen = jax.random.randint(pick_key, (groups,), 0, SEQ_DEV)
    full_rows = jnp.arange(groups, dtype=jnp.int32) * SEQ_DEV + chosen
    lengths = lengths.at[full_rows].set(LENGTH)
    return lengths.astype(jnp.int32)


def block_scale(stream_key, extent, split, smallest, largest):
    level = 1.0
    for dim, shards_of in split:
        steps = jax.random.uniform(jax.random.fold_in(jax.random.fold_in(stream_key, 6), dim), (shards_of,), jnp.float32, smallest / len(split), largest / len(split))
        level = level * jnp.repeat(jnp.exp(steps), extent[dim] // shards_of).reshape((-1,) + (1,) * (len(extent) - 1 - dim))
    return level


def centred(rng, shape, spread, reach, cuts=(), held_as=jnp.bfloat16):
    values = spread * jax.random.normal(rng, shape, jnp.float32)
    if cuts:
        values = values * block_scale(rng, shape, cuts, -0.22, 0.18)
    return jnp.clip(values, -reach, reach).astype(held_as)


def setup_inputs(seed: int = 0) -> dict:
    arg_keys = jax.random.split(jax.random.key(seed), 13)
    inputs = centred(arg_keys[0], (NSEQ, LENGTH, D), 1.0, 6.0, ((0, 4), (1, 8)))
    teacher = centred(arg_keys[1], (NSEQ, LENGTH, D), 1.0, 6.0, ((0, 4), (1, 8)))
    seq_lengths = draw_seq_lengths(jax.random.fold_in(arg_keys[12], 71), 0)
    gain_attn = jnp.clip(1.0 + 0.1 * jax.random.normal(arg_keys[3], (D,), jnp.float32), 0.5, 1.5).astype(jnp.bfloat16)
    w_query = centred(arg_keys[4], (D, H * DH), (4 * D) ** -0.5, 0.109375, ((0, 4),))
    w_key = centred(arg_keys[5], (D, H * DH), (4 * D) ** -0.5, 0.109375, ((0, 4),))
    w_value = centred(arg_keys[6], (D, H * DH), D ** -0.5, 0.21875, ((0, 4),))
    w_out = centred(arg_keys[7], (H * DH, D), (max(1, D * 8 // LENGTH)) ** -0.5, 2.5, ((0, 4),))
    bias_table = centred(arg_keys[8], (BUCKETS, H), 1.0, 4.0, ((0, 4),))
    gain_ffn = jnp.clip(1.0 + 0.1 * jax.random.normal(arg_keys[9], (D,), jnp.float32), 0.5, 1.5).astype(jnp.bfloat16)
    w_inner = centred(arg_keys[10], (D, FF), D ** -0.5, 0.21875, ((0, 4),))
    w_outer = centred(arg_keys[11], (FF, D), FF ** -0.5, 0.109375, ((0, 4),))
    return {"inputs": inputs, "teacher": teacher, "seq_lengths": seq_lengths, "gain_attn": gain_attn, "w_query": w_query, "w_key": w_key, "w_value": w_value, "w_out": w_out, "bias_table": bias_table, "gain_ffn": gain_ffn, "w_inner": w_inner, "w_outer": w_outer}


EPS = 1e-06
BUCKET_EDGES = (12, 16, 23, 32, 46, 64, 91)
HIGH = lax.Precision.HIGHEST

@jax.custom_vjp
def low(v):
    return lax.optimization_barrier(v.astype(jnp.bfloat16)).astype(jnp.float32)

@jax.custom_vjp
def low_back(v):
    return v

def low_keep(v):
    return (low(v), None)

def low_pass(kept, grad):
    return (grad,)

def back_keep(v):
    return (v, None)

def back_low(kept, grad):
    return (low(grad),)
low.defvjp(low_keep, low_pass)
low_back.defvjp(back_keep, back_low)

def both_ways(value):
    return low(low_back(value))

def bucket_index(offset):
    distance = jnp.abs(offset)
    far_bucket = 8 + sum(((distance >= edge).astype(jnp.int32) for edge in BUCKET_EDGES))
    near_or_far = jnp.where(distance < 8, distance, far_bucket)
    return near_or_far + jnp.where(offset > 0, 16, 0)

def rms_scale(values, gain_vector):
    return values * lax.rsqrt(lax.optimization_barrier(jnp.mean(values * values, axis=-1, keepdims=True)) + EPS) * gain_vector

def attend_block(query_part, key_seq, value_seq, key_valid, table_weight, row_start):
    row_count = query_part.shape[0]
    scores = jnp.einsum('qhd,khd->hqk', query_part, key_seq, precision=HIGH)
    offsets = jnp.arange(LENGTH, dtype=jnp.int32)[None, :] - (row_start + jnp.arange(row_count, dtype=jnp.int32))[:, None]
    bias_terms = jnp.take(table_weight, bucket_index(offsets), axis=0)
    scores = low_back(scores + jnp.transpose(bias_terms, (2, 0, 1)))
    scores = jnp.where(key_valid[None, None, :] > 0, scores, -1e+30)
    row_max = lax.optimization_barrier(jnp.max(scores, axis=-1, keepdims=True))
    weights = jnp.exp(scores - row_max)
    weights_low = low(weights / lax.optimization_barrier(jnp.sum(weights, axis=-1, keepdims=True)))
    return jnp.einsum('hqk,khd->qhd', weights_low, value_seq, precision=HIGH)

def reference(inputs, teacher, seq_lengths, gain_attn, w_query, w_key, w_value, w_out, bias_table, gain_ffn, w_inner, w_outer):
    valid_mask = (jnp.arange(LENGTH, dtype=jnp.int32)[None, :] < seq_lengths[:, None]).astype(jnp.float32)
    teacher_rows = teacher.astype(jnp.float32).reshape(NSEQ * LENGTH, D)
    valid_rows = valid_mask.reshape(NSEQ * LENGTH, 1)
    valid_count = jnp.sum(valid_mask)
    block_rows = math.gcd(512, LENGTH)
    block_count = LENGTH // block_rows

    def objective(input_rows, attn_gain, query_weight, key_weight, value_weight, out_weight, table_weight, ffn_gain, inner_weight, outer_weight):
        normed = low(rms_scale(input_rows, attn_gain))
        queries = both_ways(jnp.dot(normed, query_weight, precision=HIGH))
        keys_all = both_ways(jnp.dot(normed, key_weight, precision=HIGH))
        values_all = both_ways(jnp.dot(normed, value_weight, precision=HIGH))
        query_blocks = queries.reshape(NSEQ * block_count, block_rows, H, DH)
        key_seqs = keys_all.reshape(NSEQ, LENGTH, H, DH)
        value_seqs = values_all.reshape(NSEQ, LENGTH, H, DH)
        seq_ids = jnp.repeat(jnp.arange(NSEQ, dtype=jnp.int32), block_count)
        row_starts = jnp.tile(jnp.arange(block_count, dtype=jnp.int32) * block_rows, NSEQ)

        def one_block(pieces):
            query_part, seq_id, row_start = pieces
            return attend_block(query_part, key_seqs[seq_id], value_seqs[seq_id], valid_mask[seq_id], table_weight, row_start)
        mixed = lax.map(jax.checkpoint(one_block), (query_blocks, seq_ids, row_starts))
        mixed = both_ways(mixed.reshape(NSEQ * LENGTH, H * DH))
        hidden = input_rows + low_back(jnp.dot(mixed, out_weight, precision=HIGH))
        normed_ffn = low(rms_scale(hidden, ffn_gain))
        inner_sum = low_back(jnp.dot(normed_ffn, inner_weight, precision=HIGH))
        active = low(jax.nn.gelu(inner_sum, approximate=False))
        result = hidden + low_back(jnp.dot(active, outer_weight, precision=HIGH))
        deviation = result - teacher_rows
        square_sum = jnp.sum(deviation * deviation * valid_rows)
        return (0.5 * TOKENS * square_sum / valid_count, (result, square_sum / (valid_count * D)))
    input_rows = inputs.astype(jnp.float32).reshape(NSEQ * LENGTH, D)
    objective_value, pull_back, auxiliary = jax.vjp(objective, input_rows, gain_attn.astype(jnp.float32), w_query.astype(jnp.float32), w_key.astype(jnp.float32), w_value.astype(jnp.float32), w_out.astype(jnp.float32), bias_table.astype(jnp.float32), gain_ffn.astype(jnp.float32), w_inner.astype(jnp.float32), w_outer.astype(jnp.float32), has_aux=True)
    grads = pull_back(jnp.ones_like(objective_value))
    result, loss_value = auxiliary
    return (result.reshape(NSEQ, LENGTH, D).astype(jnp.bfloat16), loss_value, grads[0].reshape(NSEQ, LENGTH, D), grads[1], grads[2], grads[3], grads[4], grads[5], grads[6], grads[7], grads[8], grads[9])
```

```python
import functools

import jax
import jax.numpy as jnp
from jax import lax
from jax.experimental import pallas as pl
from jax.experimental.pallas import tpu as pltpu
from jax.sharding import PartitionSpec as P

D = 768
H = 12
DH = 64
BUCKETS = 32
SEQ_DEV = 2
PIECE = 128
TP = 4
HEADS = H // TP
COLS = HEADS * DH
ROWS = SEQ_DEV * PIECE
GROUP = ROWS * TP
EPS = 1e-06
NEG_FILL = -1e30
BUCKET_EDGES = (12, 16, 23, 32, 46, 64, 91)
AXES = ("ctx", "wsh")
ORDER = (0, 2, 1, 3)

BF16 = jnp.bfloat16
F32 = jnp.float32
NT = (((1,), (1,)), ((), ()))
TN = (((0,), (0,)), ((), ()))
NN = (((1,), (0,)), ((), ()))


def dot(left, right, dims=NN):
    return lax.dot_general(left, right, dims, preferred_element_type=F32)


def swapped(index):
    return (index & 1) * 2 + (index >> 1)


def seq_routes(n_ctx):
    spread = n_ctx // (SEQ_DEV * TP)
    same, cross = [], []
    for c in range(n_ctx):
        for w in range(TP):
            pair = c // 2
            for b in range(2):
                home = (2 * swapped(w) + b) * spread + pair // TP
                route = (c * TP + w, home * TP + swapped(pair % TP))
                (same if b == c % 2 else cross).append(route)
    return same, cross


def backwards(routes):
    return [(there, here) for here, there in routes]


def to_partner(value, offset):
    return lax.ppermute(value, "wsh", [(i, i ^ offset) for i in range(TP)])


def to_ctx(value, offset):
    n_ctx = lax.axis_size("ctx")
    return lax.ppermute(value, "ctx", [(i, i ^ offset) for i in range(n_ctx)])


def pick(stack, index):
    return lax.dynamic_index_in_dim(stack, index, 0, keepdims=False)


def by_owner(pieces, me):
    stack = jnp.stack(pieces)
    return jnp.stack([pick(stack, me ^ i) for i in range(len(pieces))])


def exchange_blocks(blocks, me):
    pieces = [pick(blocks, me)]
    for offset in range(1, TP):
        pieces.append(to_partner(pick(blocks, me ^ offset), offset))
    return by_owner(pieces, me)


def gather_group(value):
    from_y = to_partner(value, 2)
    core_own = to_partner(value, 1)
    core_y = to_partner(from_y, 1)
    return jnp.concatenate([value, from_y, core_own, core_y])


def scatter_group(keep, send):
    half = keep + to_partner(send, 1).astype(F32)
    other = half[ROWS:].astype(BF16)
    return half[:ROWS] + to_partner(other, 2).astype(F32)


def reduce_ctx(parts, ctx_me):
    n_ctx = lax.axis_size("ctx")
    if n_ctx != 8:
        return lax.psum_scatter(parts.astype(BF16), "ctx", scatter_dimension=0, tiled=False).astype(F32)
    x, z = ctx_me & 1, ctx_me >> 1
    halves = parts.reshape((4, 2) + parts.shape[1:])
    mine = lax.dynamic_index_in_dim(halves, x, 1, keepdims=False)
    other = lax.dynamic_index_in_dim(halves, 1 - x, 1, keepdims=False).astype(BF16)
    half = mine.astype(F32) + to_ctx(other, 1).astype(F32)
    total = pick(half, z)
    for offset in (1, 2, 3):
        total = total + to_ctx(pick(half, z ^ offset).astype(BF16), 2 * offset).astype(F32)
    return total


def gather_ctx(chunk, ctx_me):
    n_ctx = lax.axis_size("ctx")
    chunk = chunk.astype(BF16)
    if n_ctx != 8:
        return lax.all_gather(chunk, "ctx", axis=0, tiled=False)
    x, z = ctx_me & 1, ctx_me >> 1
    half = by_owner([chunk] + [to_ctx(chunk, 2 * offset) for offset in (1, 2, 3)], z)
    both = by_owner([half, to_ctx(half, 1)], x)
    return jnp.swapaxes(both, 0, 1).reshape((n_ctx,) + chunk.shape)


def bucket_index(offset):
    distance = jnp.abs(offset)
    far_bucket = 8 + sum(((distance >= edge).astype(jnp.int32) for edge in BUCKET_EDGES))
    near_or_far = jnp.where(distance < 8, distance, far_bucket)
    return near_or_far + jnp.where(offset > 0, 16, 0)


def gelu_and_slope(values):
    scaled = values * 0.7071067811865476
    cumulative = 0.5 * (1.0 + lax.erf(scaled))
    density = jnp.exp(-0.5 * values * values) * 0.3989422804014327
    return values * cumulative, cumulative + values * density


def repeat(count, unroll, body, carry):
    if unroll:
        for index in range(count):
            carry = body(index, carry)
        return carry
    return lax.fori_loop(0, count, body, carry)


def block_bias(bias_ref, places, head, key_block, query_block, blocks):
    tiles = []
    for i in range(blocks):
        apart = places[8 + key_block] - places[query_block + i]
        tiles.append(bias_ref[head, jnp.clip(apart, -2, 2) + 2])
    return tiles[0] if blocks == 1 else jnp.concatenate(tiles, axis=1)


def attention_kernel(
    chunk, offsets, places, q_ref, kv_ref, bias_ref, out_w_ref,
    keep_ref, send_ref, attn_ref, lse_ref, s_ref, p_ref,
):
    keys = kv_ref.shape[0]
    key_blocks = keys // PIECE
    length = places[8 + key_blocks]
    k_off, v_off = offsets
    blocks = chunk // PIECE
    unroll = key_blocks <= 8
    key_iota = lax.broadcasted_iota(jnp.int32, (PIECE, 1), 0)
    for head in range(HEADS):
        lanes = slice(head * DH, head * DH + DH)
        key_part = kv_ref[:, k_off + head * DH : k_off + head * DH + DH]
        value_part = kv_ref[:, v_off + head * DH : v_off + head * DH + DH]

        def for_queries(q_chunk, carry):
            rows = pl.ds(pl.multiple_of(q_chunk * chunk, chunk), chunk)
            s_ref[...] = dot(key_part, q_ref[rows, lanes], NT)

            def score(index, top):
                at = pl.ds(pl.multiple_of(index * PIECE, PIECE), PIECE)
                tile = s_ref[at, :] + block_bias(bias_ref, places, head, index, q_chunk * blocks, blocks)
                ok = places[8 + index] * PIECE + key_iota < length
                tile = jnp.where(ok, tile, NEG_FILL)
                s_ref[at, :] = tile
                return jnp.maximum(top, jnp.max(tile, axis=0, keepdims=True))

            top = repeat(key_blocks, unroll, score, jnp.full((1, chunk), NEG_FILL, F32))

            def weigh(index, total):
                at = pl.ds(pl.multiple_of(index * PIECE, PIECE), PIECE)
                weight = jnp.exp(s_ref[at, :] - top)
                p_ref[at, :] = weight.astype(BF16)
                return total + jnp.sum(weight, axis=0, keepdims=True)

            total = repeat(key_blocks, unroll, weigh, jnp.zeros((1, chunk), F32))
            attn_ref[lanes, rows] = dot(value_part, p_ref[...], TN) / total
            lse_ref[head : head + 1, rows] = top + jnp.log(total)
            return carry

        repeat(GROUP // chunk, unroll, for_queries, 0)
    partial = dot(attn_ref[...].astype(BF16), out_w_ref[...], TN)
    keep_ref[...] = partial[: GROUP // 2]
    send_ref[...] = partial[GROUP // 2 :].astype(BF16)


def attention_back_kernel(
    chunk, offsets, places, q_ref, kv_ref, bias_ref, out_w_ref, up_ref, attn_ref, lse_ref,
    dq_ref, dkv_ref, table_ref,
    s_ref, dp_ref, p_ref, ds_ref, do_ref, outdot_ref, dqt_ref, dkv_sum, tile_ref,
):
    keys = kv_ref.shape[0]
    key_blocks = keys // PIECE
    length = places[8 + key_blocks]
    k_off, v_off = offsets
    blocks = chunk // PIECE
    unroll = key_blocks <= 8
    key_iota = lax.broadcasted_iota(jnp.int32, (PIECE, 1), 0)
    do_ref[...] = dot(up_ref[...], out_w_ref[...], NT).astype(BF16)
    do_t = dot(out_w_ref[...], up_ref[...], NT).astype(BF16).astype(F32) * attn_ref[...]
    for head in range(HEADS):
        outdot_ref[head : head + 1, :] = jnp.sum(do_t[head * DH : head * DH + DH], axis=0, keepdims=True)
    tile_ref[...] = jnp.zeros_like(tile_ref)
    dkv_sum[...] = jnp.zeros_like(dkv_sum)
    for head in range(HEADS):
        lanes = slice(head * DH, head * DH + DH)
        key_part = kv_ref[:, k_off + head * DH : k_off + head * DH + DH]
        value_part = kv_ref[:, v_off + head * DH : v_off + head * DH + DH]

        def for_queries(q_chunk, carry):
            rows = pl.ds(pl.multiple_of(q_chunk * chunk, chunk), chunk)
            query_part = q_ref[rows, lanes]
            do_part = do_ref[rows, lanes]
            s_ref[...] = dot(key_part, query_part, NT)
            dp_ref[...] = dot(value_part, do_part, NT)
            lse = lse_ref[head : head + 1, rows]
            outdot = outdot_ref[head : head + 1, rows]

            def step(index, carry):
                at = pl.ds(pl.multiple_of(index * PIECE, PIECE), PIECE)
                tile = s_ref[at, :] + block_bias(bias_ref, places, head, index, q_chunk * blocks, blocks)
                ok = places[8 + index] * PIECE + key_iota < length
                prob = jnp.exp(jnp.where(ok, tile, NEG_FILL) - lse)
                p_ref[at, :] = prob.astype(BF16)
                grad = prob * (dp_ref[at, :] - outdot)
                ds_ref[at, :] = grad.astype(BF16)
                for i in range(blocks):
                    apart = places[8 + index] - places[q_chunk * blocks + i]
                    which = jnp.clip(apart, -2, 2) + 2
                    tile_ref[head, which] += grad[:, i * PIECE : (i + 1) * PIECE]
                return carry

            repeat(key_blocks, unroll, step, 0)
            dk = dot(ds_ref[...], query_part)
            dv = dot(p_ref[...], do_part)
            k_lanes, v_lanes = lanes, slice(COLS + head * DH, COLS + head * DH + DH)
            dkv_sum[:, k_lanes] += dk
            dkv_sum[:, v_lanes] += dv
            dqt_ref[lanes, rows] = dot(key_part, ds_ref[...], TN)
            return carry

        repeat(GROUP // chunk, unroll, for_queries, 0)
    dq_ref[...] = dqt_ref[...].T.astype(BF16)
    dkv_ref[...] = dkv_sum[...].astype(BF16)
    table_ref[...] = jnp.zeros_like(table_ref)
    apart = lax.broadcasted_iota(jnp.int32, (PIECE, PIECE), 0) - lax.broadcasted_iota(
        jnp.int32, (PIECE, PIECE), 1
    )
    for head in range(HEADS):
        for which in range(5):
            tile = tile_ref[head, which]
            if which in (0, 4):
                b = 15 if which == 0 else 31
                table_ref[head, b : b + 1, :] += jnp.sum(tile, axis=0, keepdims=True)
                continue
            ids = bucket_index(apart + (which - 2) * PIECE)
            low, high = ((1, 16), (0, 32), (17, 32))[which - 1]
            for b in range(low, high):
                part = jnp.sum(jnp.where(ids == b, tile, 0.0), axis=0, keepdims=True)
                table_ref[head, b : b + 1, :] += part


def vmem():
    return pl.BlockSpec(memory_space=pltpu.VMEM)


def smem():
    return pl.BlockSpec(memory_space=pltpu.SMEM)


def shape(dims, dtype):
    return jax.ShapeDtypeStruct(dims, dtype)


PARAMS = pltpu.CompilerParams(vmem_limit_bytes=56 * 1024 * 1024)


def attention(places, q, kv, offsets, bias, out_w, chunk):
    keys = kv.shape[0]
    return pl.pallas_call(
        functools.partial(attention_kernel, chunk, offsets),
        out_shape=(
            shape((GROUP // 2, D), F32),
            shape((GROUP // 2, D), BF16),
            shape((COLS, GROUP), F32),
            shape((8, GROUP), F32),
        ),
        in_specs=[smem()] + [vmem()] * 4,
        out_specs=(vmem(),) * 4,
        scratch_shapes=[pltpu.VMEM((keys, chunk), F32), pltpu.VMEM((keys, chunk), BF16)],
        compiler_params=PARAMS,
        cost_estimate=pl.CostEstimate(
            flops=4 * GROUP * keys * COLS, bytes_accessed=8 * 2**20, transcendentals=GROUP * keys * HEADS
        ),
    )(places, q, kv, bias, out_w)


def attention_back(places, q, kv, offsets, bias, out_w, up, attn_t, lse, chunk):
    keys = kv.shape[0]
    return pl.pallas_call(
        functools.partial(attention_back_kernel, chunk, offsets),
        out_shape=(
            shape((GROUP, COLS), BF16),
            shape((keys, 2 * COLS), BF16),
            shape((HEADS, BUCKETS, PIECE), F32),
        ),
        in_specs=[smem()] + [vmem()] * 7,
        out_specs=(vmem(),) * 3,
        scratch_shapes=[
            pltpu.VMEM((keys, chunk), F32),
            pltpu.VMEM((keys, chunk), F32),
            pltpu.VMEM((keys, chunk), BF16),
            pltpu.VMEM((keys, chunk), BF16),
            pltpu.VMEM((GROUP, COLS), BF16),
            pltpu.VMEM((8, GROUP), F32),
            pltpu.VMEM((COLS, GROUP), F32),
            pltpu.VMEM((keys, 2 * COLS), F32),
            pltpu.VMEM((HEADS, 5, PIECE, PIECE), F32),
        ],
        compiler_params=PARAMS,
        cost_estimate=pl.CostEstimate(
            flops=10 * GROUP * keys * COLS, bytes_accessed=12 * 2**20, transcendentals=GROUP * keys * HEADS
        ),
    )(places, q, kv, bias, out_w, up, attn_t, lse)


def on_device(
    inputs, teacher, seq_lengths, gain_attn, w_query, w_key, w_value, w_out, bias_table, gain_ffn, w_inner, w_outer
):
    n_ctx = lax.axis_size("ctx")
    spread = n_ctx // (SEQ_DEV * TP)
    me = lax.axis_index("wsh")
    ctx_me = lax.axis_index("ctx")
    parity = ctx_me & 1
    token_total = ROWS * n_ctx * TP
    same, cross = seq_routes(n_ctx)
    home = ctx_me // spread
    stretch = ctx_me % spread
    seq_bit = home & 1

    def to_home(pair):
        near = lax.ppermute(pick(pair, parity), AXES, same)
        far = lax.ppermute(pick(pair, 1 - parity), AXES, cross)
        return near, far

    def from_home(rows):
        near = lax.ppermute(rows[:PIECE], AXES, backwards(same))
        far = lax.ppermute(rows[PIECE:], AXES, backwards(cross))
        return jnp.where(parity == 0, jnp.stack([near, far]), jnp.stack([far, near]))

    def block_places(stretch_index):
        return [
            TP * 2 * stretch_index + 2 * swapped(me ^ r) + (seq_bit ^ e) for r in ORDER for e in (0, 1)
        ]

    query_blocks = block_places(stretch)
    key_blocks = [p for i in range(spread) for p in block_places(i)] if spread > 1 else query_blocks
    length = lax.ppermute(pick(seq_lengths, parity), AXES, same)
    places = jnp.stack(query_blocks + key_blocks + [length])

    near, far = to_home(inputs)
    x_low = jnp.concatenate([near, far])
    teacher_rows = jnp.concatenate(to_home(teacher))

    counts = jnp.sum(jnp.minimum(seq_lengths, n_ctx * PIECE)).astype(F32).reshape(1, 1)
    counts = counts + to_partner(counts, 1)
    valid_count = (counts + to_partner(counts, 2))[0, 0]

    small = jnp.concatenate([gain_attn, gain_ffn, bias_table.reshape(-1)])
    small_all = by_owner([small] + [to_partner(small, r) for r in (1, 2, 3)], me)
    attn_gain = small_all[:, :192].reshape(1, D).astype(F32)
    ffn_gain = small_all[:, 192:384].reshape(1, D).astype(F32)
    table = small_all[:, 384:].reshape(BUCKETS, TP, HEADS)
    my_table = lax.dynamic_index_in_dim(table, me, 1, keepdims=False).T.astype(F32)

    qkv_blocks = (
        jnp.stack([w_query, w_key, w_value], axis=1).reshape(192, 3, TP, COLS).transpose(2, 0, 1, 3)
    ).reshape(TP, 192, 3 * COLS)
    w_qkv = exchange_blocks(qkv_blocks, me).reshape(D, 3 * COLS)
    inner_blocks = w_inner.reshape(192, TP, D).transpose(1, 0, 2)
    w_in = exchange_blocks(inner_blocks, me).reshape(D, D)

    shift = (jnp.arange(5, dtype=jnp.int32) - 2)[:, None, None] * PIECE
    spot = jnp.arange(PIECE, dtype=jnp.int32)
    buckets = bucket_index(shift + spot[None, :, None] - spot[None, None, :])
    bias = jnp.zeros((HEADS,) + buckets.shape, F32)
    for b in range(BUCKETS):
        bias = jnp.where(buckets[None] == b, my_table[:, b, None, None, None], bias)

    x_all = gather_group(x_low).astype(F32)
    normed = (x_all * lax.rsqrt(jnp.mean(x_all * x_all, axis=-1, keepdims=True) + EPS) * attn_gain).astype(BF16)
    qkv = dot(normed, w_qkv).astype(BF16)
    if spread == 1:
        q, kv, offsets = qkv, qkv, (COLS, 2 * COLS)
        chunk = 256
    else:
        teams = [[s * spread + i for i in range(spread)] for s in range(SEQ_DEV * TP)]
        q, offsets = qkv[:, :COLS], (0, COLS)
        kv = lax.all_gather(qkv[:, COLS:], "ctx", axis=0, tiled=True, axis_index_groups=teams)
        chunk = 128
    keep, send, attn_t, lse = attention(places, q, kv, offsets, bias, w_out, chunk)
    x_rows = x_low.astype(F32)
    hidden = x_rows + scatter_group(keep, send)
    ffn_scale = lax.rsqrt(jnp.mean(hidden * hidden, axis=-1, keepdims=True) + EPS)
    ffn_low = (hidden * ffn_scale * ffn_gain).astype(BF16)
    ffn_all = gather_group(ffn_low)
    inner = dot(ffn_all, w_in)
    active, slope = gelu_and_slope(inner)
    active_low = active.astype(BF16)
    partial = dot(active_low, w_outer)
    result = hidden + scatter_group(partial[: GROUP // 2], partial[GROUP // 2 :].astype(BF16))

    layer_out = from_home(result.astype(BF16))
    row_places = jnp.concatenate([query_blocks[e] * PIECE + spot for e in (0, 1)])
    row_valid = (row_places < length).astype(F32)[:, None]
    deviation = result - teacher_rows.astype(F32)
    square_sum = jnp.sum(deviation * deviation * row_valid)
    result_grad = token_total / valid_count * deviation * row_valid

    result_all = gather_group(result_grad.astype(BF16))
    active_grad = dot(result_all, w_outer, NT)
    inner_grad = (slope * active_grad).astype(BF16)
    partial = dot(inner_grad, w_in, NT)
    outer_wgrad = dot(active_low, result_all, TN)
    inner_wgrad = dot(ffn_all, inner_grad, TN)
    ffn_grad = scatter_group(partial[: GROUP // 2], partial[GROUP // 2 :].astype(BF16))
    unit = hidden * ffn_scale
    ffn_gain_grad = jnp.sum(ffn_grad * unit, axis=0)
    scaled = ffn_gain * ffn_grad
    hidden_grad = result_grad + ffn_scale * (scaled - unit * jnp.mean(scaled * unit, axis=-1, keepdims=True))
    hidden_all = gather_group(hidden_grad.astype(BF16))
    dq, dkv, table_part = attention_back(
        places, q, kv, offsets, bias, w_out, hidden_all, attn_t, lse, chunk
    )
    if spread > 1:
        dkv = lax.psum_scatter(dkv, "ctx", scatter_dimension=0, tiled=True, axis_index_groups=teams)
    d_qkv = jnp.concatenate([dq, dkv], axis=1)
    partial = dot(d_qkv, w_qkv, NT)
    out_wgrad = dot(attn_t.astype(BF16), hidden_all)
    qkv_wgrad = dot(normed, d_qkv, TN)
    normed_grad = scatter_group(partial[: GROUP // 2], partial[GROUP // 2 :].astype(BF16))
    scale = lax.rsqrt(jnp.mean(x_rows * x_rows, axis=-1, keepdims=True) + EPS)
    unit = x_rows * scale
    attn_gain_grad = jnp.sum(normed_grad * unit, axis=0)
    scaled = attn_gain * normed_grad
    input_grad = hidden_grad + scale * (scaled - unit * jnp.mean(scaled * unit, axis=-1, keepdims=True))
    input_grad = from_home(input_grad.astype(BF16)).astype(F32)

    def natural(grad):
        parts = grad.reshape((n_ctx, grad.shape[0] // n_ctx) + grad.shape[1:])
        return gather_ctx(reduce_ctx(parts, ctx_me), ctx_me).reshape(grad.shape).astype(F32)

    def columns(grad):
        cols = grad.shape[1]
        depth = 192 // n_ctx
        parts = grad.reshape(TP, n_ctx, depth, cols).transpose(1, 0, 2, 3)
        chunk_sum = reduce_ctx(parts, ctx_me).astype(BF16)
        mine = exchange_blocks(chunk_sum, me)
        rows = gather_ctx(mine.transpose(1, 0, 2), ctx_me)
        return rows.reshape(192, TP, cols).astype(F32)

    w_outer_grad = natural(outer_wgrad)
    w_inner_grad = columns(inner_wgrad).reshape(192, TP * D)
    w_out_grad = natural(out_wgrad)
    qkv_rows = columns(qkv_wgrad).reshape(192, TP, 3, COLS)
    w_query_grad, w_key_grad, w_value_grad = (qkv_rows[:, :, i].reshape(192, D) for i in range(3))

    table_part = jnp.sum(table_part, axis=-1)
    table_spread = lax.dynamic_update_slice(
        jnp.zeros((BUCKETS, TP, HEADS), F32), table_part.T[:, None, :], (0, me, 0)
    )
    totals = lax.psum(
        jnp.concatenate([attn_gain_grad, ffn_gain_grad, table_spread.reshape(-1), square_sum.reshape(1)]), AXES
    )
    my_attn_gain = lax.dynamic_slice(totals, (me * 192,), (192,))
    my_ffn_gain = lax.dynamic_slice(totals, (D + me * 192,), (192,))
    my_rows = lax.dynamic_slice(totals, (2 * D + me * 8 * H,), (8 * H,)).reshape(8, H)
    loss_value = totals[2 * D + BUCKETS * H] / (valid_count * D)
    return (
        layer_out,
        loss_value,
        input_grad,
        my_attn_gain,
        w_query_grad,
        w_key_grad,
        w_value_grad,
        w_out_grad,
        my_rows,
        my_ffn_gain,
        w_inner_grad,
        w_outer_grad,
    )


def solution(mesh):
    rows = P("wsh", None)
    tokens = P("wsh", "ctx", None)
    return jax.shard_map(
        on_device,
        mesh=mesh,
        in_specs=(tokens, tokens, P("wsh"), P("wsh"), rows, rows, rows, rows, rows, P("wsh"), rows, rows),
        out_specs=(tokens, P(), tokens, P("wsh"), rows, rows, rows, rows, rows, P("wsh"), rows, rows),
        check_vma=False,
    )
```

```python
import functools

import jax
import jax.numpy as jnp
from jax import lax
from jax.experimental import pallas as pl
from jax.experimental.pallas import tpu as pltpu
from jax.sharding import PartitionSpec as P

D = 768
H = 12
DH = 64
BUCKETS = 32
SEQ_DEV = 2
PIECE = 128
TP = 4
HEADS = H // TP
COLS = HEADS * DH
OWN = D // TP
ROWS = SEQ_DEV * PIECE
GROUP = ROWS * TP
DEPTH = OWN // 8
EPS = 1e-06
NEG_FILL = -1e30
BUCKET_EDGES = (12, 16, 23, 32, 46, 64, 91)
AXES = ("ctx", "wsh")
ORDER = (0, 2, 1, 3)

ME, X, Z, SEQ_OWNER, SEQ_BIT, QUERY_BLOCKS = range(6)
KEY_BLOCKS = QUERY_BLOCKS + 8

BF16 = jnp.bfloat16
F32 = jnp.float32
NT = (((1,), (1,)), ((), ()))
TN = (((0,), (0,)), ((), ()))
NN = (((1,), (0,)), ((), ()))


def dot(left, right, dims=NN):
    return lax.dot_general(left, right, dims, preferred_element_type=F32)


def swapped(index):
    return (index & 1) * 2 + (index >> 1)


def seq_routes(n_ctx):
    spread = n_ctx // (SEQ_DEV * TP)
    same, cross = [], []
    for c in range(n_ctx):
        for w in range(TP):
            pair = c // 2
            for b in range(2):
                home = (2 * swapped(w) + b) * spread + pair // TP
                route = (c * TP + w, home * TP + swapped(pair % TP))
                (same if b == c % 2 else cross).append(route)
    return same, cross


def backwards(routes):
    return [(there, here) for here, there in routes]


def to_partner(value, offset):
    return lax.ppermute(value, "wsh", [(i, i ^ offset) for i in range(TP)])


def to_ctx(value, offset):
    n_ctx = lax.axis_size("ctx")
    return lax.ppermute(value, "ctx", [(i, i ^ offset) for i in range(n_ctx)])


def swap_blocks(blocks, axis, groups=None):
    return lax.all_to_all(blocks, axis, 0, 0, tiled=True, axis_index_groups=groups)


def pick(stack, index):
    return lax.dynamic_index_in_dim(stack, index, 0, keepdims=False)


def after(value, *earlier):
    return lax.optimization_barrier((value,) + earlier)[0]


def bucket_index(offset):
    distance = jnp.abs(offset)
    far_bucket = 8 + sum(((distance >= edge).astype(jnp.int32) for edge in BUCKET_EDGES))
    near_or_far = jnp.where(distance < 8, distance, far_bucket)
    return near_or_far + jnp.where(offset > 0, 16, 0)


def gelu_and_slope(values):
    cumulative = 0.5 * (1.0 + lax.erf(values * 0.7071067811865476))
    density = jnp.exp(-0.5 * values * values) * 0.3989422804014327
    return values * cumulative, cumulative + values * density


def inverse_rms(values):
    return lax.rsqrt(jnp.mean(values * values, axis=-1, keepdims=True) + EPS)


def norm_back(values, gain, grad):
    scale = inverse_rms(values)
    unit = values * scale
    scaled = gain * grad
    back = scale * (scaled - unit * jnp.mean(scaled * unit, axis=-1, keepdims=True))
    return back, jnp.sum(grad * unit, axis=0, keepdims=True)


def repeat(count, unroll, body, carry):
    if unroll:
        for index in range(count):
            carry = body(index, carry)
        return carry
    return lax.fori_loop(0, count, body, carry)


def vmem():
    return pl.BlockSpec(memory_space=pltpu.VMEM)


def smem():
    return pl.BlockSpec(memory_space=pltpu.SMEM)


def shape(*dims, dtype=F32):
    return jax.ShapeDtypeStruct(dims, dtype)


def hbm():
    return pl.BlockSpec(memory_space=pl.ANY)


def name_of(body):
    return (body.func if isinstance(body, functools.partial) else body).__name__


def run(here, *jobs, scratch=(), mib=10):
    args = [a for _, _, given in jobs for a in given]
    outs = [o for _, made, _ in jobs for o in made]

    def bodies(here, *refs):
        ins, rest = refs[: len(args)], refs[len(args) :]
        made, extra = rest[: len(outs)], rest[len(outs) :]
        i = o = 0
        for body, shapes, given in jobs:
            body(here, *ins[i : i + len(given)], *made[o : o + len(shapes)], *extra)
            i, o = i + len(given), o + len(shapes)

    bodies.__name__ = "_".join(name_of(body) for body, _, _ in jobs)
    results = list(call(bodies, outs, [here] + args, scratch, mib))
    return [tuple(results.pop(0) for _ in made) for _, made, _ in jobs]


def call(body, outs, args, scratch=(), mib=10, in_hbm=0):
    return pl.pallas_call(
        body,
        name=name_of(body),
        out_shape=tuple(outs),
        in_specs=[smem()] + [hbm()] * in_hbm + [vmem()] * (len(args) - 1 - in_hbm),
        out_specs=(vmem(),) * len(outs),
        scratch_shapes=tuple(scratch),
        compiler_params=pltpu.CompilerParams(vmem_limit_bytes=mib * 2**20),
    )(*args)


def blocks_kernel(here, wq_ref, wk_ref, wv_ref, gain_a_ref, gain_f_ref, table_ref, lengths_ref, *refs):
    outs, small_ref = refs[:4], refs[4]
    small_ref[...] = jnp.zeros(small_ref.shape, F32)
    small_ref[0:1, :OWN] = gain_a_ref[...].astype(F32)
    small_ref[1:2, :OWN] = gain_f_ref[...].astype(F32)
    high = lengths_ref[...] >> 7
    small_ref[2:3, :SEQ_DEV] = high.astype(F32)
    small_ref[3:4, :SEQ_DEV] = (lengths_ref[...] - high * 128).astype(F32)
    small_ref[8:16, :H] = table_ref[...].astype(F32)
    for k in range(TP):

        @pl.when(here[ME] == k)
        def _():
            for r in range(TP):
                for m, ref in enumerate((wq_ref, wk_ref, wv_ref)):
                    outs[r][:OWN, m * COLS : (m + 1) * COLS] = ref[:, (k ^ r) * COLS : (k ^ r) * COLS + COLS]

    for out in outs:
        out[OWN:] = small_ref[...].astype(BF16)


def inner_blocks_kernel(here, inner_ref, *outs):
    for r, out in enumerate(outs):
        out[...] = inner_ref[:, pl.ds(pl.multiple_of((here[ME] ^ r) * D, D), D)]


def gain_row(small_ref, row):
    return jnp.concatenate([small_ref[i, row : row + 1, :OWN] for i in range(TP)], axis=1)


def bias_kernel(longest, here, small_a, small_b, small_c, small_d, small_ref, info_ref, bias_ref):
    for r, ref in enumerate((small_a, small_b, small_c, small_d)):
        small_ref[here[ME] ^ r] = ref[OWN:].astype(F32)
    pair = lax.broadcasted_iota(jnp.int32, (1, SEQ_DEV), 1)
    length = jnp.zeros((1, 1), F32)
    count = jnp.zeros((1, 1), F32)
    for i in range(TP):
        lengths = small_ref[i, 2:3, :SEQ_DEV] * 128.0 + small_ref[i, 3:4, :SEQ_DEV]
        mine = (pair == here[SEQ_BIT]) & (here[SEQ_OWNER] == i)
        length = length + jnp.sum(jnp.where(mine, lengths, 0.0), axis=1, keepdims=True)
        count = count + jnp.sum(jnp.minimum(lengths, longest), axis=1, keepdims=True)
    info_ref[0:1, :] = jnp.broadcast_to(length, (1, 128))
    info_ref[1:2, :] = jnp.broadcast_to(count, (1, 128))
    table = jnp.concatenate([small_ref[i, 8:16, :] for i in range(TP)], axis=0)
    lane = lax.broadcasted_iota(jnp.int32, table.shape, 1)
    apart = lax.broadcasted_iota(jnp.int32, (PIECE, PIECE), 0) - lax.broadcasted_iota(
        jnp.int32, (PIECE, PIECE), 1
    )
    for head in range(HEADS):
        values = jnp.sum(jnp.where(lane == here[ME] * HEADS + head, table, 0.0), axis=1, keepdims=True)
        for tile in range(5):
            low, high = ((15, 16), (1, 16), (0, 32), (17, 32), (31, 32))[tile]
            ids = bucket_index(apart + (tile - 2) * PIECE)
            total = jnp.broadcast_to(values[low : low + 1], (PIECE, PIECE))
            for b in range(low + 1, high):
                total = jnp.where(ids == b, values[b : b + 1], total)
            bias_ref[head, tile] = total


def block_bias(bias_ref, here, head, key_block, query_block, blocks):
    tiles = []
    for i in range(blocks):
        apart = here[KEY_BLOCKS + key_block] - here[QUERY_BLOCKS + query_block + i]
        tiles.append(bias_ref[head, jnp.clip(apart, -2, 2) + 2])
    return tiles[0] if blocks == 1 else jnp.concatenate(tiles, axis=1)


def attend(chunk, offsets, here, q_ref, kv_ref, info_ref, bias_ref, attn_ref, lse_ref, s_ref, p_ref):
    key_blocks = kv_ref.shape[0] // PIECE
    length = info_ref[0:1, 0:1]
    k_off, v_off = offsets
    blocks = chunk // PIECE
    unroll = key_blocks <= 8
    key_iota = lax.broadcasted_iota(jnp.int32, (PIECE, 1), 0)
    for head in range(HEADS):
        lanes = slice(head * DH, head * DH + DH)
        key_part = kv_ref[:, k_off + head * DH : k_off + head * DH + DH]
        value_part = kv_ref[:, v_off + head * DH : v_off + head * DH + DH]

        def for_queries(q_chunk, carry):
            rows = pl.ds(pl.multiple_of(q_chunk * chunk, chunk), chunk)
            s_ref[...] = dot(key_part, q_ref[rows, lanes], NT)

            def score(index, top):
                at = pl.ds(pl.multiple_of(index * PIECE, PIECE), PIECE)
                tile = s_ref[at, :] + block_bias(bias_ref, here, head, index, q_chunk * blocks, blocks)
                ok = (here[KEY_BLOCKS + index] * PIECE + key_iota).astype(F32) < length
                tile = jnp.where(ok, tile, NEG_FILL)
                s_ref[at, :] = tile
                return jnp.maximum(top, jnp.max(tile, axis=0, keepdims=True))

            top = repeat(key_blocks, unroll, score, jnp.full((1, chunk), NEG_FILL, F32))

            def weigh(index, total):
                at = pl.ds(pl.multiple_of(index * PIECE, PIECE), PIECE)
                weight = jnp.exp(s_ref[at, :] - top)
                p_ref[at, :] = weight.astype(BF16)
                return total + jnp.sum(weight, axis=0, keepdims=True)

            total = repeat(key_blocks, unroll, weigh, jnp.zeros((1, chunk), F32))
            attn_ref[lanes, rows] = dot(value_part, p_ref[...], TN) / total
            lse_ref[head : head + 1, rows] = top + jnp.log(total)
            return carry

        repeat(GROUP // chunk, unroll, for_queries, 0)


def send_kernel(here, partial_ref, send_ref, *_):
    send_ref[...] = partial_ref[2 * ROWS :].astype(BF16)


def stack_rows(here, pieces, out_ref):
    for r, piece in enumerate(pieces):
        out_ref[pl.ds(pl.multiple_of((here[ME] ^ r) * OWN, OWN), OWN)] = piece[:OWN]


def project(here, small_ref, pieces, w_ref, normed_ref, qkv_ref):
    gain = gain_row(small_ref, 0)
    for i, piece in enumerate(pieces):
        values = piece[...].astype(F32)
        normed_ref[i * PIECE : (i + 1) * PIECE] = (values * inverse_rms(values) * gain).astype(BF16)
    qkv_ref[...] = dot(normed_ref[...], w_ref[...]).astype(BF16)


def project_kernel(here, small_ref, *refs):
    project(here, small_ref, refs[:8], *refs[8:])


def attention_kernel(chunk, offsets, here, q_ref, kv_ref, info_ref, bias_ref, out_w_ref, *refs):
    attn_ref, lse_ref, partial_ref, s_ref, p_ref = refs
    attend(chunk, offsets, here, q_ref, kv_ref, info_ref, bias_ref, attn_ref, lse_ref, s_ref, p_ref)
    partial_ref[...] = dot(attn_ref[...].astype(BF16), out_w_ref[...], TN)


def front_kernel(here, small_ref, *refs):
    pieces, (w_ref, info_ref, bias_ref, out_w_ref), (normed_ref, qkv_ref) = refs[:8], refs[8:12], refs[12:14]
    project(here, small_ref, pieces, w_ref, normed_ref, qkv_ref)
    attention_kernel(256, (COLS, 2 * COLS), here, qkv_ref, qkv_ref, info_ref, bias_ref, out_w_ref, *refs[14:])


def attend_back(
    chunk, offsets, here, q_ref, kv_ref, info_ref, bias_ref, out_w_ref, up_ref, attn_ref, lse_ref,
    table_ref, s_ref, dp_ref, p_ref, ds_ref, do_ref, outdot_ref, dqt_ref, dkv_ref, tile_ref,
):
    key_blocks = kv_ref.shape[0] // PIECE
    length = info_ref[0:1, 0:1]
    k_off, v_off = offsets
    blocks = chunk // PIECE
    unroll = key_blocks <= 8
    key_iota = lax.broadcasted_iota(jnp.int32, (PIECE, 1), 0)
    do_ref[...] = dot(up_ref[...], out_w_ref[...], NT).astype(BF16)
    do_t = dot(out_w_ref[...], up_ref[...], NT).astype(BF16).astype(F32) * attn_ref[...]
    for head in range(HEADS):
        outdot_ref[head : head + 1, :] = jnp.sum(do_t[head * DH : head * DH + DH], axis=0, keepdims=True)
    tile_ref[...] = jnp.zeros_like(tile_ref)
    dkv_ref[...] = jnp.zeros_like(dkv_ref)
    for head in range(HEADS):
        lanes = slice(head * DH, head * DH + DH)
        v_lanes = slice(COLS + head * DH, COLS + head * DH + DH)
        key_part = kv_ref[:, k_off + head * DH : k_off + head * DH + DH]
        value_part = kv_ref[:, v_off + head * DH : v_off + head * DH + DH]

        def for_queries(q_chunk, carry):
            rows = pl.ds(pl.multiple_of(q_chunk * chunk, chunk), chunk)
            query_part = q_ref[rows, lanes]
            do_part = do_ref[rows, lanes]
            s_ref[...] = dot(key_part, query_part, NT)
            dp_ref[...] = dot(value_part, do_part, NT)
            lse = lse_ref[head : head + 1, rows]
            outdot = outdot_ref[head : head + 1, rows]

            def step(index, carry):
                at = pl.ds(pl.multiple_of(index * PIECE, PIECE), PIECE)
                tile = s_ref[at, :] + block_bias(bias_ref, here, head, index, q_chunk * blocks, blocks)
                ok = (here[KEY_BLOCKS + index] * PIECE + key_iota).astype(F32) < length
                prob = jnp.exp(jnp.where(ok, tile, NEG_FILL) - lse)
                p_ref[at, :] = prob.astype(BF16)
                grad = prob * (dp_ref[at, :] - outdot)
                ds_ref[at, :] = grad.astype(BF16)
                for i in range(blocks):
                    apart = here[KEY_BLOCKS + index] - here[QUERY_BLOCKS + q_chunk * blocks + i]
                    which = jnp.clip(apart, -2, 2) + 2
                    tile_ref[head, which] += grad[:, i * PIECE : (i + 1) * PIECE]
                return carry

            repeat(key_blocks, unroll, step, 0)
            dkv_ref[:, lanes] += dot(ds_ref[...], query_part)
            dkv_ref[:, v_lanes] += dot(p_ref[...], do_part)
            dqt_ref[lanes, rows] = dot(key_part, ds_ref[...], TN)
            return carry

        repeat(GROUP // chunk, unroll, for_queries, 0)
    table_ref[...] = jnp.zeros_like(table_ref)
    apart = lax.broadcasted_iota(jnp.int32, (PIECE, PIECE), 0) - lax.broadcasted_iota(
        jnp.int32, (PIECE, PIECE), 1
    )
    for head in range(HEADS):
        for which in range(5):
            tile = tile_ref[head, which]
            if which in (0, 4):
                b = 15 if which == 0 else 31
                table_ref[head, b : b + 1, :] += jnp.sum(tile, axis=0, keepdims=True)
                continue
            ids = bucket_index(apart + (which - 2) * PIECE)
            low, high = ((1, 16), (0, 32), (17, 32))[which - 1]
            for b in range(low, high):
                part = jnp.sum(jnp.where(ids == b, tile, 0.0), axis=0, keepdims=True)
                table_ref[head, b : b + 1, :] += part


def back_scratch(keys, chunk):
    return (
        pltpu.VMEM((keys, chunk), F32),
        pltpu.VMEM((keys, chunk), F32),
        pltpu.VMEM((keys, chunk), BF16),
        pltpu.VMEM((keys, chunk), BF16),
        pltpu.VMEM((GROUP, COLS), BF16),
        pltpu.VMEM((8, GROUP), F32),
        pltpu.VMEM((COLS, GROUP), F32),
        pltpu.VMEM((keys, 2 * COLS), F32),
        pltpu.VMEM((HEADS, 5, PIECE, PIECE), F32),
    )


def join(pieces, up_ref):
    for i, piece in enumerate(pieces):
        up_ref[i * ROWS : (i + 1) * ROWS] = piece[...]


def attention_back_kernel(chunk, offsets, here, q_ref, kv_ref, info_ref, bias_ref, out_w_ref, attn_ref, lse_ref, *refs):
    pieces, (up_ref, dq_ref, dkv_low_ref, table_ref), scratch = refs[:4], refs[4:8], refs[8:]
    join(pieces, up_ref)
    attend_back(
        chunk, offsets, here, q_ref, kv_ref, info_ref, bias_ref, out_w_ref, up_ref, attn_ref, lse_ref, table_ref, *scratch
    )
    dq_ref[...] = scratch[6][...].T.astype(BF16)
    dkv_low_ref[...] = scratch[7][...].astype(BF16)


def finish_back(d_ref, w_ref, normed_ref, small_ref, gain_grad_ref, partial_ref):
    partial = dot(d_ref[...], w_ref[...], NT)
    partial_ref[...] = partial
    products = jnp.sum(partial * normed_ref[...].astype(F32), axis=0, keepdims=True)
    gain_grad_ref[...] = products / gain_row(small_ref, 0)


def back_kernel(here, qkv_ref, info_ref, bias_ref, out_w_ref, attn_ref, lse_ref, w_ref, normed_ref, small_ref, *refs):
    pieces, (up_ref, d_qkv_ref, table_ref, gain_grad_ref, partial_ref), scratch = refs[:4], refs[4:9], refs[9:]
    join(pieces, up_ref)
    attend_back(
        256, (COLS, 2 * COLS), here, qkv_ref, qkv_ref, info_ref, bias_ref, out_w_ref, up_ref, attn_ref, lse_ref,
        table_ref, *scratch,
    )
    d_qkv_ref[:, :COLS] = scratch[6][...].T.astype(BF16)
    d_qkv_ref[:, COLS:] = scratch[7][...].astype(BF16)
    finish_back(d_qkv_ref, w_ref, normed_ref, small_ref, gain_grad_ref, partial_ref)


def partial_kernel(here, d_ref, w_ref, normed_ref, small_ref, gain_grad_ref, partial_ref):
    finish_back(d_ref, w_ref, normed_ref, small_ref, gain_grad_ref, partial_ref)


def hidden_kernel(here, small_ref, near_ref, far_ref, keep_ref, core_ref, y_ref, hidden_ref, low_ref):
    rows = jnp.concatenate([near_ref[...], far_ref[...]], axis=0).astype(F32)
    hidden = rows + (keep_ref[:ROWS] + core_ref[:ROWS].astype(F32) + y_ref[...].astype(F32))
    hidden_ref[...] = hidden
    low_ref[...] = (hidden * inverse_rms(hidden) * gain_row(small_ref, 1)).astype(BF16)


def tail_kernel(here, keep_ref, core_ref, out_ref):
    first = 0 if keep_ref.shape[0] == ROWS else ROWS
    kept = keep_ref[first : first + ROWS]
    out_ref[...] = (kept + core_ref[core_ref.shape[0] - ROWS :].astype(F32)).astype(BF16)


def pair_kernel(here, near_ref, far_ref, out_ref):
    out_ref[here[X]] = near_ref[...].astype(out_ref.dtype)
    out_ref[1 - here[X]] = far_ref[...].astype(out_ref.dtype)


def fill_sums(here, attn_gain_ref, ffn_gain_ref, squares_ref, table_ref, out_ref):
    out_ref[...] = jnp.zeros(out_ref.shape, F32)
    for i, ref in enumerate((attn_gain_ref, ffn_gain_ref, squares_ref)):
        out_ref[i : i + 1] = ref[...]
    lane = lax.broadcasted_iota(jnp.int32, (BUCKETS, 128), 1)
    table = jnp.zeros((BUCKETS, 128), F32)
    for head in range(HEADS):
        values = jnp.sum(table_ref[head], axis=1, keepdims=True)
        table = table + jnp.where(lane == here[ME] * HEADS + head, values, 0.0)
    for i in range(TP):
        out_ref[8:16, i * 128 : (i + 1) * 128] = table[i * 8 : (i + 1) * 8]


def sums_kernel(here, *refs):
    fill_sums(here, *refs)


def small_out(here, info_ref, total, attn_gain_ref, ffn_gain_ref, rows_ref, loss_ref):
    for k in range(TP):

        @pl.when(here[ME] == k)
        def _():
            attn_gain_ref[...] = total[0:1, k * OWN : (k + 1) * OWN]
            ffn_gain_ref[...] = total[1:2, k * OWN : (k + 1) * OWN]
            rows_ref[...] = total[8:16, k * 128 : k * 128 + H]

    loss_ref[...] = jnp.sum(total[2:3], axis=1, keepdims=True) / (info_ref[1:2, 0:1] * D)


def small_out_kernel(here, info_ref, total_ref, *outs):
    small_out(here, info_ref, total_ref[...], *outs)


def rows_kernel(here, a_ref, b_ref, c_ref, d_ref, out_ref):
    stack_rows(here, (a_ref, b_ref, c_ref, d_ref), out_ref)


def ffn_body(values, in_ref, outer_ref, active_ref, slope_ref, keep_ref, send_ref):
    for i, ref in enumerate(values):
        rows = slice(i * ROWS, (i + 1) * ROWS)
        active, slope = gelu_and_slope(dot(ref[...], in_ref[...]))
        active_ref[rows] = active.astype(BF16)
        slope_ref[rows] = slope.astype(BF16)
    partial = dot(active_ref[...], outer_ref[...])
    keep_ref[...] = partial[:ROWS]
    send_ref[...] = partial[ROWS:].astype(BF16)


def ffn_kernel(here, own_ref, core_ref, in_ref, outer_ref, *outs):
    ffn_body((own_ref, core_ref), in_ref, outer_ref, *outs)


def loss_kernel(
    tokens, here, hidden_ref, keep_ref, core_ref, y_ref, near_ref, far_ref, info_ref,
    out_near_ref, out_far_ref, grad_ref, low_ref, square_ref,
):
    length = info_ref[0:1, 0:1]
    factor = tokens / info_ref[1:2, 0:1]
    result = hidden_ref[...] + (keep_ref[...] + core_ref[...].astype(F32) + y_ref[...].astype(F32))
    spot = lax.broadcasted_iota(jnp.int32, (PIECE, 1), 0)
    total = jnp.zeros((1, D), F32)
    for i, (teacher, out) in enumerate(((near_ref, out_near_ref), (far_ref, out_far_ref))):
        rows = slice(i * PIECE, (i + 1) * PIECE)
        part = result[rows]
        out[...] = part.astype(BF16)
        valid = ((here[QUERY_BLOCKS + i] * PIECE + spot).astype(F32) < length).astype(F32)
        deviation = (part - teacher[...].astype(F32)) * valid
        total = total + jnp.sum(deviation * deviation, axis=0, keepdims=True)
        grad = deviation * factor
        grad_ref[rows] = grad
        low_ref[rows] = grad.astype(BF16)
    square_ref[...] = total


def ffn_back_kernel(here, own_ref, core_ref, slope_ref, in_ref, outer_ref, inner_ref, keep_ref, send_ref):
    for i, ref in enumerate((own_ref, core_ref)):
        rows = slice(i * ROWS, (i + 1) * ROWS)
        grad = dot(ref[...], outer_ref[...], NT)
        inner_ref[rows] = (slope_ref[rows].astype(F32) * grad).astype(BF16)
    partial = dot(inner_ref[...], in_ref[...], NT)
    keep_ref[...] = partial[:ROWS]
    send_ref[...] = partial[ROWS:].astype(BF16)


def inner_sum(refs):
    inputs, inner = refs[:4], refs[4:6]
    at = [slice(0, ROWS), slice(ROWS, 2 * ROWS)] * 2
    return sum(dot(inputs[i][...], inner[i // 2][at[i]], TN) for i in range(4))


def outer_half(active_ref, own_ref, core_ref):
    return dot(active_ref[:ROWS], own_ref[...], TN) + dot(active_ref[ROWS:], core_ref[...], TN)


def outer_own_kernel(here, active_ref, own_ref, core_ref, out_ref):
    out_ref[...] = outer_half(active_ref, own_ref, core_ref)


def outer_kernel(here, part_ref, active_ref, own_ref, core_ref, out_ref):
    out_ref[...] = (part_ref[...] + outer_half(active_ref, own_ref, core_ref)).astype(BF16)


def outer_halves_kernel(here, part_ref, active_ref, own_ref, core_ref, send, mine, total_ref):
    total_ref[...] = part_ref[...] + outer_half(active_ref, own_ref, core_ref)
    quarter = D // 8
    for x, out in ((1 - here[X], send), (here[X], mine)):
        for z in range(4):
            start = pl.multiple_of((4 * x + z) * quarter, quarter)
            out[z] = total_ref[pl.ds(start, quarter)].astype(BF16)


def inner_kernel(here, *refs):
    refs[6][...] = inner_sum(refs).astype(BF16)


def inner_halves_kernel(here, *refs):
    send, mine, total_ref = refs[6:]
    total_ref[...] = inner_sum(refs)
    for x, out in ((1 - here[X], send), (here[X], mine)):
        for z in range(4):
            for w in range(TP):
                start = pl.multiple_of(w * OWN + (4 * x + z) * DEPTH, 8)
                out[z * TP + w] = total_ref[pl.ds(start, DEPTH)].astype(BF16)


def hidden_back_kernel(
    here, small_ref, hidden_ref, result_grad_ref, keep_ref, core_ref, y_ref, grad_ref, low_ref, gain_grad_ref
):
    upper = keep_ref[...] + core_ref[...].astype(F32) + y_ref[...].astype(F32)
    back, gain_grad_ref[...] = norm_back(hidden_ref[...], gain_row(small_ref, 1), upper)
    grad = result_grad_ref[...] + back
    grad_ref[...] = grad
    low_ref[...] = grad.astype(BF16)


def qkv_grads(normed_ref, d_qkv_ref, put):
    d_qkv = dot(normed_ref[...], d_qkv_ref[...], TN)
    for m in range(3):
        for i in range(TP):
            block = d_qkv[i * OWN : (i + 1) * OWN, m * COLS : (m + 1) * COLS]
            put(m, slice(i * COLS, (i + 1) * COLS), block)


def attention_grads_kernel(here, normed_ref, d_qkv_ref, attn_ref, up_ref, out_ref):
    def put(m, lanes, block):
        out_ref[m, :, lanes] = block.astype(BF16)

    qkv_grads(normed_ref, d_qkv_ref, put)
    out_ref[3] = dot(attn_ref[...].astype(BF16), up_ref[...]).astype(BF16)


SUM_ROWS = 16


def added(ref, other, index):
    return ref[index].astype(F32) + other[index].astype(F32)


def split_low(here, mine, came, send, keep):
    per = mine.shape[0] // 4
    low = here[Z] & 1
    for high in range(2):
        for i in range(per):
            at = high * per + i
            send[at] = added(mine, came, (2 * high + 1 - low) * per + i).astype(BF16)
            keep[at] = added(mine, came, (2 * high + low) * per + i).astype(BF16)


def split_high(here, mine, came, send, keep, *_):
    per = mine.shape[0] // 2
    high = here[Z] >> 1
    for i in range(per):
        send[i] = added(mine, came, (1 - high) * per + i).astype(BF16)
        keep[i] = added(mine, came, high * per + i).astype(BF16)


def finish(here, mine, came, chunk):
    for i in range(mine.shape[0]):
        chunk[i] = added(mine, came, i).astype(BF16)


def join_high(here, mine, came, pair):
    per = mine.shape[0]
    high = here[Z] >> 1
    for i in range(per):
        pair[high * per + i] = mine[i]
        pair[(1 - high) * per + i] = came[i]


def join_low(here, mine, came, half):
    per = mine.shape[0] // 2
    low = here[Z] & 1
    for high in range(2):
        for i in range(per):
            half[(2 * high + low) * per + i] = mine[high * per + i]
            half[(2 * high + 1 - low) * per + i] = came[high * per + i]


def outer_rows(here, half, came, out):
    rows = half.shape[1]
    for x, ref in ((here[X], half), (1 - here[X], came)):
        for z in range(4):
            out[pl.ds(pl.multiple_of((4 * x + z) * rows, 8), rows)] = ref[z].astype(F32)


def out_grads(here, attn_ref, a_ref, b_ref, c_ref, d_ref, send_ref, mine_ref, send, mine, total_ref):
    total = None
    for i, ref in enumerate((a_ref, b_ref, c_ref, d_ref)):
        part = dot(attn_ref[:, i * ROWS : (i + 1) * ROWS].astype(BF16), ref[...])
        total = part if total is None else total + part
    total_ref[...] = total
    for x, ref, out in ((1 - here[X], send_ref, send), (here[X], mine_ref, mine)):
        for z in range(4):
            for w in range(TP):
                out[z * (TP + 1) + w] = ref[z * TP + w]
            start = pl.multiple_of((4 * x + z) * DEPTH, 8)
            out[z * (TP + 1) + TP] = total_ref[pl.ds(start, DEPTH)].astype(BF16)


def inner_finish(here, mine, came, own, *others):
    own[0] = added(mine, came, here[ME]).astype(BF16)
    own[1] = added(mine, came, TP).astype(BF16)
    for r, other in enumerate(others):
        other[0] = added(mine, came, here[ME] ^ (r + 1)).astype(BF16)


def inner_collect(here, own, a_ref, b_ref, c_ref, chunk):
    for r, ref in enumerate((own, a_ref, b_ref, c_ref)):
        chunk[here[ME] ^ r] = ref[0]
    chunk[TP] = own[1]


def inner_rows(here, half, came, inner_out, out_out):
    for x, ref in ((here[X], half), (1 - here[X], came)):
        for z in range(4):
            rows = pl.ds(pl.multiple_of((4 * x + z) * DEPTH, 8), DEPTH)
            for w in range(TP):
                inner_out[rows, w * D : (w + 1) * D] = ref[z * (TP + 1) + w].astype(F32)
            out_out[rows] = ref[z * (TP + 1) + TP].astype(F32)


def send_sums(total, send):
    last = send.shape[0]
    high = total.astype(BF16)
    send[last - 2, :SUM_ROWS] = high
    send[last - 1, :SUM_ROWS] = (total - high.astype(F32)).astype(BF16)


def take_sums(sums, came):
    last = came.shape[0]
    return sums[...] + (came[last - 2, :SUM_ROWS].astype(F32) + came[last - 1, :SUM_ROWS].astype(F32))


def qkv_halves_kernel(
    here, normed_ref, d_qkv_ref, attn_gain_ref, ffn_gain_ref, squares_ref, table_ref, send, mine, sums, total_ref
):
    fill_sums(here, attn_gain_ref, ffn_gain_ref, squares_ref, table_ref, sums)
    send_sums(sums[...], send)

    def put(m, lanes, block):
        total_ref[m, :, lanes] = block

    qkv_grads(normed_ref, d_qkv_ref, put)
    for x, out in ((1 - here[X], send), (here[X], mine)):
        for z in range(4):
            start = pl.multiple_of((4 * x + z) * DEPTH, 8)
            for m in range(3):
                out[z * 3 + m] = total_ref[m, pl.ds(start, DEPTH), :].astype(BF16)


def qkv_low(here, mine, sums, came, send, keep, total):
    split_low(here, mine, came, send, keep)
    total[...] = take_sums(sums, came)
    send_sums(total[...], send)


def qkv_high(here, mine, sums, came, send, keep, total):
    split_high(here, mine, came, send, keep)
    total[...] = take_sums(sums, came)
    send_sums(total[...], send)


def qkv_finish(here, mine, sums, came, own, a_ref, b_ref, c_ref, total):
    total[...] = take_sums(sums, came)
    for ref in (a_ref, b_ref, c_ref):
        send_sums(total[...], ref)
    for k in range(TP):

        @pl.when(here[ME] == k)
        def _():
            for m in range(3):
                values = added(mine, came, m).astype(BF16)
                for r, ref in enumerate((own, a_ref, b_ref, c_ref)):
                    ref[m, :, :COLS] = values[:, (k ^ r) * COLS : (k ^ r) * COLS + COLS]


def qkv_collect(here, info_ref, own, sums, a_ref, b_ref, c_ref, chunk, *outs):
    total = take_sums(sums, a_ref)
    for ref in (b_ref, c_ref):
        last = ref.shape[0]
        total = total + (ref[last - 2, :SUM_ROWS].astype(F32) + ref[last - 1, :SUM_ROWS].astype(F32))
    small_out(here, info_ref, total, *outs)
    for k in range(TP):

        @pl.when(here[ME] == k)
        def _():
            for m in range(3):
                for r, ref in enumerate((own, a_ref, b_ref, c_ref)):
                    chunk[m, :, (k ^ r) * COLS : (k ^ r) * COLS + COLS] = ref[m, :, :COLS]


def qkv_rows(here, half, came, *outs):
    for x, ref in ((here[X], half), (1 - here[X], came)):
        for z in range(4):
            for m, out in enumerate(outs):
                out[pl.ds(pl.multiple_of((4 * x + z) * DEPTH, 8), DEPTH)] = ref[z * 3 + m].astype(F32)


def input_kernel(
    here, small_ref, near_ref, far_ref, hidden_grad_ref, keep_ref, core_ref, y_ref,
    out_near_ref, out_far_ref,
):
    values = jnp.concatenate([near_ref[...], far_ref[...]], axis=0).astype(F32)
    upper = keep_ref[:ROWS] + core_ref[:ROWS].astype(F32) + y_ref[...].astype(F32)
    back, _ = norm_back(values, gain_row(small_ref, 0), upper)
    grad = (hidden_grad_ref[...] + back).astype(BF16)
    out_near_ref[...] = grad[:PIECE]
    out_far_ref[...] = grad[PIECE:]


def on_device(
    inputs, teacher, seq_lengths, gain_attn, w_query, w_key, w_value, w_out, bias_table, gain_ffn, w_inner, w_outer
):
    n_ctx = lax.axis_size("ctx")
    spread = n_ctx // (SEQ_DEV * TP)
    me = lax.axis_index("wsh")
    ctx_me = lax.axis_index("ctx")
    parity = ctx_me & 1
    token_total = ROWS * n_ctx * TP
    same, cross = seq_routes(n_ctx)
    home = ctx_me // spread
    stretch = ctx_me % spread
    seq_bit = home & 1
    by_steps = n_ctx == 8

    def halves(pair):
        return pick(pair, parity), pick(pair, 1 - parity)

    def to_home(pair):
        return lax.ppermute(pair[0], AXES, same), lax.ppermute(pair[1], AXES, cross)

    def from_home(near, far):
        near = lax.ppermute(near, AXES, backwards(same))
        far = lax.ppermute(far, AXES, backwards(cross))
        return near, far

    def own_pair(pair, dtype):
        return call(pair_kernel, (shape(SEQ_DEV, PIECE, D, dtype=dtype),), (here,) + pair)[0]

    def block_places(stretch_index):
        return [
            TP * 2 * stretch_index + 2 * swapped(me ^ r) + (seq_bit ^ e) for r in ORDER for e in (0, 1)
        ]

    query_blocks = block_places(stretch)
    key_blocks = [p for i in range(spread) for p in block_places(i)] if spread > 1 else query_blocks

    scalars = [me, parity, (ctx_me >> 1) & 3, swapped(home >> 1), seq_bit] + query_blocks + key_blocks
    here = jnp.stack([jnp.asarray(v, jnp.int32) for v in scalars])

    low = functools.partial(shape, dtype=BF16)
    x_halves = halves(inputs)
    x_near, x_far = to_home(x_halves)
    teacher_halves = halves(teacher)
    qkv_blocks = call(
        blocks_kernel,
        (low(OWN + 16, 3 * COLS),) * 4,
        (
            here, after(w_query, x_halves[0]), w_key, w_value, gain_attn.reshape(1, OWN), gain_ffn.reshape(1, OWN),
            bias_table, seq_lengths.reshape(1, SEQ_DEV),
        ),
        scratch=(pltpu.VMEM((16, 3 * COLS), F32),),
    )

    def group_blocks(values):
        return (values[0],) + tuple(to_partner(values[r], r) for r in (1, 2, 3))

    w_qkv_pieces = group_blocks(qkv_blocks)
    (small, info, bias), (w_qkv,) = run(
        here,
        (
            functools.partial(bias_kernel, float(n_ctx * PIECE)),
            (shape(TP, 16, 3 * COLS), shape(8, 128), shape(HEADS, 5, PIECE, PIECE)),
            w_qkv_pieces,
        ),
        (rows_kernel, (low(D, 3 * COLS),), w_qkv_pieces),
    )

    x_own = (after(x_near, w_qkv), after(x_far, w_qkv))
    inner_blocks = call(inner_blocks_kernel, (low(OWN, D),) * 4, (here, after(w_inner, x_own[1])))
    x_y = tuple(to_partner(v, 2) for v in x_own)
    pieces = x_own + x_y + tuple(to_partner(v, 1) for v in x_own + x_y)
    attn_shapes = (shape(COLS, GROUP), shape(8, GROUP), shape(GROUP, D))
    send_job = (send_kernel, (low(2 * ROWS, D),))
    proj_shapes = (low(GROUP, D), low(GROUP, 3 * COLS))

    def attn_scratch(keys, chunk):
        return (pltpu.VMEM((keys, chunk), F32), pltpu.VMEM((keys, chunk), BF16))

    if spread == 1:
        normed, qkv, attn_t, lse, partial = call(
            front_kernel,
            proj_shapes + attn_shapes,
            (here, small) + pieces + (w_qkv, info, bias, w_out),
            scratch=attn_scratch(GROUP, 256),
            mib=14,
        )
    else:
        teams = [[s * spread + i for i in range(spread)] for s in range(SEQ_DEV * TP)]
        normed, qkv = call(project_kernel, proj_shapes, (here, small) + pieces + (w_qkv,))
        kv = lax.all_gather(qkv[:, COLS:], "ctx", axis=0, tiled=True, axis_index_groups=teams)
        q = qkv[:, :COLS]
        attn_t, lse, partial = call(
            functools.partial(attention_kernel, 128, (0, COLS)),
            attn_shapes,
            (here, q, kv, info, bias, w_out),
            scratch=attn_scratch(kv.shape[0], 128),
            mib=56,
        )

    def scatter_tail(keep_y, from_core):
        return call(tail_kernel, (low(ROWS, D),), (here, keep_y, from_core))[0]

    w_in_pieces = group_blocks(inner_blocks)
    teacher_near, teacher_far = to_home([after(v, x_y[1]) for v in teacher_halves])
    (send,), (w_in,) = run(
        here, send_job + ((partial,),), (rows_kernel, (low(D, D),), w_in_pieces)
    )
    core = to_partner(send, 1)
    going = scatter_tail(partial, core)
    across = to_partner(going, 2)
    partial, teacher_near, teacher_far = lax.optimization_barrier((partial, teacher_near, teacher_far))
    hidden, ffn_low = call(
        hidden_kernel,
        (shape(ROWS, D), low(ROWS, D)),
        (here, small, x_near, x_far, partial, core, across),
    )

    def gathered(value):
        from_y = to_partner(value, 2)
        return to_partner(value, 1), from_y

    def both_halves(first_call, second_call, value):
        from_core, from_y = gathered(value)
        first, done = first_call((value, from_core))
        core_y = to_partner(after(from_y, done), 1)
        second = second_call((from_y, core_y))
        core_own = to_partner(first[-1], 1)
        going = scatter_tail(second[-2], to_partner(second[-1], 1))
        across = to_partner(going, 2)
        return (value, from_core, from_y, core_y), first, second, (first[-2], core_own, across), going

    half = low(2 * ROWS, D)
    piece_shapes = (shape(ROWS, D), low(ROWS, D))
    def ffn(values):
        return call(ffn_kernel, (half, half) + piece_shapes, (here,) + values + (w_in, w_outer))

    def ffn_first(values):
        outs = ffn(values)
        return outs, outs[-1]

    ffn_all, (active_a, slope_a, *_), (active_b, slope_b, *_), parts, _ = both_halves(ffn_first, ffn, ffn_low)
    out_near, out_far, result_grad, result_low, squares = call(
        functools.partial(loss_kernel, float(token_total)),
        (low(PIECE, D), low(PIECE, D), shape(ROWS, D), low(ROWS, D), shape(1, D)),
        (here, hidden) + parts + (teacher_near, teacher_far, info),
    )

    depth = OWN // n_ctx

    def parts_of(count, rows=DEPTH):
        return low(count, rows, D)

    def ffn_back(values, slope):
        return call(ffn_back_kernel, (half,) + piece_shapes, (here,) + values + (slope, w_in, w_outer))

    def ffn_back_first(values):
        outs = ffn_back(values, slope_a)
        (part,) = call(
            outer_own_kernel, (shape(D, D),), (here, after(active_a, outs[-1])) + values, mib=12
        )
        grads.append(part)
        return outs, part

    def ffn_back_second(values):
        args = (here, grads[0], active_b) + values
        if by_steps:
            outs = (parts_of(4, D // 8),) * 2
            grads[:] = call(outer_halves_kernel, outs, args, scratch=(pltpu.VMEM((D, D), F32),), mib=14)
        else:
            grads[:] = call(outer_kernel, (low(D, D),), args, mib=12)
        return ffn_back((after(values[0], grads[0]), values[1]), slope_b)

    grads = []
    result_all, (inner_a, *_), (inner_b, *_), parts, going = both_halves(
        ffn_back_first, ffn_back_second, result_low
    )
    layer_pair = from_home(out_near, out_far)
    inner_args = (here,) + ffn_all + (inner_a, after(inner_b, going))
    ahead = []
    if by_steps:
        outer_send, outer_mine = grads
        outer_came = to_ctx(outer_send, 1)
        inner_send, inner_mine = call(
            inner_halves_kernel, (parts_of(4 * TP),) * 2, inner_args, scratch=(pltpu.VMEM((D, D), F32),), mib=14
        )
        ordered = inner_send
        ahead.append((split_low, (parts_of(2, D // 8),) * 2, (outer_mine, outer_came)))
    else:
        (outer_wgrad,) = grads
        (inner_wgrad,) = call(inner_kernel, (low(D, D),), inner_args, mib=14)
        ordered = inner_wgrad
    (hidden_grad, hidden_low, ffn_gain_grad), (layer_out,), *ahead = run(
        here,
        (
            hidden_back_kernel,
            (shape(ROWS, D), low(ROWS, D), shape(1, D)),
            (small, after(hidden, ordered), result_grad) + parts,
        ),
        (pair_kernel, (low(SEQ_DEV, PIECE, D),), layer_pair),
        *ahead,
    )
    from_core, from_y = gathered(hidden_low)
    up_pieces = (hidden_low, from_y, from_core, to_partner(from_y, 1))
    table_shape = shape(HEADS, BUCKETS, PIECE)
    if by_steps:
        ((outer_send, outer_keep),) = ahead
        outer_came = to_ctx(outer_send, 2)
        (inner_send, inner_mine), (outer_send, outer_keep) = run(
            here,
            (
                out_grads,
                (parts_of(4 * TP + 4),) * 2,
                (attn_t,) + up_pieces + (inner_send, inner_mine),
            ),
            (split_high, (parts_of(1, D // 8),) * 2, (outer_keep, outer_came)),
            scratch=(pltpu.VMEM((OWN, D), F32),),
        )
        inner_came = to_ctx(inner_send, 1)
        outer_came = to_ctx(outer_send, 4)
        up_pieces = (after(hidden_low, outer_keep),) + up_pieces[1:]
    if spread == 1:
        hidden_all, d_qkv, table_part, attn_gain_grad, partial = call(
            back_kernel,
            (low(GROUP, D), proj_shapes[1], table_shape, shape(1, D), shape(GROUP, D)),
            (here, qkv, info, bias, w_out, attn_t, lse, w_qkv, normed, small) + up_pieces,
            scratch=back_scratch(GROUP, 256),
            mib=20,
        )
    else:
        hidden_all, dq, dkv, table_part = call(
            functools.partial(attention_back_kernel, 128, (0, COLS)),
            (low(GROUP, D), low(GROUP, COLS), low(kv.shape[0], 2 * COLS), table_shape),
            (here, q, kv, info, bias, w_out, attn_t, lse) + up_pieces,
            scratch=back_scratch(kv.shape[0], 128),
            mib=60,
        )
        dkv = lax.psum_scatter(dkv, "ctx", scatter_dimension=0, tiled=True, axis_index_groups=teams)
        d_qkv = jnp.concatenate([dq, dkv], axis=1)
        attn_gain_grad, partial = call(
            partial_kernel, (shape(1, D), shape(GROUP, D)), (here, d_qkv, w_qkv, normed, small)
        )
    if by_steps:
        (send,), (outer_chunk,), (inner_send, inner_keep) = run(
            here,
            send_job + ((partial,),),
            (finish, (parts_of(1, D // 8),), (outer_keep, outer_came)),
            (split_low, (parts_of(2 * TP + 2),) * 2, (inner_mine, inner_came)),
        )
        outer_came = to_ctx(outer_chunk, 4)
        inner_came = to_ctx(inner_send, 2)
    else:
        ((send,),) = run(here, send_job + ((partial,),))
    core = to_partner(send, 1)
    input_job = (
        input_kernel,
        (low(PIECE, D), low(PIECE, D)),
        (small, x_near, x_far, hidden_grad, partial, core),
    )
    small_shapes = (shape(1, OWN), shape(1, OWN), shape(8, H), shape(1, 1))
    sums_shape = shape(SUM_ROWS, D)
    pair_out = (shape(SEQ_DEV, PIECE, D),)
    sum_args = (attn_gain_grad, ffn_gain_grad, squares, table_part)

    if by_steps:
        going = scatter_tail(partial, core)
        across = to_partner(going, 2)
        qkv_send, qkv_mine, sums = call(
            qkv_halves_kernel,
            (parts_of(12 + 2), parts_of(12), sums_shape),
            (here, normed, after(d_qkv, going)) + sum_args,
            scratch=(pltpu.VMEM((3, OWN, D), F32),),
        )
        qkv_came = to_ctx(qkv_send, 1)
        (inner_send, inner_keep), (outer_pair,) = run(
            here,
            (split_high, (parts_of(TP + 1),) * 2, (after(inner_keep, qkv_send), inner_came)),
            (join_high, (parts_of(2, D // 8),), (outer_chunk, outer_came)),
        )
        inner_came = to_ctx(inner_send, 4)
        outer_came = to_ctx(outer_pair, 2)
        ((in_near, in_far),) = run(
            here, (input_job[0], input_job[1], input_job[2] + (after(across, inner_keep),))
        )
        input_pair = from_home(in_near, in_far)
        (qkv_send, qkv_keep, sums), inner_blocks, (outer_half,) = run(
            here,
            (qkv_low, (parts_of(6 + 2), parts_of(6), sums_shape), (qkv_mine, sums, after(qkv_came, in_near))),
            (inner_finish, (parts_of(2),) + (parts_of(1),) * 3, (inner_keep, inner_came)),
            (join_low, (parts_of(4, D // 8),), (outer_pair, outer_came)),
        )
        qkv_came = to_ctx(qkv_send, 2)
        inner_blocks = group_blocks(inner_blocks)
        outer_came = to_ctx(outer_half, 1)
        (qkv_send, qkv_keep, sums), (inner_chunk,) = run(
            here,
            (qkv_high, (parts_of(3 + 2), parts_of(3), sums_shape), (qkv_keep, sums, qkv_came)),
            (inner_collect, (parts_of(TP + 1),), inner_blocks),
        )
        qkv_came = to_ctx(qkv_send, 4)
        inner_came = to_ctx(inner_chunk, 4)
        (*qkv_blocks, sums), (inner_pair,), (w_outer_grad,) = run(
            here,
            (qkv_finish, (parts_of(3),) + (parts_of(3 + 2),) * 3 + (sums_shape,), (qkv_keep, sums, qkv_came)),
            (join_high, (parts_of(2 * TP + 2),), (inner_chunk, inner_came)),
            (outer_rows, (shape(D, D),), (outer_half, outer_came)),
        )
        qkv_own, *qkv_others = group_blocks(qkv_blocks)
        inner_came = to_ctx(inner_pair, 2)
        (qkv_chunk, my_attn_gain, my_ffn_gain, my_rows, loss_value), (inner_half,), (input_grad,) = run(
            here,
            (qkv_collect, (parts_of(3),) + small_shapes, (info, qkv_own, sums) + tuple(qkv_others)),
            (join_low, (parts_of(4 * TP + 4),), (inner_pair, inner_came)),
            (pair_kernel, pair_out, input_pair),
        )
        qkv_came = to_ctx(qkv_chunk, 4)
        inner_came = to_ctx(inner_half, 1)
        ((qkv_pair,),) = run(here, (join_high, (parts_of(6),), (qkv_chunk, qkv_came)))
        qkv_came = to_ctx(qkv_pair, 2)
        ((qkv_half,),) = run(here, (join_low, (parts_of(12),), (qkv_pair, qkv_came)))
        qkv_came = to_ctx(qkv_half, 1)
        ((w_inner_grad, w_out_grad),) = run(
            here,
            (inner_rows, (shape(OWN, TP * D), shape(OWN, D)), (after(inner_half, qkv_half), inner_came)),
        )
        ((w_query_grad, w_key_grad, w_value_grad),) = run(
            here, (qkv_rows, (shape(OWN, D),) * 3, (after(qkv_half, w_out_grad), qkv_came))
        )
    else:
        across = to_partner(scatter_tail(partial, core), 2)
        ((in_near, in_far),) = run(here, (input_job[0], input_job[1], input_job[2] + (across,)))
        input_grad = own_pair(from_home(in_near, in_far), F32)
        (sums,) = call(sums_kernel, (sums_shape,), (here,) + sum_args)
        my_attn_gain, my_ffn_gain, my_rows, loss_value = call(
            small_out_kernel, small_shapes, (here, info, lax.psum(sums, AXES))
        )

        def summed(parts):
            return lax.psum_scatter(parts, "ctx", scatter_dimension=0)

        def inner_to_rows(chunk):
            return swap_blocks(chunk, "wsh").transpose(1, 0, 2).reshape(depth, TP * D)

        def attn_to_rows(chunk):
            blocks = chunk[:3].reshape(3, depth, TP, COLS).transpose(2, 0, 1, 3)
            mine = swap_blocks(blocks, "wsh").transpose(1, 2, 0, 3).reshape(3, depth, D)
            return jnp.concatenate([mine, chunk[3:]])

        (attn_wgrad,) = call(
            attention_grads_kernel, (low(4, OWN, D),), (here, normed, d_qkv, attn_t, hidden_all)
        )
        outer_full = lax.all_gather(summed(outer_wgrad.reshape(n_ctx, D // n_ctx, D)), "ctx")
        inner_parts = inner_wgrad.reshape(TP, n_ctx, depth, D).transpose(1, 0, 2, 3)
        inner_full = lax.all_gather(inner_to_rows(summed(inner_parts)), "ctx")
        attn_parts = attn_wgrad.reshape(4, n_ctx, depth, D).transpose(1, 0, 2, 3)
        attn_full = lax.all_gather(attn_to_rows(summed(attn_parts)), "ctx")
        w_outer_grad = outer_full.reshape(D, D).astype(F32)
        w_inner_grad = inner_full.reshape(OWN, TP * D).astype(F32)
        w_query_grad, w_key_grad, w_value_grad, w_out_grad = (
            attn_full[:, m].reshape(OWN, D).astype(F32) for m in range(4)
        )

    return (
        layer_out,
        loss_value.reshape(()),
        input_grad,
        my_attn_gain.reshape(-1),
        w_query_grad,
        w_key_grad,
        w_value_grad,
        w_out_grad,
        my_rows,
        my_ffn_gain.reshape(-1),
        w_inner_grad,
        w_outer_grad,
    )


def solution(mesh):
    rows = P("wsh", None)
    tokens = P("wsh", "ctx", None)
    return jax.shard_map(
        on_device,
        mesh=mesh,
        in_specs=(tokens, tokens, P("wsh"), P("wsh"), rows, rows, rows, rows, rows, P("wsh"), rows, rows),
        out_specs=(tokens, P(), tokens, P("wsh"), rows, rows, rows, rows, rows, P("wsh"), rows, rows),
        check_vma=False,
    )
```

```python
import functools

import jax
import jax.numpy as jnp
from jax import lax
from jax.experimental import pallas as pl
from jax.experimental.pallas import tpu as pltpu
from jax.sharding import PartitionSpec as P

D = 768
H = 12
DH = 64
BUCKETS = 32
SEQ_DEV = 2
PIECE = 128
TP = 4
HEADS = H // TP
COLS = HEADS * DH
OWN = D // TP
ROWS = SEQ_DEV * PIECE
GROUP = ROWS * TP
DEPTH = OWN // 8
START_MIB = 60
EPS = 1e-06
NEG_FILL = -1e30
BUCKET_EDGES = (12, 16, 23, 32, 46, 64, 91)
AXES = ("ctx", "wsh")
ORDER = (0, 2, 1, 3)

ME, X, Z, SEQ_OWNER, SEQ_BIT, QUERY_BLOCKS = range(6)
KEY_BLOCKS = QUERY_BLOCKS + 8

BF16 = jnp.bfloat16
F32 = jnp.float32
NT = (((1,), (1,)), ((), ()))
TN = (((0,), (0,)), ((), ()))
NN = (((1,), (0,)), ((), ()))


def dot(left, right, dims=NN):
    return lax.dot_general(left, right, dims, preferred_element_type=F32)


def swapped(index):
    return (index & 1) * 2 + (index >> 1)


def seq_routes(n_ctx):
    spread = n_ctx // (SEQ_DEV * TP)
    same, cross = [], []
    for c in range(n_ctx):
        for w in range(TP):
            pair = c // 2
            for b in range(2):
                home = (2 * swapped(w) + b) * spread + pair // TP
                route = (c * TP + w, home * TP + swapped(pair % TP))
                (same if b == c % 2 else cross).append(route)
    return same, cross


def backwards(routes):
    return [(there, here) for here, there in routes]


def to_partner(value, offset):
    return lax.ppermute(value, "wsh", [(i, i ^ offset) for i in range(TP)])


def to_ctx(value, offset):
    n_ctx = lax.axis_size("ctx")
    return lax.ppermute(value, "ctx", [(i, i ^ offset) for i in range(n_ctx)])


def swap_blocks(blocks, axis, groups=None):
    return lax.all_to_all(blocks, axis, 0, 0, tiled=True, axis_index_groups=groups)


def pick(stack, index):
    return lax.dynamic_index_in_dim(stack, index, 0, keepdims=False)


def after(value, *earlier):
    return lax.optimization_barrier((value,) + earlier)[0]


def bucket_index(offset):
    distance = jnp.abs(offset)
    far_bucket = 8 + sum(((distance >= edge).astype(jnp.int32) for edge in BUCKET_EDGES))
    near_or_far = jnp.where(distance < 8, distance, far_bucket)
    return near_or_far + jnp.where(offset > 0, 16, 0)


def gelu_and_slope(values):
    cumulative = 0.5 * (1.0 + lax.erf(values * 0.7071067811865476))
    density = jnp.exp(-0.5 * values * values) * 0.3989422804014327
    return values * cumulative, cumulative + values * density


def inverse_rms(values):
    return lax.rsqrt(jnp.mean(values * values, axis=-1, keepdims=True) + EPS)


def norm_back(values, gain, grad):
    scale = inverse_rms(values)
    unit = values * scale
    scaled = gain * grad
    back = scale * (scaled - unit * jnp.mean(scaled * unit, axis=-1, keepdims=True))
    return back, jnp.sum(grad * unit, axis=0, keepdims=True)


def repeat(count, unroll, body, carry):
    if unroll:
        for index in range(count):
            carry = body(index, carry)
        return carry
    return lax.fori_loop(0, count, body, carry)


def vmem():
    return pl.BlockSpec(memory_space=pltpu.VMEM)


def smem():
    return pl.BlockSpec(memory_space=pltpu.SMEM)


def shape(*dims, dtype=F32):
    return jax.ShapeDtypeStruct(dims, dtype)


def hbm():
    return pl.BlockSpec(memory_space=pl.ANY)


def name_of(body):
    return (body.func if isinstance(body, functools.partial) else body).__name__


def run(here, *jobs, scratch=(), mib=10, weight=1):
    args = [a for _, _, given in jobs for a in given]
    outs = [o for _, made, _ in jobs for o in made]

    def bodies(here, *refs):
        ins, rest = refs[: len(args)], refs[len(args) :]
        made, extra = rest[: len(outs)], rest[len(outs) :]
        i = o = 0
        for body, shapes, given in jobs:
            body(here, *ins[i : i + len(given)], *made[o : o + len(shapes)], *extra)
            i, o = i + len(given), o + len(shapes)

    bodies.__name__ = "_".join(name_of(body) for body, _, _ in jobs)
    results = list(call(bodies, outs, [here] + args, scratch, mib, weight=weight))
    return [tuple(results.pop(0) for _ in made) for _, made, _ in jobs]


def call(body, outs, args, scratch=(), mib=10, in_hbm=0, weight=1):
    return pl.pallas_call(
        body,
        name=name_of(body),
        out_shape=tuple(outs),
        in_specs=[smem()] + [hbm()] * in_hbm + [vmem()] * (len(args) - 1 - in_hbm),
        out_specs=(vmem(),) * len(outs),
        scratch_shapes=tuple(scratch),
        compiler_params=pltpu.CompilerParams(vmem_limit_bytes=mib * 2**20),
        cost_estimate=pl.CostEstimate(flops=int(2e9 * weight), bytes_accessed=int(2**23 * weight), transcendentals=0),
    )(*args)


def start_kernel(
    here, x_hbm, wq_hbm, wk_hbm, wv_hbm, gain_a_hbm, gain_f_hbm, table_hbm, lengths_hbm, *refs
):
    halves, outs, small_ref = refs[:2], refs[2:6], refs[6]
    weights, (gain_a_ref, gain_f_ref, table_ref, lengths_ref), sems = refs[7:10], refs[10:14], refs[14]
    moves = [(x_hbm.at[here[X]], halves[0]), (x_hbm.at[1 - here[X]], halves[1])]
    moves += list(zip((wq_hbm, wk_hbm, wv_hbm), weights))
    moves += [(gain_a_hbm, gain_a_ref), (gain_f_hbm, gain_f_ref), (table_hbm, table_ref), (lengths_hbm, lengths_ref)]
    copies = [pltpu.make_async_copy(src, dst, sems.at[i]) for i, (src, dst) in enumerate(moves)]
    for copy in copies:
        copy.start()
    small_ref[...] = jnp.zeros(small_ref.shape, F32)
    for copy in copies:
        copy.wait()
    small_ref[0:1, :OWN] = gain_a_ref[...].astype(F32).reshape(1, OWN)
    small_ref[1:2, :OWN] = gain_f_ref[...].astype(F32).reshape(1, OWN)
    lengths = lengths_ref[...].reshape(1, SEQ_DEV)
    high = lengths >> 7
    small_ref[2:3, :SEQ_DEV] = high.astype(F32)
    small_ref[3:4, :SEQ_DEV] = (lengths - high * 128).astype(F32)
    small_ref[8:16, :H] = table_ref[...].astype(F32)
    for k in range(TP):

        @pl.when(here[ME] == k)
        def _():
            for r in range(TP):
                for m, ref in enumerate(weights):
                    outs[r][:OWN, m * COLS : (m + 1) * COLS] = ref[:, (k ^ r) * COLS : (k ^ r) * COLS + COLS]

    for out in outs:
        out[OWN:] = small_ref[...].astype(BF16)


def inner_blocks_kernel(here, inner_ref, teacher_ref, near_ref, far_ref, *outs):
    near_ref[...] = teacher_ref[here[X]]
    far_ref[...] = teacher_ref[1 - here[X]]
    for r, out in enumerate(outs):
        out[...] = inner_ref[:, pl.ds(pl.multiple_of((here[ME] ^ r) * D, D), D)]


def gain_row(small_ref, row):
    return jnp.concatenate([small_ref[i, row : row + 1, :OWN] for i in range(TP)], axis=1)


def bias_kernel(longest, here, small_a, small_b, small_c, small_d, small_ref, info_ref, bias_ref):
    for r, ref in enumerate((small_a, small_b, small_c, small_d)):
        small_ref[here[ME] ^ r] = ref[OWN:].astype(F32)
    pair = lax.broadcasted_iota(jnp.int32, (1, SEQ_DEV), 1)
    length = jnp.zeros((1, 1), F32)
    count = jnp.zeros((1, 1), F32)
    for i in range(TP):
        lengths = small_ref[i, 2:3, :SEQ_DEV] * 128.0 + small_ref[i, 3:4, :SEQ_DEV]
        mine = (pair == here[SEQ_BIT]) & (here[SEQ_OWNER] == i)
        length = length + jnp.sum(jnp.where(mine, lengths, 0.0), axis=1, keepdims=True)
        count = count + jnp.sum(jnp.minimum(lengths, longest), axis=1, keepdims=True)
    info_ref[0:1, :] = jnp.broadcast_to(length, (1, 128))
    info_ref[1:2, :] = jnp.broadcast_to(count, (1, 128))
    table = jnp.concatenate([small_ref[i, 8:16, :] for i in range(TP)], axis=0)
    lane = lax.broadcasted_iota(jnp.int32, table.shape, 1)
    apart = lax.broadcasted_iota(jnp.int32, (PIECE, PIECE), 0) - lax.broadcasted_iota(
        jnp.int32, (PIECE, PIECE), 1
    )
    for head in range(HEADS):
        values = jnp.sum(jnp.where(lane == here[ME] * HEADS + head, table, 0.0), axis=1, keepdims=True)
        for tile in range(5):
            low, high = ((15, 16), (1, 16), (0, 32), (17, 32), (31, 32))[tile]
            ids = bucket_index(apart + (tile - 2) * PIECE)
            total = jnp.broadcast_to(values[low : low + 1], (PIECE, PIECE))
            for b in range(low + 1, high):
                total = jnp.where(ids == b, values[b : b + 1], total)
            bias_ref[head, tile] = total


def block_bias(bias_ref, here, head, key_block, query_block, blocks):
    tiles = []
    for i in range(blocks):
        apart = here[KEY_BLOCKS + key_block] - here[QUERY_BLOCKS + query_block + i]
        tiles.append(bias_ref[head, jnp.clip(apart, -2, 2) + 2])
    return tiles[0] if blocks == 1 else jnp.concatenate(tiles, axis=1)


def attend(chunk, offsets, here, q_ref, kv_ref, info_ref, bias_ref, attn_ref, lse_ref, s_ref, p_ref):
    key_blocks = kv_ref.shape[0] // PIECE
    length = info_ref[0:1, 0:1]
    k_off, v_off = offsets
    blocks = chunk // PIECE
    unroll = key_blocks <= 8
    key_iota = lax.broadcasted_iota(jnp.int32, (PIECE, 1), 0)
    for head in range(HEADS):
        lanes = slice(head * DH, head * DH + DH)
        key_part = kv_ref[:, k_off + head * DH : k_off + head * DH + DH]
        value_part = kv_ref[:, v_off + head * DH : v_off + head * DH + DH]

        def for_queries(q_chunk, carry):
            rows = pl.ds(pl.multiple_of(q_chunk * chunk, chunk), chunk)
            s_ref[...] = dot(key_part, q_ref[rows, lanes], NT)

            def score(index, top):
                at = pl.ds(pl.multiple_of(index * PIECE, PIECE), PIECE)
                tile = s_ref[at, :] + block_bias(bias_ref, here, head, index, q_chunk * blocks, blocks)
                ok = (here[KEY_BLOCKS + index] * PIECE + key_iota).astype(F32) < length
                tile = jnp.where(ok, tile, NEG_FILL)
                s_ref[at, :] = tile
                return jnp.maximum(top, jnp.max(tile, axis=0, keepdims=True))

            top = repeat(key_blocks, unroll, score, jnp.full((1, chunk), NEG_FILL, F32))

            def weigh(index, total):
                at = pl.ds(pl.multiple_of(index * PIECE, PIECE), PIECE)
                weight = jnp.exp(s_ref[at, :] - top)
                p_ref[at, :] = weight.astype(BF16)
                return total + jnp.sum(weight, axis=0, keepdims=True)

            total = repeat(key_blocks, unroll, weigh, jnp.zeros((1, chunk), F32))
            attn_ref[lanes, rows] = dot(value_part, p_ref[...], TN) / total
            lse_ref[head : head + 1, rows] = top + jnp.log(total)
            return carry

        repeat(GROUP // chunk, unroll, for_queries, 0)


def send_kernel(here, partial_ref, send_ref, *_):
    send_ref[...] = partial_ref[2 * ROWS :].astype(BF16)


def stack_rows(here, pieces, out_ref):
    for r, piece in enumerate(pieces):
        out_ref[pl.ds(pl.multiple_of((here[ME] ^ r) * OWN, OWN), OWN)] = piece[:OWN]


def project(here, small_ref, pieces, w_ref, normed_ref, qkv_ref):
    gain = gain_row(small_ref, 0)
    for i, piece in enumerate(pieces):
        values = piece[...].astype(F32)
        normed_ref[i * PIECE : (i + 1) * PIECE] = (values * inverse_rms(values) * gain).astype(BF16)
    qkv_ref[...] = dot(normed_ref[...], w_ref[...]).astype(BF16)


def project_kernel(here, small_ref, *refs):
    project(here, small_ref, refs[:8], *refs[8:])


def attention_kernel(chunk, offsets, here, q_ref, kv_ref, info_ref, bias_ref, out_w_ref, *refs):
    attn_ref, lse_ref, partial_ref, s_ref, p_ref = refs
    attend(chunk, offsets, here, q_ref, kv_ref, info_ref, bias_ref, attn_ref, lse_ref, s_ref, p_ref)
    partial_ref[...] = dot(attn_ref[...].astype(BF16), out_w_ref[...], TN)


def front_kernel(here, small_ref, *refs):
    pieces, (w_ref, info_ref, bias_ref, out_w_ref), (normed_ref, qkv_ref) = refs[:8], refs[8:12], refs[12:14]
    project(here, small_ref, pieces, w_ref, normed_ref, qkv_ref)
    attention_kernel(256, (COLS, 2 * COLS), here, qkv_ref, qkv_ref, info_ref, bias_ref, out_w_ref, *refs[14:])


def attend_back(
    chunk, offsets, here, q_ref, kv_ref, info_ref, bias_ref, out_w_ref, pieces, attn_ref, lse_ref,
    tile_ref, s_ref, dp_ref, p_ref, ds_ref, do_ref, outdot_ref, dqt_ref, dkv_ref,
):
    key_blocks = kv_ref.shape[0] // PIECE
    length = info_ref[0:1, 0:1]
    k_off, v_off = offsets
    blocks = chunk // PIECE
    unroll = key_blocks <= 8
    key_iota = lax.broadcasted_iota(jnp.int32, (PIECE, 1), 0)
    for i, piece in enumerate(pieces):
        at = slice(i * ROWS, (i + 1) * ROWS)
        do_ref[at] = dot(piece[...], out_w_ref[...], NT).astype(BF16)
        do_t = dot(out_w_ref[...], piece[...], NT).astype(BF16).astype(F32) * attn_ref[:, at]
        for head in range(HEADS):
            outdot_ref[head : head + 1, at] = jnp.sum(do_t[head * DH : head * DH + DH], axis=0, keepdims=True)
    tile_ref[...] = jnp.zeros_like(tile_ref)
    dkv_ref[...] = jnp.zeros_like(dkv_ref)
    for head in range(HEADS):
        lanes = slice(head * DH, head * DH + DH)
        v_lanes = slice(COLS + head * DH, COLS + head * DH + DH)
        key_part = kv_ref[:, k_off + head * DH : k_off + head * DH + DH]
        value_part = kv_ref[:, v_off + head * DH : v_off + head * DH + DH]

        def for_queries(q_chunk, carry):
            rows = pl.ds(pl.multiple_of(q_chunk * chunk, chunk), chunk)
            query_part = q_ref[rows, lanes]
            do_part = do_ref[rows, lanes]
            s_ref[...] = dot(key_part, query_part, NT)
            dp_ref[...] = dot(value_part, do_part, NT)
            lse = lse_ref[head : head + 1, rows]
            outdot = outdot_ref[head : head + 1, rows]

            def step(index, carry):
                at = pl.ds(pl.multiple_of(index * PIECE, PIECE), PIECE)
                tile = s_ref[at, :] + block_bias(bias_ref, here, head, index, q_chunk * blocks, blocks)
                ok = (here[KEY_BLOCKS + index] * PIECE + key_iota).astype(F32) < length
                prob = jnp.exp(jnp.where(ok, tile, NEG_FILL) - lse)
                p_ref[at, :] = prob.astype(BF16)
                grad = prob * (dp_ref[at, :] - outdot)
                ds_ref[at, :] = grad.astype(BF16)
                for i in range(blocks):
                    apart = here[KEY_BLOCKS + index] - here[QUERY_BLOCKS + q_chunk * blocks + i]
                    which = jnp.clip(apart, -2, 2) + 2
                    tile_ref[head, which] += grad[:, i * PIECE : (i + 1) * PIECE]
                return carry

            repeat(key_blocks, unroll, step, 0)
            dkv_ref[:, lanes] += dot(ds_ref[...], query_part)
            dkv_ref[:, v_lanes] += dot(p_ref[...], do_part)
            dqt_ref[lanes, rows] = dot(key_part, ds_ref[...], TN)
            return carry

        repeat(GROUP // chunk, unroll, for_queries, 0)


def bucket_sums(tile_ref, head):
    apart = lax.broadcasted_iota(jnp.int32, (PIECE, PIECE), 0) - lax.broadcasted_iota(
        jnp.int32, (PIECE, PIECE), 1
    )
    bucket = lax.broadcasted_iota(jnp.int32, (BUCKETS, 128), 0)
    table = jnp.zeros((BUCKETS, 128), F32)
    for which in range(5):
        tile = tile_ref[head, which]
        low, high = ((15, 16), (1, 16), (0, 32), (17, 32), (31, 32))[which]
        ids = bucket_index(apart + (which - 2) * PIECE)
        for b in range(low, high):
            chosen = tile if high == low + 1 else jnp.where(ids == b, tile, 0.0)
            table = table + jnp.where(bucket == b, jnp.sum(chosen, axis=0, keepdims=True), 0.0)
    return table


def back_scratch(keys, chunk):
    return (
        pltpu.VMEM((keys, chunk), F32),
        pltpu.VMEM((keys, chunk), F32),
        pltpu.VMEM((keys, chunk), BF16),
        pltpu.VMEM((keys, chunk), BF16),
        pltpu.VMEM((GROUP, COLS), BF16),
        pltpu.VMEM((8, GROUP), F32),
        pltpu.VMEM((COLS, GROUP), F32),
        pltpu.VMEM((keys, 2 * COLS), F32),
    )


def join_kernel(here, *refs):
    for i, piece in enumerate(refs[:4]):
        refs[4][i * ROWS : (i + 1) * ROWS] = piece[...]


def attention_back_kernel(chunk, offsets, here, q_ref, kv_ref, info_ref, bias_ref, out_w_ref, attn_ref, lse_ref, *refs):
    pieces, (dq_ref, dkv_low_ref, tile_ref), scratch = refs[:4], refs[4:7], refs[7:]
    attend_back(
        chunk, offsets, here, q_ref, kv_ref, info_ref, bias_ref, out_w_ref, pieces, attn_ref, lse_ref, tile_ref,
        *scratch,
    )
    dq_ref[...] = scratch[6][...].T.astype(BF16)
    dkv_low_ref[...] = scratch[7][...].astype(BF16)


def back_kernel(here, qkv_ref, info_ref, bias_ref, out_w_ref, attn_ref, lse_ref, w_ref, *refs):
    pieces, (d_qkv_ref, tile_ref, partial_ref), scratch = refs[:4], refs[4:7], refs[7:]
    attend_back(
        256, (COLS, 2 * COLS), here, qkv_ref, qkv_ref, info_ref, bias_ref, out_w_ref, pieces, attn_ref, lse_ref,
        tile_ref, *scratch,
    )
    d_qkv_ref[:, :COLS] = scratch[6][...].T.astype(BF16)
    d_qkv_ref[:, COLS:] = scratch[7][...].astype(BF16)
    partial_ref[...] = dot(d_qkv_ref[...], w_ref[...], NT)


def partial_kernel(here, d_ref, w_ref, partial_ref):
    partial_ref[...] = dot(d_ref[...], w_ref[...], NT)


def hidden_kernel(here, small_ref, near_ref, far_ref, keep_ref, core_ref, y_ref, hidden_ref, low_ref):
    rows = jnp.concatenate([near_ref[...], far_ref[...]], axis=0).astype(F32)
    hidden = rows + (keep_ref[:ROWS] + core_ref[:ROWS].astype(F32) + y_ref[...].astype(F32))
    hidden_ref[...] = hidden
    low_ref[...] = (hidden * inverse_rms(hidden) * gain_row(small_ref, 1)).astype(BF16)


def tail_kernel(here, keep_ref, core_ref, out_ref):
    first = 0 if keep_ref.shape[0] == ROWS else ROWS
    kept = keep_ref[first : first + ROWS]
    out_ref[...] = (kept + core_ref[core_ref.shape[0] - ROWS :].astype(F32)).astype(BF16)


def pair_kernel(here, near_ref, far_ref, layer_ref, grad_ref):
    for place, ref in ((here[X], near_ref), (1 - here[X], far_ref)):
        layer_ref[place] = ref[0]
        grad_ref[place] = ref[1].astype(F32)


def sums_kernel(here, partial_ref, normed_ref, small_ref, ffn_gain_ref, squares_ref, tile_ref, out_ref):
    out_ref[...] = jnp.zeros(out_ref.shape, F32)
    products = jnp.sum(partial_ref[...] * normed_ref[...].astype(F32), axis=0, keepdims=True)
    out_ref[0:1] = products / gain_row(small_ref, 0)
    out_ref[1:2] = ffn_gain_ref[...]
    out_ref[2:3] = squares_ref[...]
    lane = lax.broadcasted_iota(jnp.int32, (BUCKETS, 128), 1)
    table = jnp.zeros((BUCKETS, 128), F32)
    for head in range(HEADS):
        values = jnp.sum(bucket_sums(tile_ref, head), axis=1, keepdims=True)
        table = table + jnp.where(lane == here[ME] * HEADS + head, values, 0.0)
    for i in range(TP):
        out_ref[8:16, i * 128 : (i + 1) * 128] = table[i * 8 : (i + 1) * 8]


def small_out(here, info_ref, total, attn_gain_ref, ffn_gain_ref, rows_ref, loss_ref):
    for k in range(TP):

        @pl.when(here[ME] == k)
        def _():
            attn_gain_ref[...] = total[0:1, k * OWN : (k + 1) * OWN]
            ffn_gain_ref[...] = total[1:2, k * OWN : (k + 1) * OWN]
            rows_ref[...] = total[8:16, k * 128 : k * 128 + H]

    loss_ref[...] = jnp.sum(total[2:3], axis=1, keepdims=True) / (info_ref[1:2, 0:1] * D)


def small_out_kernel(here, info_ref, total_ref, *outs):
    small_out(here, info_ref, total_ref[...], *outs)


def rows_kernel(here, a_ref, b_ref, c_ref, d_ref, out_ref):
    stack_rows(here, (a_ref, b_ref, c_ref, d_ref), out_ref)


def ffn_body(values, in_ref, outer_ref, active_ref, slope_ref, keep_ref, send_ref):
    for i, ref in enumerate(values):
        rows = slice(i * ROWS, (i + 1) * ROWS)
        active, slope = gelu_and_slope(dot(ref[...], in_ref[...]))
        active_ref[rows] = active.astype(BF16)
        slope_ref[rows] = slope.astype(BF16)
    partial = dot(active_ref[...], outer_ref[...])
    keep_ref[...] = partial[:ROWS]
    send_ref[...] = partial[ROWS:].astype(BF16)


def ffn_kernel(here, own_ref, core_ref, in_ref, outer_ref, *outs):
    ffn_body((own_ref, core_ref), in_ref, outer_ref, *outs)


def loss_kernel(
    tokens, here, hidden_ref, keep_ref, core_ref, y_ref, near_ref, far_ref, info_ref,
    out_near_ref, out_far_ref, grad_ref, low_ref, square_ref,
):
    length = info_ref[0:1, 0:1]
    factor = tokens / info_ref[1:2, 0:1]
    result = hidden_ref[...] + (keep_ref[...] + core_ref[...].astype(F32) + y_ref[...].astype(F32))
    spot = lax.broadcasted_iota(jnp.int32, (PIECE, 1), 0)
    total = jnp.zeros((1, D), F32)
    for i, (teacher, out) in enumerate(((near_ref, out_near_ref), (far_ref, out_far_ref))):
        rows = slice(i * PIECE, (i + 1) * PIECE)
        part = result[rows]
        out[...] = part.astype(BF16)
        valid = ((here[QUERY_BLOCKS + i] * PIECE + spot).astype(F32) < length).astype(F32)
        deviation = (part - teacher[...].astype(F32)) * valid
        total = total + jnp.sum(deviation * deviation, axis=0, keepdims=True)
        grad = deviation * factor
        grad_ref[rows] = grad
        low_ref[rows] = grad.astype(BF16)
    square_ref[...] = total


def ffn_back_kernel(here, own_ref, core_ref, slope_ref, in_ref, outer_ref, inner_ref, keep_ref, send_ref):
    for i, ref in enumerate((own_ref, core_ref)):
        rows = slice(i * ROWS, (i + 1) * ROWS)
        grad = dot(ref[...], outer_ref[...], NT)
        inner_ref[rows] = (slope_ref[rows].astype(F32) * grad).astype(BF16)
    partial = dot(inner_ref[...], in_ref[...], NT)
    keep_ref[...] = partial[:ROWS]
    send_ref[...] = partial[ROWS:].astype(BF16)


def inner_sum(refs):
    inputs, inner = refs[:4], refs[4:6]
    at = [slice(0, ROWS), slice(ROWS, 2 * ROWS)] * 2
    return sum(dot(inputs[i][...], inner[i // 2][at[i]], TN) for i in range(4))


def outer_half(active_ref, own_ref, core_ref):
    return dot(active_ref[:ROWS], own_ref[...], TN) + dot(active_ref[ROWS:], core_ref[...], TN)


def outer_own_kernel(here, active_ref, own_ref, core_ref, out_ref):
    out_ref[...] = outer_half(active_ref, own_ref, core_ref)


def outer_kernel(here, part_ref, active_ref, own_ref, core_ref, out_ref):
    out_ref[...] = (part_ref[...] + outer_half(active_ref, own_ref, core_ref)).astype(BF16)


def outer_halves_kernel(here, part_ref, active_ref, own_ref, core_ref, send, mine, total_ref):
    total_ref[...] = part_ref[...] + outer_half(active_ref, own_ref, core_ref)
    quarter = D // 8
    for x, out in ((1 - here[X], send), (here[X], mine)):
        for z in range(4):
            start = pl.multiple_of((4 * x + z) * quarter, quarter)
            out[z] = total_ref[pl.ds(start, quarter)].astype(BF16)


def inner_kernel(here, *refs):
    refs[6][...] = inner_sum(refs).astype(BF16)


def inner_halves_kernel(here, *refs):
    send, mine, total_ref = refs[6:]
    total_ref[...] = inner_sum(refs)
    for x, out in ((1 - here[X], send), (here[X], mine)):
        for z in range(4):
            for w in range(TP):
                start = pl.multiple_of(w * OWN + (4 * x + z) * DEPTH, 8)
                out[z * TP + w] = total_ref[pl.ds(start, DEPTH)].astype(BF16)


def hidden_back_kernel(
    here, small_ref, hidden_ref, result_grad_ref, keep_ref, core_ref, y_ref, grad_ref, low_ref, gain_grad_ref
):
    upper = keep_ref[...] + core_ref[...].astype(F32) + y_ref[...].astype(F32)
    back, gain_grad_ref[...] = norm_back(hidden_ref[...], gain_row(small_ref, 1), upper)
    grad = result_grad_ref[...] + back
    grad_ref[...] = grad
    low_ref[...] = grad.astype(BF16)


def qkv_grads(normed_ref, d_qkv_ref, put):
    d_qkv = dot(normed_ref[...], d_qkv_ref[...], TN)
    for m in range(3):
        for i in range(TP):
            block = d_qkv[i * OWN : (i + 1) * OWN, m * COLS : (m + 1) * COLS]
            put(m, slice(i * COLS, (i + 1) * COLS), block)


def attention_grads_kernel(here, normed_ref, d_qkv_ref, attn_ref, up_ref, out_ref):
    def put(m, lanes, block):
        out_ref[m, :, lanes] = block.astype(BF16)

    qkv_grads(normed_ref, d_qkv_ref, put)
    out_ref[3] = dot(attn_ref[...].astype(BF16), up_ref[...]).astype(BF16)


SUM_ROWS = 16


def added(ref, other, index):
    return ref[index].astype(F32) + other[index].astype(F32)


def split_low(here, mine, came, send, keep):
    per = mine.shape[0] // 4
    low = here[Z] & 1
    for high in range(2):
        for i in range(per):
            at = high * per + i
            send[at] = added(mine, came, (2 * high + 1 - low) * per + i).astype(BF16)
            keep[at] = added(mine, came, (2 * high + low) * per + i).astype(BF16)


def split_high(here, mine, came, send, keep, *_):
    per = mine.shape[0] // 2
    high = here[Z] >> 1
    for i in range(per):
        send[i] = added(mine, came, (1 - high) * per + i).astype(BF16)
        keep[i] = added(mine, came, high * per + i).astype(BF16)


def finish(here, mine, came, chunk):
    for i in range(mine.shape[0]):
        chunk[i] = added(mine, came, i).astype(BF16)


def join_high(here, mine, came, pair, per=1):
    high = here[Z] >> 1
    for i in range(per):
        pair[high * per + i] = mine[i]
        pair[(1 - high) * per + i] = came[i]


def join_low(here, mine, came, half, per=1):
    low = here[Z] & 1
    for high in range(2):
        for i in range(per):
            half[(2 * high + low) * per + i] = mine[high * per + i]
            half[(2 * high + 1 - low) * per + i] = came[high * per + i]


def outer_rows(here, half, came, out):
    rows = half.shape[1]
    for x, ref in ((here[X], half), (1 - here[X], came)):
        for z in range(4):
            out[pl.ds(pl.multiple_of((4 * x + z) * rows, 8), rows)] = ref[z].astype(F32)


def send_sums(total, send):
    last = send.shape[0] - 1
    high = total.astype(BF16)
    low = (total - high.astype(F32)).astype(BF16)
    send[last, :8] = high[:8]
    send[last, 8:16] = low[:8]
    send[last, 16:, : TP * 128] = high[8:, : TP * 128]


def sums_of(came):
    last = came.shape[0] - 1
    top = came[last, :8].astype(F32) + came[last, 8:16].astype(F32)
    return jnp.concatenate([top, came[last, 16:].astype(F32)], axis=0)


def out_grads(here, attn_ref, a_ref, b_ref, c_ref, d_ref, send_ref, mine_ref, send, mine, total_ref):
    total = None
    for i, ref in enumerate((a_ref, b_ref, c_ref, d_ref)):
        part = dot(attn_ref[:, i * ROWS : (i + 1) * ROWS].astype(BF16), ref[...])
        total = part if total is None else total + part
    total_ref[...] = total
    for x, ref, out in ((1 - here[X], send_ref, send), (here[X], mine_ref, mine)):
        for z in range(4):
            for w in range(TP):
                out[z * (TP + 1) + w] = ref[z * TP + w]
            start = pl.multiple_of((4 * x + z) * DEPTH, 8)
            out[z * (TP + 1) + TP] = total_ref[pl.ds(start, DEPTH)].astype(BF16)


def inner_finish(here, mine, came, sums, own, *others):
    own[0] = added(mine, came, here[ME]).astype(BF16)
    own[1] = added(mine, came, TP).astype(BF16)
    for r, other in enumerate(others):
        other[0] = added(mine, came, here[ME] ^ (r + 1)).astype(BF16)
        send_sums(sums[...], other)


def inner_collect(here, own, a_ref, b_ref, c_ref, sums, chunk, total):
    for r, ref in enumerate((own, a_ref, b_ref, c_ref)):
        chunk[here[ME] ^ r] = ref[0]
    chunk[TP] = own[1]
    value = sums[...]
    for ref in (a_ref, b_ref, c_ref):
        value = value + sums_of(ref)
    total[...] = value
    send_sums(value, chunk)


def inner_high(here, chunk, came, sums, pair, total):
    join_high(here, chunk, came, pair, TP + 1)
    total[...] = sums[...] + sums_of(came)
    send_sums(total[...], pair)


def inner_low(here, pair, came, sums, half, total):
    join_low(here, pair, came, half, TP + 1)
    total[...] = sums[...] + sums_of(came)
    send_sums(total[...], half)


def inner_rows(here, info_ref, half, came, sums, inner_out, out_out, *small):
    for x, ref in ((here[X], half), (1 - here[X], came)):
        for z in range(4):
            rows = pl.ds(pl.multiple_of((4 * x + z) * DEPTH, 8), DEPTH)
            for w in range(TP):
                inner_out[rows, w * D : (w + 1) * D] = ref[z * (TP + 1) + w].astype(F32)
            out_out[rows] = ref[z * (TP + 1) + TP].astype(F32)
    small_out(here, info_ref, sums[...] + sums_of(came), *small)


def qkv_halves_kernel(here, normed_ref, d_qkv_ref, send, mine, total_ref):
    def put(m, lanes, block):
        total_ref[m, :, lanes] = block

    qkv_grads(normed_ref, d_qkv_ref, put)
    for x, out in ((1 - here[X], send), (here[X], mine)):
        for z in range(4):
            start = pl.multiple_of((4 * x + z) * DEPTH, 8)
            for m in range(3):
                out[z * 3 + m] = total_ref[m, pl.ds(start, DEPTH), :].astype(BF16)


def qkv_finish(here, mine, came, *outs):
    for k in range(TP):

        @pl.when(here[ME] == k)
        def _():
            for m in range(3):
                values = added(mine, came, m).astype(BF16)
                for r, out in enumerate(outs):
                    out[m] = values[:, (k ^ r) * COLS : (k ^ r) * COLS + COLS]


def qkv_collect(here, own, a_ref, b_ref, c_ref, chunk):
    for k in range(TP):

        @pl.when(here[ME] == k)
        def _():
            for m in range(3):
                for r, ref in enumerate((own, a_ref, b_ref, c_ref)):
                    chunk[m, :, (k ^ r) * COLS : (k ^ r) * COLS + COLS] = ref[m]


def qkv_high(here, chunk, came, pair):
    join_high(here, chunk, came, pair, 3)


def qkv_low(here, pair, came, half):
    join_low(here, pair, came, half, 3)


def qkv_rows(here, half, came, *outs):
    for x, ref in ((here[X], half), (1 - here[X], came)):
        for z in range(4):
            for m, out in enumerate(outs):
                out[pl.ds(pl.multiple_of((4 * x + z) * DEPTH, 8), DEPTH)] = ref[z * 3 + m].astype(F32)


def input_kernel(
    here, small_ref, near_ref, far_ref, hidden_grad_ref, keep_ref, core_ref, layer_near_ref, layer_far_ref, y_ref,
    out_near_ref, out_far_ref,
):
    values = jnp.concatenate([near_ref[...], far_ref[...]], axis=0).astype(F32)
    upper = keep_ref[:ROWS] + core_ref[:ROWS].astype(F32) + y_ref[...].astype(F32)
    back, _ = norm_back(values, gain_row(small_ref, 0), upper)
    grad = (hidden_grad_ref[...] + back).astype(BF16)
    out_near_ref[0] = layer_near_ref[...]
    out_near_ref[1] = grad[:PIECE]
    out_far_ref[0] = layer_far_ref[...]
    out_far_ref[1] = grad[PIECE:]


def on_device(
    inputs, teacher, seq_lengths, gain_attn, w_query, w_key, w_value, w_out, bias_table, gain_ffn, w_inner, w_outer
):
    n_ctx = lax.axis_size("ctx")
    spread = n_ctx // (SEQ_DEV * TP)
    me = lax.axis_index("wsh")
    ctx_me = lax.axis_index("ctx")
    parity = ctx_me & 1
    token_total = ROWS * n_ctx * TP
    same, cross = seq_routes(n_ctx)
    home = ctx_me // spread
    stretch = ctx_me % spread
    seq_bit = home & 1
    by_steps = n_ctx == 8

    def to_home(pair):
        return lax.ppermute(pair[0], AXES, same), lax.ppermute(pair[1], AXES, cross)

    def from_home(near, far):
        near = lax.ppermute(near, AXES, backwards(same))
        far = lax.ppermute(far, AXES, backwards(cross))
        return near, far

    def block_places(stretch_index):
        return [
            TP * 2 * stretch_index + 2 * swapped(me ^ r) + (seq_bit ^ e) for r in ORDER for e in (0, 1)
        ]

    query_blocks = block_places(stretch)
    key_blocks = [p for i in range(spread) for p in block_places(i)] if spread > 1 else query_blocks

    scalars = [me, parity, (ctx_me >> 1) & 3, swapped(home >> 1), seq_bit] + query_blocks + key_blocks
    here = jnp.stack([jnp.asarray(v, jnp.int32) for v in scalars])

    low = functools.partial(shape, dtype=BF16)
    x_here, x_there, *qkv_blocks = call(
        start_kernel,
        (low(PIECE, D),) * 2 + (low(OWN + 16, 3 * COLS),) * 4,
        (here, inputs, w_query, w_key, w_value, gain_attn, gain_ffn, bias_table, seq_lengths),
        scratch=(pltpu.VMEM((16, 3 * COLS), F32),) + (pltpu.VMEM((OWN, D), BF16),) * 3
        + (pltpu.VMEM((OWN,), BF16),) * 2 + (pltpu.VMEM((8, H), BF16), pltpu.VMEM((SEQ_DEV,), jnp.int32))
        + (pltpu.SemaphoreType.DMA((9,)),),
        mib=START_MIB,
        in_hbm=8,
    )
    x_near, x_far = to_home((x_here, x_there))

    def group_blocks(values):
        return (values[0],) + tuple(to_partner(values[r], r) for r in (1, 2, 3))

    w_qkv_pieces = group_blocks(qkv_blocks)
    (small, info, bias), (w_qkv,) = run(
        here,
        (
            functools.partial(bias_kernel, float(n_ctx * PIECE)),
            (shape(TP, 16, 3 * COLS), shape(8, 128), shape(HEADS, 5, PIECE, PIECE)),
            w_qkv_pieces,
        ),
        (rows_kernel, (low(D, 3 * COLS),), w_qkv_pieces),
    )
    x_own = (x_near, x_far)
    *teacher_halves, a, b, c, d = call(
        inner_blocks_kernel, (low(PIECE, D),) * 2 + (low(OWN, D),) * 4, (here, after(w_inner, w_qkv), teacher)
    )
    inner_blocks = (a, b, c, d)
    x_y = tuple(to_partner(v, 2) for v in x_own)
    x_y = tuple(after(v, w_qkv) for v in x_y)
    pieces = x_own + x_y + tuple(to_partner(v, 1) for v in x_own + x_y)
    attn_shapes = (shape(COLS, GROUP), shape(8, GROUP), shape(GROUP, D))
    send_job = (send_kernel, (low(2 * ROWS, D),))
    proj_shapes = (low(GROUP, D), low(GROUP, 3 * COLS))

    def attn_scratch(keys, chunk):
        return (pltpu.VMEM((keys, chunk), F32), pltpu.VMEM((keys, chunk), BF16))

    if spread == 1:
        normed, qkv, attn_t, lse, partial = call(
            front_kernel,
            proj_shapes + attn_shapes,
            (here, small) + pieces + (w_qkv, info, bias, w_out),
            scratch=attn_scratch(GROUP, 256),
            mib=14,
        )
    else:
        teams = [[s * spread + i for i in range(spread)] for s in range(SEQ_DEV * TP)]
        normed, qkv = call(project_kernel, proj_shapes, (here, small) + pieces + (w_qkv,))
        kv = lax.all_gather(qkv[:, COLS:], "ctx", axis=0, tiled=True, axis_index_groups=teams)
        q = qkv[:, :COLS]
        attn_t, lse, partial = call(
            functools.partial(attention_kernel, 128, (0, COLS)),
            attn_shapes,
            (here, q, kv, info, bias, w_out),
            scratch=attn_scratch(kv.shape[0], 128),
            mib=56,
        )

    def scatter_tail(keep_y, from_core):
        return call(tail_kernel, (low(ROWS, D),), (here, keep_y, from_core))[0]

    w_in_pieces = group_blocks([after(v, *x_y) for v in inner_blocks])
    (send,), (w_in,) = run(
        here,
        send_job + ((partial,),),
        (rows_kernel, (low(D, D),), w_in_pieces),
    )
    core = to_partner(send, 1)
    going = scatter_tail(partial, core)
    across = to_partner(going, 2)
    teacher_near, teacher_far = to_home([after(v, going) for v in teacher_halves])
    partial, teacher_near, teacher_far = lax.optimization_barrier((partial, teacher_near, teacher_far))
    hidden, ffn_low = call(
        hidden_kernel,
        (shape(ROWS, D), low(ROWS, D)),
        (here, small, x_near, x_far, partial, core, across),
    )

    def gathered(value):
        from_y = to_partner(value, 2)
        return to_partner(value, 1), from_y

    def both_halves(first_call, second_call, value):
        from_core, from_y = gathered(value)
        first, done = first_call((value, from_core))
        core_y = to_partner(after(from_y, done), 1)
        second = second_call((from_y, core_y))
        core_own = to_partner(first[-1], 1)
        going = scatter_tail(second[-2], to_partner(second[-1], 1))
        across = to_partner(going, 2)
        return (value, from_core, from_y, core_y), first, second, (first[-2], core_own, across), going

    half = low(2 * ROWS, D)
    piece_shapes = (shape(ROWS, D), low(ROWS, D))
    def ffn(values):
        return call(ffn_kernel, (half, half) + piece_shapes, (here,) + values + (w_in, w_outer))

    def ffn_first(values):
        outs = ffn(values)
        return outs, outs[-1]

    ffn_all, (active_a, slope_a, *_), (active_b, slope_b, *_), parts, _ = both_halves(ffn_first, ffn, ffn_low)
    out_near, out_far, result_grad, result_low, squares = call(
        functools.partial(loss_kernel, float(token_total)),
        (low(PIECE, D), low(PIECE, D), shape(ROWS, D), low(ROWS, D), shape(1, D)),
        (here, hidden) + parts + (teacher_near, teacher_far, info),
    )

    depth = OWN // n_ctx

    def parts_of(count, rows=DEPTH):
        return low(count, rows, D)

    def ffn_back(values, slope):
        return call(ffn_back_kernel, (half,) + piece_shapes, (here,) + values + (slope, w_in, w_outer))

    def ffn_back_first(values):
        outs = ffn_back(values, slope_a)
        (part,) = call(
            outer_own_kernel, (shape(D, D),), (here, after(active_a, outs[-1])) + values, mib=12
        )
        grads.append(part)
        return outs, part

    def ffn_back_second(values):
        args = (here, grads[0], active_b) + values
        if by_steps:
            outs = (parts_of(4, D // 8),) * 2
            grads[:] = call(outer_halves_kernel, outs, args, scratch=(pltpu.VMEM((D, D), F32),), mib=14)
        else:
            grads[:] = call(outer_kernel, (low(D, D),), args, mib=12)
        return ffn_back((after(values[0], grads[0]), values[1]), slope_b)

    grads = []
    result_all, (inner_a, *_), (inner_b, *_), parts, going = both_halves(
        ffn_back_first, ffn_back_second, result_low
    )
    inner_args = (here,) + ffn_all + (inner_a, after(inner_b, going))
    ahead = []
    if by_steps:
        outer_send, outer_mine = grads
        outer_came = to_ctx(outer_send, 1)
        inner_send, inner_mine = call(
            inner_halves_kernel, (parts_of(4 * TP),) * 2, inner_args, scratch=(pltpu.VMEM((D, D), F32),), mib=14
        )
        ordered = inner_send
        ahead.append((split_low, (parts_of(2, D // 8),) * 2, (outer_mine, outer_came)))
    else:
        (outer_wgrad,) = grads
        (inner_wgrad,) = call(inner_kernel, (low(D, D),), inner_args, mib=14)
        ordered = inner_wgrad
    (hidden_grad, hidden_low, ffn_gain_grad), *ahead = run(
        here,
        (
            hidden_back_kernel,
            (shape(ROWS, D), low(ROWS, D), shape(1, D)),
            (small, after(hidden, ordered), result_grad) + parts,
        ),
        *ahead,
    )
    from_core, from_y = gathered(hidden_low)
    if by_steps:
        ((outer_send, outer_keep),) = ahead
        outer_came = to_ctx(outer_send, 2)
        from_y = after(from_y, outer_came)
    up_pieces = (hidden_low, from_y, from_core, to_partner(from_y, 1))
    table_shape = shape(HEADS, 5, PIECE, PIECE)
    if by_steps:
        (inner_send, inner_mine), (outer_send, outer_keep) = run(
            here,
            (
                out_grads,
                (parts_of(4 * TP + 4),) * 2,
                (attn_t,) + up_pieces + (inner_send, inner_mine),
            ),
            (split_high, (parts_of(1, D // 8),) * 2, (outer_keep, outer_came)),
            scratch=(pltpu.VMEM((OWN, D), F32),),
        )
        inner_came = to_ctx(inner_send, 1)
        outer_came = to_ctx(outer_send, 4)
        up_pieces = (after(hidden_low, outer_keep),) + up_pieces[1:]
    if spread == 1:
        d_qkv, table_part, partial = call(
            back_kernel,
            (proj_shapes[1], table_shape, shape(GROUP, D)),
            (here, qkv, info, bias, w_out, attn_t, lse, w_qkv) + up_pieces,
            scratch=back_scratch(GROUP, 256),
            mib=20,
        )
    else:
        dq, dkv, table_part = call(
            functools.partial(attention_back_kernel, 128, (0, COLS)),
            (low(GROUP, COLS), low(kv.shape[0], 2 * COLS), table_shape),
            (here, q, kv, info, bias, w_out, attn_t, lse) + up_pieces,
            scratch=back_scratch(kv.shape[0], 128),
            mib=60,
        )
        dkv = lax.psum_scatter(dkv, "ctx", scatter_dimension=0, tiled=True, axis_index_groups=teams)
        d_qkv = jnp.concatenate([dq, dkv], axis=1)
        (partial,) = call(partial_kernel, (shape(GROUP, D),), (here, d_qkv, w_qkv))
    if by_steps:
        (send,), (outer_chunk,), (inner_send, inner_keep) = run(
            here,
            send_job + ((partial,),),
            (finish, (parts_of(1, D // 8),), (outer_keep, outer_came)),
            (split_low, (parts_of(2 * TP + 2),) * 2, (inner_mine, inner_came)),
        )
        outer_came = to_ctx(outer_chunk, 4)
        inner_came = to_ctx(inner_send, 2)
    else:
        ((send,),) = run(here, send_job + ((partial,),))
    core = to_partner(send, 1)
    input_job = (
        input_kernel,
        (low(2, PIECE, D), low(2, PIECE, D)),
        (small, x_near, x_far, hidden_grad, partial, core, out_near, out_far),
    )
    small_shapes = (shape(1, OWN), shape(1, OWN), shape(8, H), shape(1, 1))
    sums_shape = shape(SUM_ROWS, D)
    pair_out = (low(SEQ_DEV, PIECE, D), shape(SEQ_DEV, PIECE, D))
    sum_args = (partial, normed, small, ffn_gain_grad, squares, table_part)

    if by_steps:
        going = scatter_tail(partial, core)
        across = to_partner(going, 2)
        qkv_send, qkv_mine = call(
            qkv_halves_kernel,
            (parts_of(12),) * 2,
            (here, normed, after(d_qkv, going)),
            scratch=(pltpu.VMEM((3, OWN, D), F32),),
        )
        qkv_came = to_ctx(qkv_send, 1)
        inner_keep, across = lax.optimization_barrier((after(inner_keep, qkv_send), across))
        (inner_send, inner_keep), (outer_pair,) = run(
            here,
            (split_high, (parts_of(TP + 1),) * 2, (inner_keep, inner_came)),
            (join_high, (parts_of(2, D // 8),), (outer_chunk, outer_came)),
        )
        inner_came = to_ctx(inner_send, 4)
        outer_came = to_ctx(outer_pair, 2)
        ((in_near, in_far),) = run(
            here, (input_job[0], input_job[1], input_job[2] + (after(across, inner_keep),))
        )
        home_near, home_far = from_home(in_near, in_far)
        ((qkv_send, qkv_keep),) = run(
            here, (split_low, (parts_of(6),) * 2, (after(qkv_mine, in_near), qkv_came))
        )
        qkv_came = to_ctx(qkv_send, 2)
        (sums,) = call(sums_kernel, (sums_shape,), (here, after(partial, qkv_send)) + sum_args[1:])
        inner_blocks, (outer_half,) = run(
            here,
            (
                inner_finish,
                (parts_of(2),) + (parts_of(1 + 1),) * 3,
                (after(inner_keep, qkv_keep), inner_came, sums),
            ),
            (join_low, (parts_of(4, D // 8),), (outer_pair, outer_came)),
        )
        inner_blocks = group_blocks(inner_blocks)
        outer_came = to_ctx(outer_half, 1)
        ((qkv_send, qkv_keep),) = run(
            here, (split_high, (parts_of(3),) * 2, (after(qkv_keep, outer_half), qkv_came))
        )
        qkv_came = to_ctx(qkv_send, 4)
        ((inner_chunk, sums),) = run(
            here,
            (
                inner_collect,
                (parts_of(TP + 1 + 1), sums_shape),
                (after(inner_blocks[0], qkv_keep, home_far),) + inner_blocks[1:] + (sums,),
            ),
        )
        inner_came = to_ctx(inner_chunk, 4)
        (qkv_blocks,) = run(
            here, (qkv_finish, (low(3, DEPTH, COLS),) * 4, (after(qkv_keep, inner_chunk), qkv_came))
        )
        qkv_blocks = group_blocks(qkv_blocks)
        (inner_pair, sums), (w_outer_grad,) = run(
            here,
            (
                inner_high,
                (parts_of(2 * TP + 2 + 1), sums_shape),
                (after(inner_chunk, qkv_blocks[0]), inner_came, sums),
            ),
            (outer_rows, (shape(D, D),), (outer_half, outer_came)),
        )
        inner_came = to_ctx(inner_pair, 2)
        ((qkv_chunk,),) = run(
            here, (qkv_collect, (parts_of(3),), (after(qkv_blocks[0], inner_pair),) + qkv_blocks[1:])
        )
        qkv_came = to_ctx(qkv_chunk, 4)
        ((inner_half, sums),) = run(
            here,
            (
                inner_low,
                (parts_of(4 * TP + 4 + 1), sums_shape),
                (after(inner_pair, qkv_chunk), inner_came, sums),
            ),
        )
        inner_came = to_ctx(inner_half, 1)
        ((qkv_pair,),) = run(here, (qkv_high, (parts_of(6),), (after(qkv_chunk, inner_half), qkv_came)))
        qkv_came = to_ctx(qkv_pair, 2)
        ((qkv_half,),) = run(here, (qkv_low, (parts_of(12),), (qkv_pair, qkv_came)))
        qkv_came = to_ctx(qkv_half, 1)
        ((w_inner_grad, w_out_grad, my_attn_gain, my_ffn_gain, my_rows, loss_value),) = run(
            here,
            (
                inner_rows,
                (shape(OWN, TP * D), shape(OWN, D)) + small_shapes,
                (info, after(inner_half, qkv_half), inner_came, sums),
            ),
        )
        (layer_out, input_grad), (w_query_grad, w_key_grad, w_value_grad) = run(
            here,
            (pair_kernel, pair_out, (home_near, home_far)),
            (qkv_rows, (shape(OWN, D),) * 3, (after(qkv_half, w_out_grad), qkv_came)),
        )
    else:
        across = to_partner(scatter_tail(partial, core), 2)
        ((in_near, in_far),) = run(here, (input_job[0], input_job[1], input_job[2] + (across,)))
        ((layer_out, input_grad),) = run(here, (pair_kernel, pair_out, from_home(in_near, in_far)))
        (sums,) = call(sums_kernel, (sums_shape,), (here,) + sum_args)
        (hidden_all,) = call(join_kernel, (low(GROUP, D),), (here,) + up_pieces)
        my_attn_gain, my_ffn_gain, my_rows, loss_value = call(
            small_out_kernel, small_shapes, (here, info, lax.psum(sums, AXES))
        )

        def summed(parts):
            return lax.psum_scatter(parts, "ctx", scatter_dimension=0)

        def inner_to_rows(chunk):
            return swap_blocks(chunk, "wsh").transpose(1, 0, 2).reshape(depth, TP * D)

        def attn_to_rows(chunk):
            blocks = chunk[:3].reshape(3, depth, TP, COLS).transpose(2, 0, 1, 3)
            mine = swap_blocks(blocks, "wsh").transpose(1, 2, 0, 3).reshape(3, depth, D)
            return jnp.concatenate([mine, chunk[3:]])

        (attn_wgrad,) = call(
            attention_grads_kernel, (low(4, OWN, D),), (here, normed, d_qkv, attn_t, hidden_all)
        )
        outer_full = lax.all_gather(summed(outer_wgrad.reshape(n_ctx, D // n_ctx, D)), "ctx")
        inner_parts = inner_wgrad.reshape(TP, n_ctx, depth, D).transpose(1, 0, 2, 3)
        inner_full = lax.all_gather(inner_to_rows(summed(inner_parts)), "ctx")
        attn_parts = attn_wgrad.reshape(4, n_ctx, depth, D).transpose(1, 0, 2, 3)
        attn_full = lax.all_gather(attn_to_rows(summed(attn_parts)), "ctx")
        w_outer_grad = outer_full.reshape(D, D).astype(F32)
        w_inner_grad = inner_full.reshape(OWN, TP * D).astype(F32)
        w_query_grad, w_key_grad, w_value_grad, w_out_grad = (
            attn_full[:, m].reshape(OWN, D).astype(F32) for m in range(4)
        )

    return (
        layer_out,
        loss_value.reshape(()),
        input_grad,
        my_attn_gain.reshape(-1),
        w_query_grad,
        w_key_grad,
        w_value_grad,
        w_out_grad,
        my_rows,
        my_ffn_gain.reshape(-1),
        w_inner_grad,
        w_outer_grad,
    )


def solution(mesh):
    rows = P("wsh", None)
    tokens = P("wsh", "ctx", None)
    return jax.shard_map(
        on_device,
        mesh=mesh,
        in_specs=(tokens, tokens, P("wsh"), P("wsh"), rows, rows, rows, rows, rows, P("wsh"), rows, rows),
        out_specs=(tokens, P(), tokens, P("wsh"), rows, rows, rows, rows, rows, P("wsh"), rows, rows),
        check_vma=False,
    )
```

```python
import functools

import jax
import jax.numpy as jnp
from jax import lax
from jax.experimental import pallas as pl
from jax.experimental.pallas import tpu as pltpu
from jax.sharding import PartitionSpec as P

D = 768
H = 12
DH = 64
BUCKETS = 32
SEQ_DEV = 2
PIECE = 128
TP = 4
HEADS = H // TP
COLS = HEADS * DH
OWN = D // TP
ROWS = SEQ_DEV * PIECE
GROUP = ROWS * TP
DEPTH = OWN // 8
START_MIB = 60
EPS = 1e-06
NEG_FILL = -1e30
BUCKET_EDGES = (12, 16, 23, 32, 46, 64, 91)
AXES = ("ctx", "wsh")
ORDER = (0, 2, 1, 3)

ME, X, Z, SEQ_OWNER, SEQ_BIT, QUERY_BLOCKS = range(6)
KEY_BLOCKS = QUERY_BLOCKS + 8

BF16 = jnp.bfloat16
F32 = jnp.float32
NT = (((1,), (1,)), ((), ()))
TN = (((0,), (0,)), ((), ()))
NN = (((1,), (0,)), ((), ()))


def dot(left, right, dims=NN):
    return lax.dot_general(left, right, dims, preferred_element_type=F32)


def swapped(index):
    return (index & 1) * 2 + (index >> 1)


def seq_routes(n_ctx):
    spread = n_ctx // (SEQ_DEV * TP)
    same, cross = [], []
    for c in range(n_ctx):
        for w in range(TP):
            pair = c // 2
            for b in range(2):
                home = (2 * swapped(w) + b) * spread + pair // TP
                route = (c * TP + w, home * TP + swapped(pair % TP))
                (same if b == c % 2 else cross).append(route)
    return same, cross


def backwards(routes):
    return [(there, here) for here, there in routes]


def to_partner(value, offset):
    return lax.ppermute(value, "wsh", [(i, i ^ offset) for i in range(TP)])


def to_ctx(value, offset):
    n_ctx = lax.axis_size("ctx")
    return lax.ppermute(value, "ctx", [(i, i ^ offset) for i in range(n_ctx)])


def swap_blocks(blocks, axis, groups=None):
    return lax.all_to_all(blocks, axis, 0, 0, tiled=True, axis_index_groups=groups)


def pick(stack, index):
    return lax.dynamic_index_in_dim(stack, index, 0, keepdims=False)


def after(value, *earlier):
    return lax.optimization_barrier((value,) + earlier)[0]


def bucket_index(offset):
    distance = jnp.abs(offset)
    far_bucket = 8 + sum(((distance >= edge).astype(jnp.int32) for edge in BUCKET_EDGES))
    near_or_far = jnp.where(distance < 8, distance, far_bucket)
    return near_or_far + jnp.where(offset > 0, 16, 0)


def gelu_and_slope(values):
    cumulative = 0.5 * (1.0 + lax.erf(values * 0.7071067811865476))
    density = jnp.exp(-0.5 * values * values) * 0.3989422804014327
    return values * cumulative, cumulative + values * density


def inverse_rms(values):
    return lax.rsqrt(jnp.mean(values * values, axis=-1, keepdims=True) + EPS)


def norm_back(values, gain, grad):
    scale = inverse_rms(values)
    unit = values * scale
    scaled = gain * grad
    back = scale * (scaled - unit * jnp.mean(scaled * unit, axis=-1, keepdims=True))
    return back, jnp.sum(grad * unit, axis=0, keepdims=True)


def repeat(count, unroll, body, carry):
    if unroll:
        for index in range(count):
            carry = body(index, carry)
        return carry
    return lax.fori_loop(0, count, body, carry)


def vmem():
    return pl.BlockSpec(memory_space=pltpu.VMEM)


def smem():
    return pl.BlockSpec(memory_space=pltpu.SMEM)


def shape(*dims, dtype=F32):
    return jax.ShapeDtypeStruct(dims, dtype)


def hbm():
    return pl.BlockSpec(memory_space=pl.ANY)


def name_of(body):
    return (body.func if isinstance(body, functools.partial) else body).__name__


def run(here, *jobs, scratch=(), mib=10, weight=1):
    args = [a for _, _, given in jobs for a in given]
    outs = [o for _, made, _ in jobs for o in made]

    def bodies(here, *refs):
        ins, rest = refs[: len(args)], refs[len(args) :]
        made, extra = rest[: len(outs)], rest[len(outs) :]
        i = o = 0
        for body, shapes, given in jobs:
            body(here, *ins[i : i + len(given)], *made[o : o + len(shapes)], *extra)
            i, o = i + len(given), o + len(shapes)

    bodies.__name__ = "_".join(name_of(body) for body, _, _ in jobs)
    results = list(call(bodies, outs, [here] + args, scratch, mib, weight=weight))
    return [tuple(results.pop(0) for _ in made) for _, made, _ in jobs]


def call(body, outs, args, scratch=(), mib=10, in_hbm=0, weight=1):
    return pl.pallas_call(
        body,
        name=name_of(body),
        out_shape=tuple(outs),
        in_specs=[smem()] + [hbm()] * in_hbm + [vmem()] * (len(args) - 1 - in_hbm),
        out_specs=(vmem(),) * len(outs),
        scratch_shapes=tuple(scratch),
        compiler_params=pltpu.CompilerParams(vmem_limit_bytes=mib * 2**20),
        cost_estimate=pl.CostEstimate(flops=int(2e9 * weight), bytes_accessed=int(2**23 * weight), transcendentals=0),
    )(*args)


def start_kernel(
    here, x_hbm, wq_hbm, wk_hbm, wv_hbm, gain_a_hbm, gain_f_hbm, table_hbm, lengths_hbm, *refs
):
    halves, outs, small_ref = refs[:2], refs[2:6], refs[6]
    weights, (gain_a_ref, gain_f_ref, table_ref, lengths_ref), sems = refs[7:10], refs[10:14], refs[14]
    moves = [(x_hbm.at[here[X]], halves[0]), (x_hbm.at[1 - here[X]], halves[1])]
    moves += list(zip((wq_hbm, wk_hbm, wv_hbm), weights))
    moves += [(gain_a_hbm, gain_a_ref), (gain_f_hbm, gain_f_ref), (table_hbm, table_ref), (lengths_hbm, lengths_ref)]
    copies = [pltpu.make_async_copy(src, dst, sems.at[i]) for i, (src, dst) in enumerate(moves)]
    for copy in copies:
        copy.start()
    small_ref[...] = jnp.zeros(small_ref.shape, F32)
    for copy in copies:
        copy.wait()
    small_ref[0:1, :OWN] = gain_a_ref[...].astype(F32).reshape(1, OWN)
    small_ref[1:2, :OWN] = gain_f_ref[...].astype(F32).reshape(1, OWN)
    lengths = lengths_ref[...].reshape(1, SEQ_DEV)
    high = lengths >> 7
    small_ref[2:3, :SEQ_DEV] = high.astype(F32)
    small_ref[3:4, :SEQ_DEV] = (lengths - high * 128).astype(F32)
    small_ref[8:16, :H] = table_ref[...].astype(F32)
    for k in range(TP):

        @pl.when(here[ME] == k)
        def _():
            for r in range(TP):
                for m, ref in enumerate(weights):
                    outs[r][:OWN, m * COLS : (m + 1) * COLS] = ref[:, (k ^ r) * COLS : (k ^ r) * COLS + COLS]

    for out in outs:
        out[OWN:] = small_ref[...].astype(BF16)


def inner_blocks_kernel(here, inner_ref, teacher_ref, near_ref, far_ref, own_ref, core_ref, across_ref):
    near_ref[...] = teacher_ref[here[X]]
    far_ref[...] = teacher_ref[1 - here[X]]

    def lanes(r):
        return pl.ds(pl.multiple_of((here[ME] ^ r) * D, D), D)

    own_ref[...] = inner_ref[:, lanes(0)]
    core_ref[...] = inner_ref[:, lanes(1)]
    rows = across_ref.shape[1]
    for i in range(2):
        across_ref[i] = inner_ref[pl.ds(pl.multiple_of(here[X] * rows, rows), rows), lanes(2 + i)]


def inner_rows_kernel(here, own_ref, core_ref, y_ref, x_ref, core_y_ref, core_x_ref, out_ref):
    rows = y_ref.shape[1]
    me, x = here[ME], here[X]
    out_ref[pl.ds(pl.multiple_of(me * OWN, OWN), OWN)] = own_ref[...]
    out_ref[pl.ds(pl.multiple_of((me ^ 1) * OWN, OWN), OWN)] = core_ref[...]
    for r, ref, half in ((2, y_ref, x), (2, x_ref, 1 - x), (3, core_y_ref, x), (3, core_x_ref, 1 - x)):
        start = (me ^ r) * OWN + half * rows
        out_ref[pl.ds(pl.multiple_of(start, rows), rows)] = ref[r - 2]


def gain_row(small_ref, row):
    return jnp.concatenate([small_ref[i, row : row + 1, :OWN] for i in range(TP)], axis=1)


def bias_kernel(longest, here, small_a, small_b, small_c, small_d, small_ref, info_ref, bias_ref):
    for r, ref in enumerate((small_a, small_b, small_c, small_d)):
        small_ref[here[ME] ^ r] = ref[OWN:].astype(F32)
    pair = lax.broadcasted_iota(jnp.int32, (1, SEQ_DEV), 1)
    length = jnp.zeros((1, 1), F32)
    count = jnp.zeros((1, 1), F32)
    for i in range(TP):
        lengths = small_ref[i, 2:3, :SEQ_DEV] * 128.0 + small_ref[i, 3:4, :SEQ_DEV]
        mine = (pair == here[SEQ_BIT]) & (here[SEQ_OWNER] == i)
        length = length + jnp.sum(jnp.where(mine, lengths, 0.0), axis=1, keepdims=True)
        count = count + jnp.sum(jnp.minimum(lengths, longest), axis=1, keepdims=True)
    info_ref[0:1, :] = jnp.broadcast_to(length, (1, 128))
    info_ref[1:2, :] = jnp.broadcast_to(count, (1, 128))
    table = jnp.concatenate([small_ref[i, 8:16, :] for i in range(TP)], axis=0)
    lane = lax.broadcasted_iota(jnp.int32, table.shape, 1)
    apart = lax.broadcasted_iota(jnp.int32, (PIECE, PIECE), 0) - lax.broadcasted_iota(
        jnp.int32, (PIECE, PIECE), 1
    )
    for head in range(HEADS):
        values = jnp.sum(jnp.where(lane == here[ME] * HEADS + head, table, 0.0), axis=1, keepdims=True)
        for tile in range(5):
            low, high = ((15, 16), (1, 16), (0, 32), (17, 32), (31, 32))[tile]
            ids = bucket_index(apart + (tile - 2) * PIECE)
            total = jnp.broadcast_to(values[low : low + 1], (PIECE, PIECE))
            for b in range(low + 1, high):
                total = jnp.where(ids == b, values[b : b + 1], total)
            bias_ref[head, tile] = total


def block_bias(bias_ref, here, head, key_block, query_block, blocks):
    tiles = []
    for i in range(blocks):
        apart = here[KEY_BLOCKS + key_block] - here[QUERY_BLOCKS + query_block + i]
        tiles.append(bias_ref[head, jnp.clip(apart, -2, 2) + 2])
    return tiles[0] if blocks == 1 else jnp.concatenate(tiles, axis=1)


def attend(chunk, offsets, here, q_ref, kv_ref, info_ref, bias_ref, attn_ref, lse_ref, s_ref, p_ref):
    key_blocks = kv_ref.shape[0] // PIECE
    length = info_ref[0:1, 0:1]
    k_off, v_off = offsets
    blocks = chunk // PIECE
    unroll = key_blocks <= 8
    key_iota = lax.broadcasted_iota(jnp.int32, (PIECE, 1), 0)
    for head in range(HEADS):
        lanes = slice(head * DH, head * DH + DH)
        key_part = kv_ref[:, k_off + head * DH : k_off + head * DH + DH]
        value_part = kv_ref[:, v_off + head * DH : v_off + head * DH + DH]

        def for_queries(q_chunk, carry):
            rows = pl.ds(pl.multiple_of(q_chunk * chunk, chunk), chunk)
            s_ref[...] = dot(key_part, q_ref[rows, lanes], NT)

            def score(index, top):
                at = pl.ds(pl.multiple_of(index * PIECE, PIECE), PIECE)
                tile = s_ref[at, :] + block_bias(bias_ref, here, head, index, q_chunk * blocks, blocks)
                ok = (here[KEY_BLOCKS + index] * PIECE + key_iota).astype(F32) < length
                tile = jnp.where(ok, tile, NEG_FILL)
                s_ref[at, :] = tile
                return jnp.maximum(top, jnp.max(tile, axis=0, keepdims=True))

            top = repeat(key_blocks, unroll, score, jnp.full((1, chunk), NEG_FILL, F32))

            def weigh(index, total):
                at = pl.ds(pl.multiple_of(index * PIECE, PIECE), PIECE)
                weight = jnp.exp(s_ref[at, :] - top)
                p_ref[at, :] = weight.astype(BF16)
                return total + jnp.sum(weight, axis=0, keepdims=True)

            total = repeat(key_blocks, unroll, weigh, jnp.zeros((1, chunk), F32))
            attn_ref[lanes, rows] = dot(value_part, p_ref[...], TN) / total
            lse_ref[head : head + 1, rows] = top + jnp.log(total)
            return carry

        repeat(GROUP // chunk, unroll, for_queries, 0)


def send_kernel(here, partial_ref, send_ref, *_):
    send_ref[...] = partial_ref[2 * ROWS :].astype(BF16)


def stack_rows(here, pieces, out_ref):
    for r, piece in enumerate(pieces):
        out_ref[pl.ds(pl.multiple_of((here[ME] ^ r) * OWN, OWN), OWN)] = piece[:OWN]


def project(here, small_ref, pieces, w_ref, normed_ref, qkv_ref):
    gain = gain_row(small_ref, 0)
    for i, piece in enumerate(pieces):
        values = piece[...].astype(F32)
        normed_ref[i * PIECE : (i + 1) * PIECE] = (values * inverse_rms(values) * gain).astype(BF16)
    qkv_ref[...] = dot(normed_ref[...], w_ref[...]).astype(BF16)


def project_kernel(here, small_ref, *refs):
    project(here, small_ref, refs[:8], *refs[8:])


def attention_kernel(chunk, offsets, here, q_ref, kv_ref, info_ref, bias_ref, out_w_ref, *refs):
    attn_ref, lse_ref, partial_ref, s_ref, p_ref = refs
    attend(chunk, offsets, here, q_ref, kv_ref, info_ref, bias_ref, attn_ref, lse_ref, s_ref, p_ref)
    partial_ref[...] = dot(attn_ref[...].astype(BF16), out_w_ref[...], TN)


def front_kernel(here, small_ref, *refs):
    pieces, (w_ref, info_ref, bias_ref, out_w_ref), (normed_ref, qkv_ref) = refs[:8], refs[8:12], refs[12:14]
    project(here, small_ref, pieces, w_ref, normed_ref, qkv_ref)
    attention_kernel(512, (COLS, 2 * COLS), here, qkv_ref, qkv_ref, info_ref, bias_ref, out_w_ref, *refs[14:])


def attend_back(
    chunk, offsets, here, q_ref, kv_ref, info_ref, bias_ref, out_w_ref, pieces, attn_ref, lse_ref,
    tile_ref, s_ref, dp_ref, p_ref, ds_ref, do_ref, outdot_ref, dqt_ref, dkv_ref,
):
    key_blocks = kv_ref.shape[0] // PIECE
    length = info_ref[0:1, 0:1]
    k_off, v_off = offsets
    blocks = chunk // PIECE
    unroll = key_blocks <= 8
    key_iota = lax.broadcasted_iota(jnp.int32, (PIECE, 1), 0)
    for i, piece in enumerate(pieces):
        at = slice(i * ROWS, (i + 1) * ROWS)
        do_ref[at] = dot(piece[...], out_w_ref[...], NT).astype(BF16)
        do_t = dot(out_w_ref[...], piece[...], NT).astype(BF16).astype(F32) * attn_ref[:, at]
        for head in range(HEADS):
            outdot_ref[head : head + 1, at] = jnp.sum(do_t[head * DH : head * DH + DH], axis=0, keepdims=True)
    tile_ref[...] = jnp.zeros_like(tile_ref)
    dkv_ref[...] = jnp.zeros_like(dkv_ref)
    for head in range(HEADS):
        lanes = slice(head * DH, head * DH + DH)
        v_lanes = slice(COLS + head * DH, COLS + head * DH + DH)
        key_part = kv_ref[:, k_off + head * DH : k_off + head * DH + DH]
        value_part = kv_ref[:, v_off + head * DH : v_off + head * DH + DH]

        def for_queries(q_chunk, carry):
            rows = pl.ds(pl.multiple_of(q_chunk * chunk, chunk), chunk)
            query_part = q_ref[rows, lanes]
            do_part = do_ref[rows, lanes]
            s_ref[...] = dot(key_part, query_part, NT)
            dp_ref[...] = dot(value_part, do_part, NT)
            lse = lse_ref[head : head + 1, rows]
            outdot = outdot_ref[head : head + 1, rows]

            def step(index, carry):
                at = pl.ds(pl.multiple_of(index * PIECE, PIECE), PIECE)
                tile = s_ref[at, :] + block_bias(bias_ref, here, head, index, q_chunk * blocks, blocks)
                ok = (here[KEY_BLOCKS + index] * PIECE + key_iota).astype(F32) < length
                prob = jnp.exp(jnp.where(ok, tile, NEG_FILL) - lse)
                p_ref[at, :] = prob.astype(BF16)
                grad = prob * (dp_ref[at, :] - outdot)
                ds_ref[at, :] = grad.astype(BF16)
                for i in range(blocks):
                    apart = here[KEY_BLOCKS + index] - here[QUERY_BLOCKS + q_chunk * blocks + i]
                    which = jnp.clip(apart, -2, 2) + 2
                    tile_ref[head, which] += grad[:, i * PIECE : (i + 1) * PIECE]
                return carry

            repeat(key_blocks, unroll, step, 0)
            dkv_ref[:, lanes] += dot(ds_ref[...], query_part)
            dkv_ref[:, v_lanes] += dot(p_ref[...], do_part)
            dqt_ref[lanes, rows] = dot(key_part, ds_ref[...], TN)
            return carry

        repeat(GROUP // chunk, unroll, for_queries, 0)


def bucket_sums(tile_ref, head):
    apart = lax.broadcasted_iota(jnp.int32, (PIECE, PIECE), 0) - lax.broadcasted_iota(
        jnp.int32, (PIECE, PIECE), 1
    )
    bucket = lax.broadcasted_iota(jnp.int32, (BUCKETS, 128), 0)
    table = jnp.zeros((BUCKETS, 128), F32)
    for which in range(5):
        tile = tile_ref[head, which]
        low, high = ((15, 16), (1, 16), (0, 32), (17, 32), (31, 32))[which]
        ids = bucket_index(apart + (which - 2) * PIECE)
        for b in range(low, high):
            chosen = tile if high == low + 1 else jnp.where(ids == b, tile, 0.0)
            table = table + jnp.where(bucket == b, jnp.sum(chosen, axis=0, keepdims=True), 0.0)
    return table


def back_scratch(keys, chunk):
    return (
        pltpu.VMEM((keys, chunk), F32),
        pltpu.VMEM((keys, chunk), F32),
        pltpu.VMEM((keys, chunk), BF16),
        pltpu.VMEM((keys, chunk), BF16),
        pltpu.VMEM((GROUP, COLS), BF16),
        pltpu.VMEM((8, GROUP), F32),
        pltpu.VMEM((COLS, GROUP), F32),
        pltpu.VMEM((keys, 2 * COLS), F32),
    )


def join_kernel(here, *refs):
    for i, piece in enumerate(refs[:4]):
        refs[4][i * ROWS : (i + 1) * ROWS] = piece[...]


def attention_back_kernel(chunk, offsets, here, q_ref, kv_ref, info_ref, bias_ref, out_w_ref, attn_ref, lse_ref, *refs):
    pieces, (dq_ref, dkv_low_ref, tile_ref), scratch = refs[:4], refs[4:7], refs[7:]
    attend_back(
        chunk, offsets, here, q_ref, kv_ref, info_ref, bias_ref, out_w_ref, pieces, attn_ref, lse_ref, tile_ref,
        *scratch,
    )
    dq_ref[...] = scratch[6][...].T.astype(BF16)
    dkv_low_ref[...] = scratch[7][...].astype(BF16)


def back_kernel(here, qkv_ref, info_ref, bias_ref, out_w_ref, attn_ref, lse_ref, w_ref, *refs):
    pieces, (d_qkv_ref, tile_ref, partial_ref), scratch = refs[:4], refs[4:7], refs[7:]
    attend_back(
        256, (COLS, 2 * COLS), here, qkv_ref, qkv_ref, info_ref, bias_ref, out_w_ref, pieces, attn_ref, lse_ref,
        tile_ref, *scratch,
    )
    d_qkv_ref[:, :COLS] = scratch[6][...].T.astype(BF16)
    d_qkv_ref[:, COLS:] = scratch[7][...].astype(BF16)
    partial_ref[...] = dot(d_qkv_ref[...], w_ref[...], NT)


def partial_kernel(here, d_ref, w_ref, partial_ref):
    partial_ref[...] = dot(d_ref[...], w_ref[...], NT)


def hidden_kernel(here, small_ref, near_ref, far_ref, keep_ref, core_ref, y_ref, hidden_ref, low_ref):
    rows = jnp.concatenate([near_ref[...], far_ref[...]], axis=0).astype(F32)
    hidden = rows + (keep_ref[:ROWS] + core_ref[:ROWS].astype(F32) + y_ref[...].astype(F32))
    hidden_ref[...] = hidden
    low_ref[...] = (hidden * inverse_rms(hidden) * gain_row(small_ref, 1)).astype(BF16)


def tail_kernel(here, keep_ref, core_ref, out_ref):
    first = 0 if keep_ref.shape[0] == ROWS else ROWS
    kept = keep_ref[first : first + ROWS]
    out_ref[...] = (kept + core_ref[core_ref.shape[0] - ROWS :].astype(F32)).astype(BF16)


def pair_kernel(here, near_ref, far_ref, layer_ref, grad_ref):
    for place, ref in ((here[X], near_ref), (1 - here[X], far_ref)):
        layer_ref[place] = ref[0]
        grad_ref[place] = ref[1].astype(F32)


def sums_kernel(here, partial_ref, normed_ref, small_ref, ffn_gain_ref, squares_ref, tile_ref, out_ref):
    out_ref[...] = jnp.zeros(out_ref.shape, F32)
    products = jnp.sum(partial_ref[...] * normed_ref[...].astype(F32), axis=0, keepdims=True)
    out_ref[0:1] = products / gain_row(small_ref, 0)
    out_ref[1:2] = ffn_gain_ref[...]
    out_ref[2:3] = squares_ref[...]
    lane = lax.broadcasted_iota(jnp.int32, (BUCKETS, 128), 1)
    table = jnp.zeros((BUCKETS, 128), F32)
    for head in range(HEADS):
        values = jnp.sum(bucket_sums(tile_ref, head), axis=1, keepdims=True)
        table = table + jnp.where(lane == here[ME] * HEADS + head, values, 0.0)
    for i in range(TP):
        out_ref[8:16, i * 128 : (i + 1) * 128] = table[i * 8 : (i + 1) * 8]


def small_out(here, info_ref, total, attn_gain_ref, ffn_gain_ref, rows_ref, loss_ref):
    for k in range(TP):

        @pl.when(here[ME] == k)
        def _():
            attn_gain_ref[...] = total[0:1, k * OWN : (k + 1) * OWN]
            ffn_gain_ref[...] = total[1:2, k * OWN : (k + 1) * OWN]
            rows_ref[...] = total[8:16, k * 128 : k * 128 + H]

    loss_ref[...] = jnp.sum(total[2:3], axis=1, keepdims=True) / (info_ref[1:2, 0:1] * D)


def small_out_kernel(here, info_ref, total_ref, *outs):
    small_out(here, info_ref, total_ref[...], *outs)


def rows_kernel(here, a_ref, b_ref, c_ref, d_ref, out_ref):
    stack_rows(here, (a_ref, b_ref, c_ref, d_ref), out_ref)


def ffn_body(values, in_ref, outer_ref, active_ref, slope_ref, keep_ref, send_ref):
    for i, ref in enumerate(values):
        rows = slice(i * ROWS, (i + 1) * ROWS)
        active, slope = gelu_and_slope(dot(ref[...], in_ref[...]))
        active_ref[rows] = active.astype(BF16)
        slope_ref[rows] = slope.astype(BF16)
    partial = dot(active_ref[...], outer_ref[...])
    keep_ref[...] = partial[:ROWS]
    send_ref[...] = partial[ROWS:].astype(BF16)


def ffn_kernel(here, own_ref, core_ref, in_ref, outer_ref, *outs):
    ffn_body((own_ref, core_ref), in_ref, outer_ref, *outs)


def loss_kernel(
    tokens, here, hidden_ref, keep_ref, core_ref, y_ref, near_ref, far_ref, info_ref,
    out_near_ref, out_far_ref, grad_ref, low_ref, square_ref,
):
    length = info_ref[0:1, 0:1]
    factor = tokens / info_ref[1:2, 0:1]
    result = hidden_ref[...] + (keep_ref[...] + core_ref[...].astype(F32) + y_ref[...].astype(F32))
    spot = lax.broadcasted_iota(jnp.int32, (PIECE, 1), 0)
    total = jnp.zeros((1, D), F32)
    for i, (teacher, out) in enumerate(((near_ref, out_near_ref), (far_ref, out_far_ref))):
        rows = slice(i * PIECE, (i + 1) * PIECE)
        part = result[rows]
        out[...] = part.astype(BF16)
        valid = ((here[QUERY_BLOCKS + i] * PIECE + spot).astype(F32) < length).astype(F32)
        deviation = (part - teacher[...].astype(F32)) * valid
        total = total + jnp.sum(deviation * deviation, axis=0, keepdims=True)
        grad = deviation * factor
        grad_ref[rows] = grad
        low_ref[rows] = grad.astype(BF16)
    square_ref[...] = total


def ffn_back_kernel(here, own_ref, core_ref, slope_ref, in_ref, outer_ref, inner_ref, keep_ref, send_ref):
    for i, ref in enumerate((own_ref, core_ref)):
        rows = slice(i * ROWS, (i + 1) * ROWS)
        grad = dot(ref[...], outer_ref[...], NT)
        inner_ref[rows] = (slope_ref[rows].astype(F32) * grad).astype(BF16)
    partial = dot(inner_ref[...], in_ref[...], NT)
    keep_ref[...] = partial[:ROWS]
    send_ref[...] = partial[ROWS:].astype(BF16)


def inner_sum(refs):
    inputs, inner = refs[:4], refs[4:6]
    at = [slice(0, ROWS), slice(ROWS, 2 * ROWS)] * 2
    return sum(dot(inputs[i][...], inner[i // 2][at[i]], TN) for i in range(4))


def outer_half(active_ref, own_ref, core_ref):
    return dot(active_ref[:ROWS], own_ref[...], TN) + dot(active_ref[ROWS:], core_ref[...], TN)


def outer_own_kernel(here, active_ref, own_ref, core_ref, out_ref):
    out_ref[...] = outer_half(active_ref, own_ref, core_ref)


def outer_kernel(here, part_ref, active_ref, own_ref, core_ref, out_ref):
    out_ref[...] = (part_ref[...] + outer_half(active_ref, own_ref, core_ref)).astype(BF16)


def outer_halves_kernel(here, part_ref, active_ref, own_ref, core_ref, send, mine, total_ref):
    total_ref[...] = part_ref[...] + outer_half(active_ref, own_ref, core_ref)
    quarter = D // 8
    for x, out in ((1 - here[X], send), (here[X], mine)):
        for z in range(4):
            start = pl.multiple_of((4 * x + z) * quarter, quarter)
            out[z] = total_ref[pl.ds(start, quarter)].astype(BF16)


def inner_kernel(here, *refs):
    refs[6][...] = inner_sum(refs).astype(BF16)


def inner_halves_kernel(here, *refs):
    send, mine, total_ref = refs[6:]
    total_ref[...] = inner_sum(refs)
    for x, out in ((1 - here[X], send), (here[X], mine)):
        for z in range(4):
            for w in range(TP):
                start = pl.multiple_of(w * OWN + (4 * x + z) * DEPTH, 8)
                out[z * TP + w] = total_ref[pl.ds(start, DEPTH)].astype(BF16)


def hidden_back_kernel(
    here, small_ref, hidden_ref, result_grad_ref, keep_ref, core_ref, y_ref, grad_ref, low_ref, gain_grad_ref
):
    upper = keep_ref[...] + core_ref[...].astype(F32) + y_ref[...].astype(F32)
    back, gain_grad_ref[...] = norm_back(hidden_ref[...], gain_row(small_ref, 1), upper)
    grad = result_grad_ref[...] + back
    grad_ref[...] = grad
    low_ref[...] = grad.astype(BF16)


def qkv_grads(normed_ref, d_qkv_ref, put):
    d_qkv = dot(normed_ref[...], d_qkv_ref[...], TN)
    for m in range(3):
        for i in range(TP):
            block = d_qkv[i * OWN : (i + 1) * OWN, m * COLS : (m + 1) * COLS]
            put(m, slice(i * COLS, (i + 1) * COLS), block)


def attention_grads_kernel(here, normed_ref, d_qkv_ref, attn_ref, up_ref, out_ref):
    def put(m, lanes, block):
        out_ref[m, :, lanes] = block.astype(BF16)

    qkv_grads(normed_ref, d_qkv_ref, put)
    out_ref[3] = dot(attn_ref[...].astype(BF16), up_ref[...]).astype(BF16)


SUM_ROWS = 16


def added(ref, other, index):
    return ref[index].astype(F32) + other[index].astype(F32)


def split_low(here, mine, came, send, keep):
    per = mine.shape[0] // 4
    low = here[Z] & 1
    for high in range(2):
        for i in range(per):
            at = high * per + i
            send[at] = added(mine, came, (2 * high + 1 - low) * per + i).astype(BF16)
            keep[at] = added(mine, came, (2 * high + low) * per + i).astype(BF16)


def split_high(here, mine, came, send, keep, *_):
    per = mine.shape[0] // 2
    high = here[Z] >> 1
    for i in range(per):
        send[i] = added(mine, came, (1 - high) * per + i).astype(BF16)
        keep[i] = added(mine, came, high * per + i).astype(BF16)


def finish(here, mine, came, chunk):
    for i in range(mine.shape[0]):
        chunk[i] = added(mine, came, i).astype(BF16)


def join_high(here, mine, came, pair, per=1):
    high = here[Z] >> 1
    for i in range(per):
        pair[high * per + i] = mine[i]
        pair[(1 - high) * per + i] = came[i]


def join_low(here, mine, came, half, per=1):
    low = here[Z] & 1
    for high in range(2):
        for i in range(per):
            half[(2 * high + low) * per + i] = mine[high * per + i]
            half[(2 * high + 1 - low) * per + i] = came[high * per + i]


def outer_rows(here, half, came, out):
    rows = half.shape[1]
    for x, ref in ((here[X], half), (1 - here[X], came)):
        for z in range(4):
            out[pl.ds(pl.multiple_of((4 * x + z) * rows, 8), rows)] = ref[z].astype(F32)


def send_sums(total, send):
    last = send.shape[0] - 1
    high = total.astype(BF16)
    low = (total - high.astype(F32)).astype(BF16)
    send[last, :8] = high[:8]
    send[last, 8:16] = low[:8]
    send[last, 16:, : TP * 128] = high[8:, : TP * 128]


def sums_of(came):
    last = came.shape[0] - 1
    top = came[last, :8].astype(F32) + came[last, 8:16].astype(F32)
    return jnp.concatenate([top, came[last, 16:].astype(F32)], axis=0)


def out_grads(here, attn_ref, a_ref, b_ref, c_ref, d_ref, send_ref, mine_ref, send, mine, total_ref):
    total = None
    for i, ref in enumerate((a_ref, b_ref, c_ref, d_ref)):
        part = dot(attn_ref[:, i * ROWS : (i + 1) * ROWS].astype(BF16), ref[...])
        total = part if total is None else total + part
    total_ref[...] = total
    for x, ref, out in ((1 - here[X], send_ref, send), (here[X], mine_ref, mine)):
        for z in range(4):
            for w in range(TP):
                out[z * (TP + 1) + w] = ref[z * TP + w]
            start = pl.multiple_of((4 * x + z) * DEPTH, 8)
            out[z * (TP + 1) + TP] = total_ref[pl.ds(start, DEPTH)].astype(BF16)


def inner_finish(here, mine, came, sums, own, *others):
    own[0] = added(mine, came, here[ME]).astype(BF16)
    own[1] = added(mine, came, TP).astype(BF16)
    for r, other in enumerate(others):
        other[0] = added(mine, came, here[ME] ^ (r + 1)).astype(BF16)
        send_sums(sums[...], other)


def inner_collect(here, own, a_ref, b_ref, c_ref, sums, chunk, total):
    for r, ref in enumerate((own, a_ref, b_ref, c_ref)):
        chunk[here[ME] ^ r] = ref[0]
    chunk[TP] = own[1]
    value = sums[...]
    for ref in (a_ref, b_ref, c_ref):
        value = value + sums_of(ref)
    total[...] = value
    send_sums(value, chunk)


def inner_high(here, chunk, came, sums, pair, total):
    join_high(here, chunk, came, pair, TP + 1)
    total[...] = sums[...] + sums_of(came)
    send_sums(total[...], pair)


def inner_low(here, pair, came, sums, half, total):
    join_low(here, pair, came, half, TP + 1)
    total[...] = sums[...] + sums_of(came)
    send_sums(total[...], half)


def inner_rows(here, info_ref, half, came, sums, inner_out, out_out, *small):
    for x, ref in ((here[X], half), (1 - here[X], came)):
        for z in range(4):
            rows = pl.ds(pl.multiple_of((4 * x + z) * DEPTH, 8), DEPTH)
            for w in range(TP):
                inner_out[rows, w * D : (w + 1) * D] = ref[z * (TP + 1) + w].astype(F32)
            out_out[rows] = ref[z * (TP + 1) + TP].astype(F32)
    small_out(here, info_ref, sums[...] + sums_of(came), *small)


def qkv_halves_kernel(here, normed_ref, d_qkv_ref, send, mine, total_ref):
    def put(m, lanes, block):
        total_ref[m, :, lanes] = block

    qkv_grads(normed_ref, d_qkv_ref, put)
    for x, out in ((1 - here[X], send), (here[X], mine)):
        for z in range(4):
            start = pl.multiple_of((4 * x + z) * DEPTH, 8)
            for m in range(3):
                out[z * 3 + m] = total_ref[m, pl.ds(start, DEPTH), :].astype(BF16)


def qkv_finish(here, mine, came, *outs):
    for k in range(TP):

        @pl.when(here[ME] == k)
        def _():
            for m in range(3):
                values = added(mine, came, m).astype(BF16)
                for r, out in enumerate(outs):
                    out[m] = values[:, (k ^ r) * COLS : (k ^ r) * COLS + COLS]


def qkv_collect(here, own, a_ref, b_ref, c_ref, chunk):
    for k in range(TP):

        @pl.when(here[ME] == k)
        def _():
            for m in range(3):
                for r, ref in enumerate((own, a_ref, b_ref, c_ref)):
                    chunk[m, :, (k ^ r) * COLS : (k ^ r) * COLS + COLS] = ref[m]


def qkv_high(here, chunk, came, pair):
    join_high(here, chunk, came, pair, 3)


def qkv_low(here, pair, came, half):
    join_low(here, pair, came, half, 3)


def qkv_rows(here, half, came, *outs):
    for x, ref in ((here[X], half), (1 - here[X], came)):
        for z in range(4):
            for m, out in enumerate(outs):
                out[pl.ds(pl.multiple_of((4 * x + z) * DEPTH, 8), DEPTH)] = ref[z * 3 + m].astype(F32)


def input_kernel(
    here, small_ref, near_ref, far_ref, hidden_grad_ref, keep_ref, core_ref, layer_near_ref, layer_far_ref, y_ref,
    out_near_ref, out_far_ref,
):
    values = jnp.concatenate([near_ref[...], far_ref[...]], axis=0).astype(F32)
    upper = keep_ref[:ROWS] + core_ref[:ROWS].astype(F32) + y_ref[...].astype(F32)
    back, _ = norm_back(values, gain_row(small_ref, 0), upper)
    grad = (hidden_grad_ref[...] + back).astype(BF16)
    out_near_ref[0] = layer_near_ref[...]
    out_near_ref[1] = grad[:PIECE]
    out_far_ref[0] = layer_far_ref[...]
    out_far_ref[1] = grad[PIECE:]


def on_device(
    inputs, teacher, seq_lengths, gain_attn, w_query, w_key, w_value, w_out, bias_table, gain_ffn, w_inner, w_outer
):
    n_ctx = lax.axis_size("ctx")
    spread = n_ctx // (SEQ_DEV * TP)
    me = lax.axis_index("wsh")
    ctx_me = lax.axis_index("ctx")
    parity = ctx_me & 1
    token_total = ROWS * n_ctx * TP
    same, cross = seq_routes(n_ctx)
    home = ctx_me // spread
    stretch = ctx_me % spread
    seq_bit = home & 1
    by_steps = n_ctx == 8

    def to_home(pair):
        return lax.ppermute(pair[0], AXES, same), lax.ppermute(pair[1], AXES, cross)

    def from_home(near, far):
        near = lax.ppermute(near, AXES, backwards(same))
        far = lax.ppermute(far, AXES, backwards(cross))
        return near, far

    def block_places(stretch_index):
        return [
            TP * 2 * stretch_index + 2 * swapped(me ^ r) + (seq_bit ^ e) for r in ORDER for e in (0, 1)
        ]

    query_blocks = block_places(stretch)
    key_blocks = [p for i in range(spread) for p in block_places(i)] if spread > 1 else query_blocks

    scalars = [me, parity, (ctx_me >> 1) & 3, swapped(home >> 1), seq_bit] + query_blocks + key_blocks
    here = jnp.stack([jnp.asarray(v, jnp.int32) for v in scalars])

    low = functools.partial(shape, dtype=BF16)
    x_here, x_there, *qkv_blocks = call(
        start_kernel,
        (low(PIECE, D),) * 2 + (low(OWN + 16, 3 * COLS),) * 4,
        (here, inputs, w_query, w_key, w_value, gain_attn, gain_ffn, bias_table, seq_lengths),
        scratch=(pltpu.VMEM((16, 3 * COLS), F32),) + (pltpu.VMEM((OWN, D), BF16),) * 3
        + (pltpu.VMEM((OWN,), BF16),) * 2 + (pltpu.VMEM((8, H), BF16), pltpu.VMEM((SEQ_DEV,), jnp.int32))
        + (pltpu.SemaphoreType.DMA((9,)),),
        mib=START_MIB,
        in_hbm=8,
    )
    x_near, x_far = to_home((x_here, x_there))

    def group_blocks(values):
        return (values[0],) + tuple(to_partner(values[r], r) for r in (1, 2, 3))

    w_qkv_pieces = group_blocks(qkv_blocks)
    (small, info, bias), (w_qkv,) = run(
        here,
        (
            functools.partial(bias_kernel, float(n_ctx * PIECE)),
            (shape(TP, 16, 3 * COLS), shape(8, 128), shape(HEADS, 5, PIECE, PIECE)),
            w_qkv_pieces,
        ),
        (rows_kernel, (low(D, 3 * COLS),), w_qkv_pieces),
    )
    x_own = (x_near, x_far)
    *teacher_halves, in_own, in_core, in_across = call(
        inner_blocks_kernel,
        (low(PIECE, D),) * 2 + (low(OWN, D),) * 2 + (low(2, OWN // 2, D),),
        (here, after(w_inner, w_qkv), teacher),
    )
    x_y = tuple(to_partner(v, 2) for v in x_own)
    x_y = tuple(after(v, w_qkv) for v in x_y)
    pieces = x_own + x_y + tuple(to_partner(v, 1) for v in x_own + x_y)
    attn_shapes = (shape(COLS, GROUP), shape(8, GROUP), shape(GROUP, D))
    send_job = (send_kernel, (low(2 * ROWS, D),))
    proj_shapes = (low(GROUP, D), low(GROUP, 3 * COLS))

    def attn_scratch(keys, chunk):
        return (pltpu.VMEM((keys, chunk), F32), pltpu.VMEM((keys, chunk), BF16))

    if spread == 1:
        normed, qkv, attn_t, lse, partial = call(
            front_kernel,
            proj_shapes + attn_shapes,
            (here, small) + pieces + (w_qkv, info, bias, w_out),
            scratch=attn_scratch(GROUP, 512),
            mib=14,
        )
    else:
        teams = [[s * spread + i for i in range(spread)] for s in range(SEQ_DEV * TP)]
        normed, qkv = call(project_kernel, proj_shapes, (here, small) + pieces + (w_qkv,))
        kv = lax.all_gather(qkv[:, COLS:], "ctx", axis=0, tiled=True, axis_index_groups=teams)
        q = qkv[:, :COLS]
        attn_t, lse, partial = call(
            functools.partial(attention_kernel, 128, (0, COLS)),
            attn_shapes,
            (here, q, kv, info, bias, w_out),
            scratch=attn_scratch(kv.shape[0], 128),
            mib=56,
        )

    def scatter_tail(keep_y, from_core):
        return call(tail_kernel, (low(ROWS, D),), (here, keep_y, from_core))[0]

    from_y = to_partner(after(in_across, *x_y), 2)
    teacher_near, teacher_far = to_home([after(v, *x_y) for v in teacher_halves])
    partial, from_y, teacher_near, teacher_far = lax.optimization_barrier((partial, from_y, teacher_near, teacher_far))
    ((send,),) = run(here, send_job + ((partial,),))
    core = to_partner(send, 1)
    from_x = to_ctx(after(from_y, send), 1)
    in_core = to_partner(after(in_core, send), 1)
    going = scatter_tail(partial, core)
    across = to_partner(going, 2)
    hidden, ffn_low = call(
        hidden_kernel,
        (shape(ROWS, D), low(ROWS, D)),
        (here, small, x_near, x_far, partial, core, across),
    )
    core_y, core_x = to_partner(after(from_y, send), 1), to_partner(after(from_x, ffn_low), 1)
    (w_in,) = call(
        inner_rows_kernel, (low(D, D),), (here, after(in_own, ffn_low), in_core, from_y, from_x, core_y, core_x)
    )

    def gathered(value):
        from_y = to_partner(value, 2)
        return to_partner(value, 1), from_y

    def both_halves(first_call, second_call, value):
        from_core, from_y = gathered(value)
        first, done = first_call((value, from_core))
        core_y = to_partner(after(from_y, done), 1)
        second = second_call((from_y, core_y))
        core_own = to_partner(first[-1], 1)
        going = scatter_tail(second[-2], to_partner(second[-1], 1))
        across = to_partner(going, 2)
        return (value, from_core, from_y, core_y), first, second, (first[-2], core_own, across), going

    half = low(2 * ROWS, D)
    piece_shapes = (shape(ROWS, D), low(ROWS, D))
    def ffn(values):
        return call(ffn_kernel, (half, half) + piece_shapes, (here,) + values + (w_in, w_outer))

    def ffn_first(values):
        outs = ffn(values)
        return outs, outs[-1]

    ffn_all, (active_a, slope_a, *_), (active_b, slope_b, *_), parts, _ = both_halves(ffn_first, ffn, ffn_low)
    out_near, out_far, result_grad, result_low, squares = call(
        functools.partial(loss_kernel, float(token_total)),
        (low(PIECE, D), low(PIECE, D), shape(ROWS, D), low(ROWS, D), shape(1, D)),
        (here, hidden) + parts + (teacher_near, teacher_far, info),
    )

    depth = OWN // n_ctx

    def parts_of(count, rows=DEPTH):
        return low(count, rows, D)

    def ffn_back(values, slope):
        return call(ffn_back_kernel, (half,) + piece_shapes, (here,) + values + (slope, w_in, w_outer))

    def ffn_back_first(values):
        outs = ffn_back(values, slope_a)
        (part,) = call(
            outer_own_kernel, (shape(D, D),), (here, after(active_a, outs[-1])) + values, mib=12
        )
        grads.append(part)
        return outs, part

    def ffn_back_second(values):
        args = (here, grads[0], active_b) + values
        if by_steps:
            outs = (parts_of(4, D // 8),) * 2
            grads[:] = call(outer_halves_kernel, outs, args, scratch=(pltpu.VMEM((D, D), F32),), mib=14)
        else:
            grads[:] = call(outer_kernel, (low(D, D),), args, mib=12)
        return ffn_back((after(values[0], grads[0]), values[1]), slope_b)

    grads = []
    result_all, (inner_a, *_), (inner_b, *_), parts, going = both_halves(
        ffn_back_first, ffn_back_second, result_low
    )
    inner_args = (here,) + ffn_all + (inner_a, after(inner_b, going))
    ahead = []
    if by_steps:
        outer_send, outer_mine = grads
        outer_came = to_ctx(outer_send, 1)
        inner_send, inner_mine = call(
            inner_halves_kernel, (parts_of(4 * TP),) * 2, inner_args, scratch=(pltpu.VMEM((D, D), F32),), mib=14
        )
        ordered = inner_send
        ahead.append((split_low, (parts_of(2, D // 8),) * 2, (outer_mine, outer_came)))
    else:
        (outer_wgrad,) = grads
        (inner_wgrad,) = call(inner_kernel, (low(D, D),), inner_args, mib=14)
        ordered = inner_wgrad
    (hidden_grad, hidden_low, ffn_gain_grad), *ahead = run(
        here,
        (
            hidden_back_kernel,
            (shape(ROWS, D), low(ROWS, D), shape(1, D)),
            (small, after(hidden, ordered), result_grad) + parts,
        ),
        *ahead,
    )
    from_core, from_y = gathered(hidden_low)
    if by_steps:
        ((outer_send, outer_keep),) = ahead
        outer_came = to_ctx(outer_send, 2)
        from_y = after(from_y, outer_came)
    up_pieces = (hidden_low, from_y, from_core, to_partner(from_y, 1))
    table_shape = shape(HEADS, 5, PIECE, PIECE)
    if by_steps:
        (inner_send, inner_mine), (outer_send, outer_keep) = run(
            here,
            (
                out_grads,
                (parts_of(4 * TP + 4),) * 2,
                (attn_t,) + up_pieces + (inner_send, inner_mine),
            ),
            (split_high, (parts_of(1, D // 8),) * 2, (outer_keep, outer_came)),
            scratch=(pltpu.VMEM((OWN, D), F32),),
        )
        inner_came = to_ctx(inner_send, 1)
        outer_came = to_ctx(outer_send, 4)
        up_pieces = (after(hidden_low, outer_keep),) + up_pieces[1:]
    if spread == 1:
        d_qkv, table_part, partial = call(
            back_kernel,
            (proj_shapes[1], table_shape, shape(GROUP, D)),
            (here, qkv, info, bias, w_out, attn_t, lse, w_qkv) + up_pieces,
            scratch=back_scratch(GROUP, 256),
            mib=20,
        )
    else:
        dq, dkv, table_part = call(
            functools.partial(attention_back_kernel, 128, (0, COLS)),
            (low(GROUP, COLS), low(kv.shape[0], 2 * COLS), table_shape),
            (here, q, kv, info, bias, w_out, attn_t, lse) + up_pieces,
            scratch=back_scratch(kv.shape[0], 128),
            mib=60,
        )
        dkv = lax.psum_scatter(dkv, "ctx", scatter_dimension=0, tiled=True, axis_index_groups=teams)
        d_qkv = jnp.concatenate([dq, dkv], axis=1)
        (partial,) = call(partial_kernel, (shape(GROUP, D),), (here, d_qkv, w_qkv))
    if by_steps:
        (send,), (outer_chunk,), (inner_send, inner_keep) = run(
            here,
            send_job + ((partial,),),
            (finish, (parts_of(1, D // 8),), (outer_keep, outer_came)),
            (split_low, (parts_of(2 * TP + 2),) * 2, (inner_mine, inner_came)),
        )
        outer_came = to_ctx(outer_chunk, 4)
        inner_came = to_ctx(inner_send, 2)
    else:
        ((send,),) = run(here, send_job + ((partial,),))
    core = to_partner(send, 1)
    input_job = (
        input_kernel,
        (low(2, PIECE, D), low(2, PIECE, D)),
        (small, x_near, x_far, hidden_grad, partial, core, out_near, out_far),
    )
    small_shapes = (shape(1, OWN), shape(1, OWN), shape(8, H), shape(1, 1))
    sums_shape = shape(SUM_ROWS, D)
    pair_out = (low(SEQ_DEV, PIECE, D), shape(SEQ_DEV, PIECE, D))
    sum_args = (partial, normed, small, ffn_gain_grad, squares, table_part)

    if by_steps:
        going = scatter_tail(partial, core)
        across = to_partner(going, 2)
        qkv_send, qkv_mine = call(
            qkv_halves_kernel,
            (parts_of(12),) * 2,
            (here, normed, after(d_qkv, going)),
            scratch=(pltpu.VMEM((3, OWN, D), F32),),
        )
        qkv_came = to_ctx(qkv_send, 1)
        inner_keep, across = lax.optimization_barrier((after(inner_keep, qkv_send), across))
        (inner_send, inner_keep), (outer_pair,) = run(
            here,
            (split_high, (parts_of(TP + 1),) * 2, (inner_keep, inner_came)),
            (join_high, (parts_of(2, D // 8),), (outer_chunk, outer_came)),
        )
        inner_came = to_ctx(inner_send, 4)
        outer_came = to_ctx(outer_pair, 2)
        ((in_near, in_far),) = run(
            here, (input_job[0], input_job[1], input_job[2] + (after(across, inner_keep),))
        )
        home_near, home_far = from_home(in_near, in_far)
        ((qkv_send, qkv_keep),) = run(
            here, (split_low, (parts_of(6),) * 2, (after(qkv_mine, in_near), qkv_came))
        )
        qkv_came = to_ctx(qkv_send, 2)
        (sums,) = call(sums_kernel, (sums_shape,), (here, after(partial, qkv_send)) + sum_args[1:])
        inner_blocks, (outer_half,) = run(
            here,
            (
                inner_finish,
                (parts_of(2),) + (parts_of(1 + 1),) * 3,
                (after(inner_keep, qkv_keep), inner_came, sums),
            ),
            (join_low, (parts_of(4, D // 8),), (outer_pair, outer_came)),
        )
        inner_blocks = group_blocks(inner_blocks)
        outer_came = to_ctx(outer_half, 1)
        ((qkv_send, qkv_keep),) = run(
            here, (split_high, (parts_of(3),) * 2, (after(qkv_keep, outer_half), qkv_came))
        )
        qkv_came = to_ctx(qkv_send, 4)
        ((inner_chunk, sums),) = run(
            here,
            (
                inner_collect,
                (parts_of(TP + 1 + 1), sums_shape),
                (after(inner_blocks[0], qkv_keep, home_far),) + inner_blocks[1:] + (sums,),
            ),
        )
        inner_came = to_ctx(inner_chunk, 4)
        (qkv_blocks,) = run(
            here, (qkv_finish, (low(3, DEPTH, COLS),) * 4, (after(qkv_keep, inner_chunk), qkv_came))
        )
        qkv_blocks = group_blocks(qkv_blocks)
        (inner_pair, sums), (w_outer_grad,) = run(
            here,
            (
                inner_high,
                (parts_of(2 * TP + 2 + 1), sums_shape),
                (after(inner_chunk, qkv_blocks[0]), inner_came, sums),
            ),
            (outer_rows, (shape(D, D),), (outer_half, outer_came)),
        )
        inner_came = to_ctx(inner_pair, 2)
        ((qkv_chunk,),) = run(
            here, (qkv_collect, (parts_of(3),), (after(qkv_blocks[0], inner_pair),) + qkv_blocks[1:])
        )
        qkv_came = to_ctx(qkv_chunk, 4)
        ((inner_half, sums),) = run(
            here,
            (
                inner_low,
                (parts_of(4 * TP + 4 + 1), sums_shape),
                (after(inner_pair, qkv_chunk), inner_came, sums),
            ),
        )
        inner_came = to_ctx(inner_half, 1)
        ((qkv_pair,),) = run(here, (qkv_high, (parts_of(6),), (after(qkv_chunk, inner_half), qkv_came)))
        qkv_came = to_ctx(qkv_pair, 2)
        ((qkv_half,),) = run(here, (qkv_low, (parts_of(12),), (qkv_pair, qkv_came)))
        qkv_came = to_ctx(qkv_half, 1)
        ((w_inner_grad, w_out_grad, my_attn_gain, my_ffn_gain, my_rows, loss_value),) = run(
            here,
            (
                inner_rows,
                (shape(OWN, TP * D), shape(OWN, D)) + small_shapes,
                (info, after(inner_half, qkv_half), inner_came, sums),
            ),
        )
        (layer_out, input_grad), (w_query_grad, w_key_grad, w_value_grad) = run(
            here,
            (pair_kernel, pair_out, (home_near, home_far)),
            (qkv_rows, (shape(OWN, D),) * 3, (after(qkv_half, w_out_grad), qkv_came)),
        )
    else:
        across = to_partner(scatter_tail(partial, core), 2)
        ((in_near, in_far),) = run(here, (input_job[0], input_job[1], input_job[2] + (across,)))
        ((layer_out, input_grad),) = run(here, (pair_kernel, pair_out, from_home(in_near, in_far)))
        (sums,) = call(sums_kernel, (sums_shape,), (here,) + sum_args)
        (hidden_all,) = call(join_kernel, (low(GROUP, D),), (here,) + up_pieces)
        my_attn_gain, my_ffn_gain, my_rows, loss_value = call(
            small_out_kernel, small_shapes, (here, info, lax.psum(sums, AXES))
        )

        def summed(parts):
            return lax.psum_scatter(parts, "ctx", scatter_dimension=0)

        def inner_to_rows(chunk):
            return swap_blocks(chunk, "wsh").transpose(1, 0, 2).reshape(depth, TP * D)

        def attn_to_rows(chunk):
            blocks = chunk[:3].reshape(3, depth, TP, COLS).transpose(2, 0, 1, 3)
            mine = swap_blocks(blocks, "wsh").transpose(1, 2, 0, 3).reshape(3, depth, D)
            return jnp.concatenate([mine, chunk[3:]])

        (attn_wgrad,) = call(
            attention_grads_kernel, (low(4, OWN, D),), (here, normed, d_qkv, attn_t, hidden_all)
        )
        outer_full = lax.all_gather(summed(outer_wgrad.reshape(n_ctx, D // n_ctx, D)), "ctx")
        inner_parts = inner_wgrad.reshape(TP, n_ctx, depth, D).transpose(1, 0, 2, 3)
        inner_full = lax.all_gather(inner_to_rows(summed(inner_parts)), "ctx")
        attn_parts = attn_wgrad.reshape(4, n_ctx, depth, D).transpose(1, 0, 2, 3)
        attn_full = lax.all_gather(attn_to_rows(summed(attn_parts)), "ctx")
        w_outer_grad = outer_full.reshape(D, D).astype(F32)
        w_inner_grad = inner_full.reshape(OWN, TP * D).astype(F32)
        w_query_grad, w_key_grad, w_value_grad, w_out_grad = (
            attn_full[:, m].reshape(OWN, D).astype(F32) for m in range(4)
        )

    return (
        layer_out,
        loss_value.reshape(()),
        input_grad,
        my_attn_gain.reshape(-1),
        w_query_grad,
        w_key_grad,
        w_value_grad,
        w_out_grad,
        my_rows,
        my_ffn_gain.reshape(-1),
        w_inner_grad,
        w_outer_grad,
    )


def solution(mesh):
    rows = P("wsh", None)
    tokens = P("wsh", "ctx", None)
    return jax.shard_map(
        on_device,
        mesh=mesh,
        in_specs=(tokens, tokens, P("wsh"), P("wsh"), rows, rows, rows, rows, rows, P("wsh"), rows, rows),
        out_specs=(tokens, P(), tokens, P("wsh"), rows, rows, rows, rows, rows, P("wsh"), rows, rows),
        check_vma=False,
    )
```

```python
import functools

import jax
import jax.numpy as jnp
from jax import lax
from jax.experimental import pallas as pl
from jax.experimental.pallas import tpu as pltpu
from jax.sharding import PartitionSpec as P

D = 768
H = 12
DH = 64
BUCKETS = 32
SEQ_DEV = 2
PIECE = 128
TP = 4
HEADS = H // TP
COLS = HEADS * DH
OWN = D // TP
ROWS = SEQ_DEV * PIECE
GROUP = ROWS * TP
DEPTH = OWN // 8
START_MIB = 60
EPS = 1e-06
NEG_FILL = -1e30
BUCKET_EDGES = (12, 16, 23, 32, 46, 64, 91)
AXES = ("ctx", "wsh")
ORDER = (0, 2, 1, 3)

ME, X, Z, SEQ_OWNER, SEQ_BIT, QUERY_BLOCKS = range(6)
KEY_BLOCKS = QUERY_BLOCKS + 8

BF16 = jnp.bfloat16
F32 = jnp.float32
NT = (((1,), (1,)), ((), ()))
TN = (((0,), (0,)), ((), ()))
NN = (((1,), (0,)), ((), ()))


def dot(left, right, dims=NN):
    return lax.dot_general(left, right, dims, preferred_element_type=F32)


def swapped(index):
    return (index & 1) * 2 + (index >> 1)


def seq_routes(n_ctx):
    spread = n_ctx // (SEQ_DEV * TP)
    same, cross = [], []
    for c in range(n_ctx):
        for w in range(TP):
            pair = c // 2
            for b in range(2):
                home = (2 * swapped(w) + b) * spread + pair // TP
                route = (c * TP + w, home * TP + swapped(pair % TP))
                (same if b == c % 2 else cross).append(route)
    return same, cross


def backwards(routes):
    return [(there, here) for here, there in routes]


def to_partner(value, offset):
    return lax.ppermute(value, "wsh", [(i, i ^ offset) for i in range(TP)])


def to_ctx(value, offset):
    n_ctx = lax.axis_size("ctx")
    return lax.ppermute(value, "ctx", [(i, i ^ offset) for i in range(n_ctx)])


def swap_blocks(blocks, axis, groups=None):
    return lax.all_to_all(blocks, axis, 0, 0, tiled=True, axis_index_groups=groups)


def pick(stack, index):
    return lax.dynamic_index_in_dim(stack, index, 0, keepdims=False)


def after(value, *earlier):
    return lax.optimization_barrier((value,) + earlier)[0]


def bucket_index(offset):
    distance = jnp.abs(offset)
    far_bucket = 8 + sum(((distance >= edge).astype(jnp.int32) for edge in BUCKET_EDGES))
    near_or_far = jnp.where(distance < 8, distance, far_bucket)
    return near_or_far + jnp.where(offset > 0, 16, 0)


def gelu_and_slope(values):
    cumulative = 0.5 * (1.0 + lax.erf(values * 0.7071067811865476))
    density = jnp.exp(-0.5 * values * values) * 0.3989422804014327
    return values * cumulative, cumulative + values * density


def inverse_rms(values):
    return lax.rsqrt(jnp.mean(values * values, axis=-1, keepdims=True) + EPS)


def norm_back(values, gain, grad):
    scale = inverse_rms(values)
    unit = values * scale
    scaled = gain * grad
    back = scale * (scaled - unit * jnp.mean(scaled * unit, axis=-1, keepdims=True))
    return back, jnp.sum(grad * unit, axis=0, keepdims=True)


def repeat(count, unroll, body, carry):
    if unroll:
        for index in range(count):
            carry = body(index, carry)
        return carry
    return lax.fori_loop(0, count, body, carry)


def vmem():
    return pl.BlockSpec(memory_space=pltpu.VMEM)


def smem():
    return pl.BlockSpec(memory_space=pltpu.SMEM)


def shape(*dims, dtype=F32):
    return jax.ShapeDtypeStruct(dims, dtype)


def hbm():
    return pl.BlockSpec(memory_space=pl.ANY)


def name_of(body):
    return (body.func if isinstance(body, functools.partial) else body).__name__


def run(here, *jobs, scratch=(), mib=10, weight=1):
    args = [a for _, _, given in jobs for a in given]
    outs = [o for _, made, _ in jobs for o in made]

    def bodies(here, *refs):
        ins, rest = refs[: len(args)], refs[len(args) :]
        made, extra = rest[: len(outs)], rest[len(outs) :]
        i = o = 0
        for body, shapes, given in jobs:
            body(here, *ins[i : i + len(given)], *made[o : o + len(shapes)], *extra)
            i, o = i + len(given), o + len(shapes)

    bodies.__name__ = "_".join(name_of(body) for body, _, _ in jobs)
    results = list(call(bodies, outs, [here] + args, scratch, mib, weight=weight))
    return [tuple(results.pop(0) for _ in made) for _, made, _ in jobs]


def call(body, outs, args, scratch=(), mib=10, in_hbm=0, weight=1):
    return pl.pallas_call(
        body,
        name=name_of(body),
        out_shape=tuple(outs),
        in_specs=[smem()] + [hbm()] * in_hbm + [vmem()] * (len(args) - 1 - in_hbm),
        out_specs=(vmem(),) * len(outs),
        scratch_shapes=tuple(scratch),
        compiler_params=pltpu.CompilerParams(vmem_limit_bytes=mib * 2**20),
        cost_estimate=pl.CostEstimate(flops=int(2e9 * weight), bytes_accessed=int(2**23 * weight), transcendentals=0),
    )(*args)


def start_kernel(
    here, x_hbm, wq_hbm, wk_hbm, wv_hbm, gain_a_hbm, gain_f_hbm, table_hbm, lengths_hbm, *refs
):
    halves, outs, small_ref = refs[:2], refs[2:6], refs[6]
    weights, (gain_a_ref, gain_f_ref, table_ref, lengths_ref), sems = refs[7:10], refs[10:14], refs[14]
    moves = [(x_hbm.at[here[X]], halves[0]), (x_hbm.at[1 - here[X]], halves[1])]
    moves += list(zip((wq_hbm, wk_hbm, wv_hbm), weights))
    moves += [(gain_a_hbm, gain_a_ref), (gain_f_hbm, gain_f_ref), (table_hbm, table_ref), (lengths_hbm, lengths_ref)]
    copies = [pltpu.make_async_copy(src, dst, sems.at[i]) for i, (src, dst) in enumerate(moves)]
    for copy in copies:
        copy.start()
    small_ref[...] = jnp.zeros(small_ref.shape, F32)
    for copy in copies:
        copy.wait()
    small_ref[0:1, :OWN] = gain_a_ref[...].astype(F32).reshape(1, OWN)
    small_ref[1:2, :OWN] = gain_f_ref[...].astype(F32).reshape(1, OWN)
    lengths = lengths_ref[...].reshape(1, SEQ_DEV)
    high = lengths >> 7
    small_ref[2:3, :SEQ_DEV] = high.astype(F32)
    small_ref[3:4, :SEQ_DEV] = (lengths - high * 128).astype(F32)
    small_ref[8:16, :H] = table_ref[...].astype(F32)
    for k in range(TP):

        @pl.when(here[ME] == k)
        def _():
            for r in range(TP):
                for m, ref in enumerate(weights):
                    outs[r][:OWN, m * COLS : (m + 1) * COLS] = ref[:, (k ^ r) * COLS : (k ^ r) * COLS + COLS]

    for out in outs:
        out[OWN:] = small_ref[...].astype(BF16)


def inner_blocks_kernel(here, inner_ref, teacher_ref, near_ref, far_ref, own_ref, core_ref, across_ref):
    near_ref[...] = teacher_ref[here[X]]
    far_ref[...] = teacher_ref[1 - here[X]]

    def lanes(r):
        return pl.ds(pl.multiple_of((here[ME] ^ r) * D, D), D)

    own_ref[...] = inner_ref[:, lanes(0)]
    core_ref[...] = inner_ref[:, lanes(1)]
    rows = across_ref.shape[1]
    for i in range(2):
        across_ref[i] = inner_ref[pl.ds(pl.multiple_of(here[X] * rows, rows), rows), lanes(2 + i)]


def inner_rows_kernel(here, own_ref, core_ref, y_ref, x_ref, core_y_ref, core_x_ref, out_ref):
    rows = y_ref.shape[1]
    me, x = here[ME], here[X]
    out_ref[pl.ds(pl.multiple_of(me * OWN, OWN), OWN)] = own_ref[...]
    out_ref[pl.ds(pl.multiple_of((me ^ 1) * OWN, OWN), OWN)] = core_ref[...]
    for r, ref, half in ((2, y_ref, x), (2, x_ref, 1 - x), (3, core_y_ref, x), (3, core_x_ref, 1 - x)):
        start = (me ^ r) * OWN + half * rows
        out_ref[pl.ds(pl.multiple_of(start, rows), rows)] = ref[r - 2]


def gain_row(small_ref, row):
    return jnp.concatenate([small_ref[i, row : row + 1, :OWN] for i in range(TP)], axis=1)


def bias_kernel(longest, here, small_a, small_b, small_c, small_d, small_ref, info_ref, bias_ref):
    for r, ref in enumerate((small_a, small_b, small_c, small_d)):
        small_ref[here[ME] ^ r] = ref[OWN:].astype(F32)
    pair = lax.broadcasted_iota(jnp.int32, (1, SEQ_DEV), 1)
    length = jnp.zeros((1, 1), F32)
    count = jnp.zeros((1, 1), F32)
    for i in range(TP):
        lengths = small_ref[i, 2:3, :SEQ_DEV] * 128.0 + small_ref[i, 3:4, :SEQ_DEV]
        mine = (pair == here[SEQ_BIT]) & (here[SEQ_OWNER] == i)
        length = length + jnp.sum(jnp.where(mine, lengths, 0.0), axis=1, keepdims=True)
        count = count + jnp.sum(jnp.minimum(lengths, longest), axis=1, keepdims=True)
    info_ref[0:1, :] = jnp.broadcast_to(length, (1, 128))
    info_ref[1:2, :] = jnp.broadcast_to(count, (1, 128))
    table = jnp.concatenate([small_ref[i, 8:16, :] for i in range(TP)], axis=0)
    lane = lax.broadcasted_iota(jnp.int32, table.shape, 1)
    apart = lax.broadcasted_iota(jnp.int32, (PIECE, PIECE), 0) - lax.broadcasted_iota(
        jnp.int32, (PIECE, PIECE), 1
    )
    for head in range(HEADS):
        values = jnp.sum(jnp.where(lane == here[ME] * HEADS + head, table, 0.0), axis=1, keepdims=True)
        for tile in range(5):
            low, high = ((15, 16), (1, 16), (0, 32), (17, 32), (31, 32))[tile]
            ids = bucket_index(apart + (tile - 2) * PIECE)
            total = jnp.broadcast_to(values[low : low + 1], (PIECE, PIECE))
            for b in range(low + 1, high):
                total = jnp.where(ids == b, values[b : b + 1], total)
            bias_ref[head, tile] = total


def block_bias(bias_ref, here, head, key_block, query_block, blocks):
    tiles = []
    for i in range(blocks):
        apart = here[KEY_BLOCKS + key_block] - here[QUERY_BLOCKS + query_block + i]
        tiles.append(bias_ref[head, jnp.clip(apart, -2, 2) + 2])
    return tiles[0] if blocks == 1 else jnp.concatenate(tiles, axis=1)


def attend(chunk, offsets, here, q_ref, kv_ref, info_ref, bias_ref, attn_ref, lse_ref, s_ref, p_ref):
    key_blocks = kv_ref.shape[0] // PIECE
    length = info_ref[0:1, 0:1]
    k_off, v_off = offsets
    blocks = chunk // PIECE
    unroll = key_blocks <= 8
    key_iota = lax.broadcasted_iota(jnp.int32, (PIECE, 1), 0)
    for head in range(HEADS):
        lanes = slice(head * DH, head * DH + DH)
        key_part = kv_ref[:, k_off + head * DH : k_off + head * DH + DH]
        value_part = kv_ref[:, v_off + head * DH : v_off + head * DH + DH]

        def for_queries(q_chunk, carry):
            rows = pl.ds(pl.multiple_of(q_chunk * chunk, chunk), chunk)
            s_ref[...] = dot(key_part, q_ref[rows, lanes], NT)

            def score(index, top):
                at = pl.ds(pl.multiple_of(index * PIECE, PIECE), PIECE)
                tile = s_ref[at, :] + block_bias(bias_ref, here, head, index, q_chunk * blocks, blocks)
                ok = (here[KEY_BLOCKS + index] * PIECE + key_iota).astype(F32) < length
                tile = jnp.where(ok, tile, NEG_FILL)
                s_ref[at, :] = tile
                return jnp.maximum(top, jnp.max(tile, axis=0, keepdims=True))

            top = repeat(key_blocks, unroll, score, jnp.full((1, chunk), NEG_FILL, F32))

            def weigh(index, total):
                at = pl.ds(pl.multiple_of(index * PIECE, PIECE), PIECE)
                weight = jnp.exp(s_ref[at, :] - top)
                p_ref[at, :] = weight.astype(BF16)
                return total + jnp.sum(weight, axis=0, keepdims=True)

            total = repeat(key_blocks, unroll, weigh, jnp.zeros((1, chunk), F32))
            attn_ref[lanes, rows] = dot(value_part, p_ref[...], TN) / total
            lse_ref[head : head + 1, rows] = top + jnp.log(total)
            return carry

        repeat(GROUP // chunk, unroll, for_queries, 0)


def send_kernel(here, partial_ref, send_ref, *_):
    send_ref[...] = partial_ref[2 * ROWS :].astype(BF16)


def stack_rows(here, pieces, out_ref):
    for r, piece in enumerate(pieces):
        out_ref[pl.ds(pl.multiple_of((here[ME] ^ r) * OWN, OWN), OWN)] = piece[:OWN]


def project(here, small_ref, pieces, w_ref, normed_ref, qkv_ref):
    gain = gain_row(small_ref, 0)
    for i, piece in enumerate(pieces):
        values = piece[...].astype(F32)
        normed_ref[i * PIECE : (i + 1) * PIECE] = (values * inverse_rms(values) * gain).astype(BF16)
    qkv_ref[...] = dot(normed_ref[...], w_ref[...]).astype(BF16)


def project_kernel(here, small_ref, *refs):
    project(here, small_ref, refs[:8], *refs[8:])


def attention_kernel(chunk, offsets, here, q_ref, kv_ref, info_ref, bias_ref, out_w_ref, *refs):
    attn_ref, lse_ref, partial_ref, s_ref, p_ref = refs
    attend(chunk, offsets, here, q_ref, kv_ref, info_ref, bias_ref, attn_ref, lse_ref, s_ref, p_ref)
    partial_ref[...] = dot(attn_ref[...].astype(BF16), out_w_ref[...], TN)


def front_kernel(here, small_ref, *refs):
    pieces, (w_ref, info_ref, bias_ref, out_w_ref), (normed_ref, qkv_ref) = refs[:8], refs[8:12], refs[12:14]
    project(here, small_ref, pieces, w_ref, normed_ref, qkv_ref)
    attention_kernel(512, (COLS, 2 * COLS), here, qkv_ref, qkv_ref, info_ref, bias_ref, out_w_ref, *refs[14:])


def attend_back(
    chunk, offsets, here, q_ref, kv_ref, info_ref, bias_ref, out_w_ref, pieces, attn_ref, lse_ref,
    tile_ref, s_ref, dp_ref, p_ref, ds_ref, do_ref, outdot_ref, dqt_ref, dkv_ref,
):
    key_blocks = kv_ref.shape[0] // PIECE
    length = info_ref[0:1, 0:1]
    k_off, v_off = offsets
    blocks = chunk // PIECE
    unroll = key_blocks <= 8
    key_iota = lax.broadcasted_iota(jnp.int32, (PIECE, 1), 0)
    for i, piece in enumerate(pieces):
        at = slice(i * ROWS, (i + 1) * ROWS)
        do_ref[at] = dot(piece[...], out_w_ref[...], NT).astype(BF16)
        do_t = dot(out_w_ref[...], piece[...], NT).astype(BF16).astype(F32) * attn_ref[:, at]
        for head in range(HEADS):
            outdot_ref[head : head + 1, at] = jnp.sum(do_t[head * DH : head * DH + DH], axis=0, keepdims=True)
    tile_ref[...] = jnp.zeros_like(tile_ref)
    dkv_ref[...] = jnp.zeros_like(dkv_ref)
    for head in range(HEADS):
        lanes = slice(head * DH, head * DH + DH)
        v_lanes = slice(COLS + head * DH, COLS + head * DH + DH)
        key_part = kv_ref[:, k_off + head * DH : k_off + head * DH + DH]
        value_part = kv_ref[:, v_off + head * DH : v_off + head * DH + DH]

        def for_queries(q_chunk, carry):
            rows = pl.ds(pl.multiple_of(q_chunk * chunk, chunk), chunk)
            query_part = q_ref[rows, lanes]
            do_part = do_ref[rows, lanes]
            s_ref[...] = dot(key_part, query_part, NT)
            dp_ref[...] = dot(value_part, do_part, NT)
            lse = lse_ref[head : head + 1, rows]
            outdot = outdot_ref[head : head + 1, rows]

            def step(index, carry):
                at = pl.ds(pl.multiple_of(index * PIECE, PIECE), PIECE)
                tile = s_ref[at, :] + block_bias(bias_ref, here, head, index, q_chunk * blocks, blocks)
                ok = (here[KEY_BLOCKS + index] * PIECE + key_iota).astype(F32) < length
                prob = jnp.exp(jnp.where(ok, tile, NEG_FILL) - lse)
                p_ref[at, :] = prob.astype(BF16)
                grad = prob * (dp_ref[at, :] - outdot)
                ds_ref[at, :] = grad.astype(BF16)
                for i in range(blocks):
                    apart = here[KEY_BLOCKS + index] - here[QUERY_BLOCKS + q_chunk * blocks + i]
                    which = jnp.clip(apart, -2, 2) + 2
                    tile_ref[head, which] += grad[:, i * PIECE : (i + 1) * PIECE]
                return carry

            repeat(key_blocks, unroll, step, 0)
            dkv_ref[:, lanes] += dot(ds_ref[...], query_part)
            dkv_ref[:, v_lanes] += dot(p_ref[...], do_part)
            dqt_ref[lanes, rows] = dot(key_part, ds_ref[...], TN)
            return carry

        repeat(GROUP // chunk, unroll, for_queries, 0)


def bucket_sums(tile_ref, head):
    apart = lax.broadcasted_iota(jnp.int32, (PIECE, PIECE), 0) - lax.broadcasted_iota(
        jnp.int32, (PIECE, PIECE), 1
    )
    bucket = lax.broadcasted_iota(jnp.int32, (BUCKETS, 128), 0)
    table = jnp.zeros((BUCKETS, 128), F32)
    for which in range(5):
        tile = tile_ref[head, which]
        low, high = ((15, 16), (1, 16), (0, 32), (17, 32), (31, 32))[which]
        ids = bucket_index(apart + (which - 2) * PIECE)
        for b in range(low, high):
            chosen = tile if high == low + 1 else jnp.where(ids == b, tile, 0.0)
            table = table + jnp.where(bucket == b, jnp.sum(chosen, axis=0, keepdims=True), 0.0)
    return table


def back_scratch(keys, chunk):
    return (
        pltpu.VMEM((keys, chunk), F32),
        pltpu.VMEM((keys, chunk), F32),
        pltpu.VMEM((keys, chunk), BF16),
        pltpu.VMEM((keys, chunk), BF16),
        pltpu.VMEM((GROUP, COLS), BF16),
        pltpu.VMEM((8, GROUP), F32),
        pltpu.VMEM((COLS, GROUP), F32),
        pltpu.VMEM((keys, 2 * COLS), F32),
    )


def join_kernel(here, *refs):
    for i, piece in enumerate(refs[:4]):
        refs[4][i * ROWS : (i + 1) * ROWS] = piece[...]


def attention_back_kernel(chunk, offsets, here, q_ref, kv_ref, info_ref, bias_ref, out_w_ref, attn_ref, lse_ref, *refs):
    pieces, (dq_ref, dkv_low_ref, tile_ref), scratch = refs[:4], refs[4:7], refs[7:]
    attend_back(
        chunk, offsets, here, q_ref, kv_ref, info_ref, bias_ref, out_w_ref, pieces, attn_ref, lse_ref, tile_ref,
        *scratch,
    )
    dq_ref[...] = scratch[6][...].T.astype(BF16)
    dkv_low_ref[...] = scratch[7][...].astype(BF16)


def back_kernel(here, qkv_ref, info_ref, bias_ref, out_w_ref, attn_ref, lse_ref, w_ref, *refs):
    pieces, (d_qkv_ref, tile_ref, partial_ref), scratch = refs[:4], refs[4:7], refs[7:]
    attend_back(
        256, (COLS, 2 * COLS), here, qkv_ref, qkv_ref, info_ref, bias_ref, out_w_ref, pieces, attn_ref, lse_ref,
        tile_ref, *scratch,
    )
    d_qkv_ref[:, :COLS] = scratch[6][...].T.astype(BF16)
    d_qkv_ref[:, COLS:] = scratch[7][...].astype(BF16)
    partial_ref[...] = dot(d_qkv_ref[...], w_ref[...], NT)


def partial_kernel(here, d_ref, w_ref, partial_ref):
    partial_ref[...] = dot(d_ref[...], w_ref[...], NT)


def hidden_kernel(here, small_ref, near_ref, far_ref, keep_ref, core_ref, y_ref, hidden_ref, low_ref):
    rows = jnp.concatenate([near_ref[...], far_ref[...]], axis=0).astype(F32)
    hidden = rows + (keep_ref[:ROWS] + core_ref[:ROWS].astype(F32) + y_ref[...].astype(F32))
    hidden_ref[...] = hidden
    low_ref[...] = (hidden * inverse_rms(hidden) * gain_row(small_ref, 1)).astype(BF16)


def tail_kernel(here, keep_ref, core_ref, out_ref):
    first = 0 if keep_ref.shape[0] == ROWS else ROWS
    kept = keep_ref[first : first + ROWS]
    out_ref[...] = (kept + core_ref[core_ref.shape[0] - ROWS :].astype(F32)).astype(BF16)


def pair_kernel(here, near_ref, far_ref, layer_ref, grad_ref):
    for place, ref in ((here[X], near_ref), (1 - here[X], far_ref)):
        layer_ref[place] = ref[0]
        grad_ref[place] = ref[1].astype(F32)


def sums_kernel(here, partial_ref, normed_ref, small_ref, ffn_gain_ref, squares_ref, tile_ref, out_ref):
    out_ref[...] = jnp.zeros(out_ref.shape, F32)
    products = jnp.sum(partial_ref[...] * normed_ref[...].astype(F32), axis=0, keepdims=True)
    out_ref[0:1] = products / gain_row(small_ref, 0)
    out_ref[1:2] = ffn_gain_ref[...]
    out_ref[2:3] = squares_ref[...]
    lane = lax.broadcasted_iota(jnp.int32, (BUCKETS, 128), 1)
    table = jnp.zeros((BUCKETS, 128), F32)
    for head in range(HEADS):
        values = jnp.sum(bucket_sums(tile_ref, head), axis=1, keepdims=True)
        table = table + jnp.where(lane == here[ME] * HEADS + head, values, 0.0)
    for i in range(TP):
        out_ref[8:16, i * 128 : (i + 1) * 128] = table[i * 8 : (i + 1) * 8]


def small_out(here, info_ref, total, attn_gain_ref, ffn_gain_ref, rows_ref, loss_ref):
    for k in range(TP):

        @pl.when(here[ME] == k)
        def _():
            attn_gain_ref[...] = total[0:1, k * OWN : (k + 1) * OWN]
            ffn_gain_ref[...] = total[1:2, k * OWN : (k + 1) * OWN]
            rows_ref[...] = total[8:16, k * 128 : k * 128 + H]

    loss_ref[...] = jnp.sum(total[2:3], axis=1, keepdims=True) / (info_ref[1:2, 0:1] * D)


def small_out_kernel(here, info_ref, total_ref, *outs):
    small_out(here, info_ref, total_ref[...], *outs)


def rows_kernel(here, a_ref, b_ref, c_ref, d_ref, out_ref):
    stack_rows(here, (a_ref, b_ref, c_ref, d_ref), out_ref)


def ffn_body(values, in_ref, outer_ref, active_ref, slope_ref, keep_ref, send_ref):
    for i, ref in enumerate(values):
        rows = slice(i * ROWS, (i + 1) * ROWS)
        active, slope = gelu_and_slope(dot(ref[...], in_ref[...]))
        active_ref[rows] = active.astype(BF16)
        slope_ref[rows] = slope.astype(BF16)
    partial = dot(active_ref[...], outer_ref[...])
    keep_ref[...] = partial[:ROWS]
    send_ref[...] = partial[ROWS:].astype(BF16)


def ffn_kernel(here, own_ref, core_ref, in_ref, outer_ref, *outs):
    ffn_body((own_ref, core_ref), in_ref, outer_ref, *outs)


def loss_kernel(
    tokens, here, hidden_ref, keep_ref, core_ref, y_ref, near_ref, far_ref, info_ref,
    out_near_ref, out_far_ref, grad_ref, low_ref, square_ref,
):
    length = info_ref[0:1, 0:1]
    factor = tokens / info_ref[1:2, 0:1]
    result = hidden_ref[...] + (keep_ref[...] + core_ref[...].astype(F32) + y_ref[...].astype(F32))
    spot = lax.broadcasted_iota(jnp.int32, (PIECE, 1), 0)
    total = jnp.zeros((1, D), F32)
    for i, (teacher, out) in enumerate(((near_ref, out_near_ref), (far_ref, out_far_ref))):
        rows = slice(i * PIECE, (i + 1) * PIECE)
        part = result[rows]
        out[...] = part.astype(BF16)
        valid = ((here[QUERY_BLOCKS + i] * PIECE + spot).astype(F32) < length).astype(F32)
        deviation = (part - teacher[...].astype(F32)) * valid
        total = total + jnp.sum(deviation * deviation, axis=0, keepdims=True)
        grad = deviation * factor
        grad_ref[rows] = grad
        low_ref[rows] = grad.astype(BF16)
    square_ref[...] = total


def ffn_back_kernel(here, own_ref, core_ref, slope_ref, in_ref, outer_ref, inner_ref, keep_ref, send_ref):
    for i, ref in enumerate((own_ref, core_ref)):
        rows = slice(i * ROWS, (i + 1) * ROWS)
        grad = dot(ref[...], outer_ref[...], NT)
        inner_ref[rows] = (slope_ref[rows].astype(F32) * grad).astype(BF16)
    partial = dot(inner_ref[...], in_ref[...], NT)
    keep_ref[...] = partial[:ROWS]
    send_ref[...] = partial[ROWS:].astype(BF16)


def inner_sum(refs):
    inputs, inner = refs[:4], refs[4:6]
    at = [slice(0, ROWS), slice(ROWS, 2 * ROWS)] * 2
    return sum(dot(inputs[i][...], inner[i // 2][at[i]], TN) for i in range(4))


def outer_half(active_ref, own_ref, core_ref):
    return dot(active_ref[:ROWS], own_ref[...], TN) + dot(active_ref[ROWS:], core_ref[...], TN)


def outer_own_kernel(here, active_ref, own_ref, core_ref, out_ref):
    out_ref[...] = outer_half(active_ref, own_ref, core_ref)


def outer_kernel(here, part_ref, active_ref, own_ref, core_ref, out_ref):
    out_ref[...] = (part_ref[...] + outer_half(active_ref, own_ref, core_ref)).astype(BF16)


def outer_halves_kernel(here, part_ref, active_ref, own_ref, core_ref, send, mine, total_ref):
    total_ref[...] = part_ref[...] + outer_half(active_ref, own_ref, core_ref)
    quarter = D // 8
    for x, out in ((1 - here[X], send), (here[X], mine)):
        for z in range(4):
            start = pl.multiple_of((4 * x + z) * quarter, quarter)
            out[z] = total_ref[pl.ds(start, quarter)].astype(BF16)


def inner_kernel(here, *refs):
    refs[6][...] = inner_sum(refs).astype(BF16)


def inner_halves_kernel(here, *refs):
    send, mine, total_ref = refs[6:]
    total_ref[...] = inner_sum(refs)
    for x, out in ((1 - here[X], send), (here[X], mine)):
        for z in range(4):
            for w in range(TP):
                start = pl.multiple_of(w * OWN + (4 * x + z) * DEPTH, 8)
                out[z * TP + w] = total_ref[pl.ds(start, DEPTH)].astype(BF16)


def hidden_back_kernel(
    here, small_ref, hidden_ref, result_grad_ref, keep_ref, core_ref, y_ref, grad_ref, low_ref, gain_grad_ref
):
    upper = keep_ref[...] + core_ref[...].astype(F32) + y_ref[...].astype(F32)
    back, gain_grad_ref[...] = norm_back(hidden_ref[...], gain_row(small_ref, 1), upper)
    grad = result_grad_ref[...] + back
    grad_ref[...] = grad
    low_ref[...] = grad.astype(BF16)


def qkv_grads(normed_ref, d_qkv_ref, put):
    d_qkv = dot(normed_ref[...], d_qkv_ref[...], TN)
    for m in range(3):
        for i in range(TP):
            block = d_qkv[i * OWN : (i + 1) * OWN, m * COLS : (m + 1) * COLS]
            put(m, slice(i * COLS, (i + 1) * COLS), block)


def attention_grads_kernel(here, normed_ref, d_qkv_ref, attn_ref, up_ref, out_ref):
    def put(m, lanes, block):
        out_ref[m, :, lanes] = block.astype(BF16)

    qkv_grads(normed_ref, d_qkv_ref, put)
    out_ref[3] = dot(attn_ref[...].astype(BF16), up_ref[...]).astype(BF16)


SUM_ROWS = 16


def added(ref, other, index):
    return ref[index].astype(F32) + other[index].astype(F32)


def split_low(here, mine, came, send, keep):
    per = mine.shape[0] // 4
    low = here[Z] & 1
    for high in range(2):
        for i in range(per):
            at = high * per + i
            send[at] = added(mine, came, (2 * high + 1 - low) * per + i).astype(BF16)
            keep[at] = added(mine, came, (2 * high + low) * per + i).astype(BF16)


def split_high(here, mine, came, send, keep, *_):
    per = mine.shape[0] // 2
    high = here[Z] >> 1
    for i in range(per):
        send[i] = added(mine, came, (1 - high) * per + i).astype(BF16)
        keep[i] = added(mine, came, high * per + i).astype(BF16)


def finish(here, mine, came, chunk):
    for i in range(mine.shape[0]):
        chunk[i] = added(mine, came, i).astype(BF16)


def join_high(here, mine, came, pair, per=1):
    high = here[Z] >> 1
    for i in range(per):
        pair[high * per + i] = mine[i]
        pair[(1 - high) * per + i] = came[i]


def join_low(here, mine, came, half, per=1):
    low = here[Z] & 1
    for high in range(2):
        for i in range(per):
            half[(2 * high + low) * per + i] = mine[high * per + i]
            half[(2 * high + 1 - low) * per + i] = came[high * per + i]


def outer_rows(here, half, came, out):
    rows = half.shape[1]
    for x, ref in ((here[X], half), (1 - here[X], came)):
        for z in range(4):
            out[pl.ds(pl.multiple_of((4 * x + z) * rows, 8), rows)] = ref[z].astype(F32)


def send_sums(total, send):
    last = send.shape[0] - 1
    high = total.astype(BF16)
    low = (total - high.astype(F32)).astype(BF16)
    send[last, :8] = high[:8]
    send[last, 8:16] = low[:8]
    send[last, 16:, : TP * 128] = high[8:, : TP * 128]


def sums_of(came):
    last = came.shape[0] - 1
    top = came[last, :8].astype(F32) + came[last, 8:16].astype(F32)
    return jnp.concatenate([top, came[last, 16:].astype(F32)], axis=0)


def out_grads(here, attn_ref, a_ref, b_ref, c_ref, d_ref, send_ref, mine_ref, send, mine, total_ref):
    total = None
    for i, ref in enumerate((a_ref, b_ref, c_ref, d_ref)):
        part = dot(attn_ref[:, i * ROWS : (i + 1) * ROWS].astype(BF16), ref[...])
        total = part if total is None else total + part
    total_ref[...] = total
    for x, ref, out in ((1 - here[X], send_ref, send), (here[X], mine_ref, mine)):
        for z in range(4):
            for w in range(TP):
                out[z * (TP + 1) + w] = ref[z * TP + w]
            start = pl.multiple_of((4 * x + z) * DEPTH, 8)
            out[z * (TP + 1) + TP] = total_ref[pl.ds(start, DEPTH)].astype(BF16)


def inner_finish(here, mine, came, sums, own, *others):
    own[0] = added(mine, came, here[ME]).astype(BF16)
    own[1] = added(mine, came, TP).astype(BF16)
    for r, other in enumerate(others):
        other[0] = added(mine, came, here[ME] ^ (r + 1)).astype(BF16)
        send_sums(sums[...], other)


def inner_collect(here, own, a_ref, b_ref, c_ref, sums, chunk, total):
    for r, ref in enumerate((own, a_ref, b_ref, c_ref)):
        chunk[here[ME] ^ r] = ref[0]
    chunk[TP] = own[1]
    value = sums[...]
    for ref in (a_ref, b_ref, c_ref):
        value = value + sums_of(ref)
    total[...] = value
    send_sums(value, chunk)


def inner_high(here, chunk, came, sums, pair, total):
    join_high(here, chunk, came, pair, TP + 1)
    total[...] = sums[...] + sums_of(came)
    send_sums(total[...], pair)


def inner_low(here, pair, came, sums, half, total):
    join_low(here, pair, came, half, TP + 1)
    total[...] = sums[...] + sums_of(came)
    send_sums(total[...], half)


def inner_rows(here, info_ref, half, came, sums, inner_out, out_out, *small):
    for x, ref in ((here[X], half), (1 - here[X], came)):
        for z in range(4):
            rows = pl.ds(pl.multiple_of((4 * x + z) * DEPTH, 8), DEPTH)
            for w in range(TP):
                inner_out[rows, w * D : (w + 1) * D] = ref[z * (TP + 1) + w].astype(F32)
            out_out[rows] = ref[z * (TP + 1) + TP].astype(F32)
    small_out(here, info_ref, sums[...] + sums_of(came), *small)


def qkv_halves_kernel(here, normed_ref, d_qkv_ref, send, mine, total_ref):
    def put(m, lanes, block):
        total_ref[m, :, lanes] = block

    qkv_grads(normed_ref, d_qkv_ref, put)
    for x, out in ((1 - here[X], send), (here[X], mine)):
        for z in range(4):
            start = pl.multiple_of((4 * x + z) * DEPTH, 8)
            for m in range(3):
                out[z * 3 + m] = total_ref[m, pl.ds(start, DEPTH), :].astype(BF16)


def qkv_finish(here, mine, came, *outs):
    for k in range(TP):

        @pl.when(here[ME] == k)
        def _():
            for m in range(3):
                values = added(mine, came, m).astype(BF16)
                for r, out in enumerate(outs):
                    out[m] = values[:, (k ^ r) * COLS : (k ^ r) * COLS + COLS]


def qkv_collect(here, own, a_ref, b_ref, c_ref, chunk):
    for k in range(TP):

        @pl.when(here[ME] == k)
        def _():
            for m in range(3):
                for r, ref in enumerate((own, a_ref, b_ref, c_ref)):
                    chunk[m, :, (k ^ r) * COLS : (k ^ r) * COLS + COLS] = ref[m]


def qkv_high(here, chunk, came, pair):
    join_high(here, chunk, came, pair, 3)


def qkv_low(here, pair, came, half):
    join_low(here, pair, came, half, 3)


def qkv_rows(here, half, came, *outs):
    for x, ref in ((here[X], half), (1 - here[X], came)):
        for z in range(4):
            for m, out in enumerate(outs):
                out[pl.ds(pl.multiple_of((4 * x + z) * DEPTH, 8), DEPTH)] = ref[z * 3 + m].astype(F32)


def input_kernel(
    here, small_ref, near_ref, far_ref, hidden_grad_ref, keep_ref, core_ref, layer_near_ref, layer_far_ref, y_ref,
    out_near_ref, out_far_ref,
):
    values = jnp.concatenate([near_ref[...], far_ref[...]], axis=0).astype(F32)
    upper = keep_ref[:ROWS] + core_ref[:ROWS].astype(F32) + y_ref[...].astype(F32)
    back, _ = norm_back(values, gain_row(small_ref, 0), upper)
    grad = (hidden_grad_ref[...] + back).astype(BF16)
    out_near_ref[0] = layer_near_ref[...]
    out_near_ref[1] = grad[:PIECE]
    out_far_ref[0] = layer_far_ref[...]
    out_far_ref[1] = grad[PIECE:]


def on_device(
    inputs, teacher, seq_lengths, gain_attn, w_query, w_key, w_value, w_out, bias_table, gain_ffn, w_inner, w_outer
):
    n_ctx = lax.axis_size("ctx")
    spread = n_ctx // (SEQ_DEV * TP)
    me = lax.axis_index("wsh")
    ctx_me = lax.axis_index("ctx")
    parity = ctx_me & 1
    token_total = ROWS * n_ctx * TP
    same, cross = seq_routes(n_ctx)
    home = ctx_me // spread
    stretch = ctx_me % spread
    seq_bit = home & 1
    by_steps = n_ctx == 8

    def to_home(pair):
        return lax.ppermute(pair[0], AXES, same), lax.ppermute(pair[1], AXES, cross)

    def from_home(near, far):
        near = lax.ppermute(near, AXES, backwards(same))
        far = lax.ppermute(far, AXES, backwards(cross))
        return near, far

    def block_places(stretch_index):
        return [
            TP * 2 * stretch_index + 2 * swapped(me ^ r) + (seq_bit ^ e) for r in ORDER for e in (0, 1)
        ]

    query_blocks = block_places(stretch)
    key_blocks = [p for i in range(spread) for p in block_places(i)] if spread > 1 else query_blocks

    scalars = [me, parity, (ctx_me >> 1) & 3, swapped(home >> 1), seq_bit] + query_blocks + key_blocks
    here = jnp.stack([jnp.asarray(v, jnp.int32) for v in scalars])

    low = functools.partial(shape, dtype=BF16)
    x_here, x_there, *qkv_blocks = call(
        start_kernel,
        (low(PIECE, D),) * 2 + (low(OWN + 16, 3 * COLS),) * 4,
        (here, inputs, w_query, w_key, w_value, gain_attn, gain_ffn, bias_table, seq_lengths),
        scratch=(pltpu.VMEM((16, 3 * COLS), F32),) + (pltpu.VMEM((OWN, D), BF16),) * 3
        + (pltpu.VMEM((OWN,), BF16),) * 2 + (pltpu.VMEM((8, H), BF16), pltpu.VMEM((SEQ_DEV,), jnp.int32))
        + (pltpu.SemaphoreType.DMA((9,)),),
        mib=START_MIB,
        in_hbm=8,
    )
    x_near, x_far = to_home((x_here, x_there))

    def group_blocks(values):
        return (values[0],) + tuple(to_partner(values[r], r) for r in (1, 2, 3))

    w_qkv_pieces = group_blocks(qkv_blocks)
    (small, info, bias), (w_qkv,) = run(
        here,
        (
            functools.partial(bias_kernel, float(n_ctx * PIECE)),
            (shape(TP, 16, 3 * COLS), shape(8, 128), shape(HEADS, 5, PIECE, PIECE)),
            w_qkv_pieces,
        ),
        (rows_kernel, (low(D, 3 * COLS),), w_qkv_pieces),
    )
    x_own = (x_near, x_far)
    *teacher_halves, in_own, in_core, in_across = call(
        inner_blocks_kernel,
        (low(PIECE, D),) * 2 + (low(OWN, D),) * 2 + (low(2, OWN // 2, D),),
        (here, after(w_inner, w_qkv), teacher),
    )
    x_y = tuple(to_partner(v, 2) for v in x_own)
    x_y = tuple(after(v, w_qkv) for v in x_y)
    pieces = x_own + x_y + tuple(to_partner(v, 1) for v in x_own + x_y)
    attn_shapes = (shape(COLS, GROUP), shape(8, GROUP), shape(GROUP, D))
    send_job = (send_kernel, (low(2 * ROWS, D),))
    proj_shapes = (low(GROUP, D), low(GROUP, 3 * COLS))

    def attn_scratch(keys, chunk):
        return (pltpu.VMEM((keys, chunk), F32), pltpu.VMEM((keys, chunk), BF16))

    if spread == 1:
        normed, qkv, attn_t, lse, partial = call(
            front_kernel,
            proj_shapes + attn_shapes,
            (here, small) + pieces + (w_qkv, info, bias, w_out),
            scratch=attn_scratch(GROUP, 512),
            mib=14,
        )
    else:
        teams = [[s * spread + i for i in range(spread)] for s in range(SEQ_DEV * TP)]
        normed, qkv = call(project_kernel, proj_shapes, (here, small) + pieces + (w_qkv,))
        kv = lax.all_gather(qkv[:, COLS:], "ctx", axis=0, tiled=True, axis_index_groups=teams)
        q = qkv[:, :COLS]
        attn_t, lse, partial = call(
            functools.partial(attention_kernel, 128, (0, COLS)),
            attn_shapes,
            (here, q, kv, info, bias, w_out),
            scratch=attn_scratch(kv.shape[0], 128),
            mib=56,
        )

    def scatter_tail(keep_y, from_core):
        return call(tail_kernel, (low(ROWS, D),), (here, keep_y, from_core))[0]

    from_y = to_partner(after(in_across, *x_y), 2)
    teacher_near, teacher_far = to_home([after(v, *x_y) for v in teacher_halves])
    partial, from_y, teacher_near, teacher_far = lax.optimization_barrier((partial, from_y, teacher_near, teacher_far))
    ((send,),) = run(here, send_job + ((partial,),))
    core = to_partner(send, 1)
    from_x = to_ctx(after(from_y, send), 1)
    in_core = to_partner(after(in_core, send), 1)
    going = scatter_tail(partial, core)
    across = to_partner(going, 2)
    hidden, ffn_low = call(
        hidden_kernel,
        (shape(ROWS, D), low(ROWS, D)),
        (here, small, x_near, x_far, partial, core, across),
    )
    core_y, core_x = to_partner(after(from_y, send), 1), to_partner(after(from_x, ffn_low), 1)
    (w_in,) = call(
        inner_rows_kernel, (low(D, D),), (here, after(in_own, ffn_low), in_core, from_y, from_x, core_y, core_x)
    )

    def gathered(value):
        from_y = to_partner(value, 2)
        return to_partner(value, 1), from_y

    def both_halves(first_call, second_call, value):
        from_core, from_y = gathered(value)
        first, done = first_call((value, from_core))
        core_y = to_partner(after(from_y, done), 1)
        second = second_call((from_y, core_y))
        core_own = to_partner(first[-1], 1)
        going = scatter_tail(second[-2], to_partner(second[-1], 1))
        across = to_partner(going, 2)
        return (value, from_core, from_y, core_y), first, second, (first[-2], core_own, across), going

    half = low(2 * ROWS, D)
    piece_shapes = (shape(ROWS, D), low(ROWS, D))
    def ffn(values):
        return call(ffn_kernel, (half, half) + piece_shapes, (here,) + values + (w_in, w_outer))

    def ffn_first(values):
        outs = ffn(values)
        return outs, outs[-1]

    ffn_all, (active_a, slope_a, *_), (active_b, slope_b, *_), parts, _ = both_halves(ffn_first, ffn, ffn_low)
    out_near, out_far, result_grad, result_low, squares = call(
        functools.partial(loss_kernel, float(token_total)),
        (low(PIECE, D), low(PIECE, D), shape(ROWS, D), low(ROWS, D), shape(1, D)),
        (here, hidden) + parts + (teacher_near, teacher_far, info),
    )

    depth = OWN // n_ctx

    def parts_of(count, rows=DEPTH):
        return low(count, rows, D)

    def ffn_back(values, slope):
        return call(ffn_back_kernel, (half,) + piece_shapes, (here,) + values + (slope, w_in, w_outer))

    def ffn_back_first(values):
        outs = ffn_back(values, slope_a)
        (part,) = call(
            outer_own_kernel, (shape(D, D),), (here, after(active_a, outs[-1])) + values, mib=12
        )
        grads.append(part)
        return outs, part

    def ffn_back_second(values):
        args = (here, grads[0], active_b) + values
        if by_steps:
            outs = (parts_of(4, D // 8),) * 2
            grads[:] = call(outer_halves_kernel, outs, args, scratch=(pltpu.VMEM((D, D), F32),), mib=14)
        else:
            grads[:] = call(outer_kernel, (low(D, D),), args, mib=12)
        return ffn_back((after(values[0], grads[0]), values[1]), slope_b)

    grads = []
    result_all, (inner_a, *_), (inner_b, *_), parts, going = both_halves(
        ffn_back_first, ffn_back_second, result_low
    )
    inner_args = (here,) + ffn_all + (inner_a, after(inner_b, going))
    ahead = []
    if by_steps:
        outer_send, outer_mine = grads
        outer_came = to_ctx(outer_send, 1)
        inner_send, inner_mine = call(
            inner_halves_kernel, (parts_of(4 * TP),) * 2, inner_args, scratch=(pltpu.VMEM((D, D), F32),), mib=14
        )
        ordered = inner_send
        ahead.append((split_low, (parts_of(2, D // 8),) * 2, (outer_mine, outer_came)))
    else:
        (outer_wgrad,) = grads
        (inner_wgrad,) = call(inner_kernel, (low(D, D),), inner_args, mib=14)
        ordered = inner_wgrad
    ((hidden_grad, hidden_low, ffn_gain_grad),) = run(
        here,
        (
            hidden_back_kernel,
            (shape(ROWS, D), low(ROWS, D), shape(1, D)),
            (small, after(hidden, ordered), result_grad) + parts,
        ),
    )
    from_core, from_y = gathered(hidden_low)
    if by_steps:
        body, outs, args = ahead[0]
        ((outer_send, outer_keep),) = run(here, (body, outs, (after(args[0], hidden_low),) + args[1:]))
        outer_came = to_ctx(outer_send, 2)
        from_y = after(from_y, outer_came)
    up_pieces = (hidden_low, from_y, from_core, to_partner(from_y, 1))
    table_shape = shape(HEADS, 5, PIECE, PIECE)
    if by_steps:
        (inner_send, inner_mine), (outer_send, outer_keep) = run(
            here,
            (
                out_grads,
                (parts_of(4 * TP + 4),) * 2,
                (attn_t,) + up_pieces + (inner_send, inner_mine),
            ),
            (split_high, (parts_of(1, D // 8),) * 2, (outer_keep, outer_came)),
            scratch=(pltpu.VMEM((OWN, D), F32),),
        )
        inner_came = to_ctx(inner_send, 1)
        outer_came = to_ctx(outer_send, 4)
        up_pieces = (after(hidden_low, outer_keep),) + up_pieces[1:]
    if spread == 1:
        d_qkv, table_part, partial = call(
            back_kernel,
            (proj_shapes[1], table_shape, shape(GROUP, D)),
            (here, qkv, info, bias, w_out, attn_t, lse, w_qkv) + up_pieces,
            scratch=back_scratch(GROUP, 256),
            mib=20,
        )
    else:
        dq, dkv, table_part = call(
            functools.partial(attention_back_kernel, 128, (0, COLS)),
            (low(GROUP, COLS), low(kv.shape[0], 2 * COLS), table_shape),
            (here, q, kv, info, bias, w_out, attn_t, lse) + up_pieces,
            scratch=back_scratch(kv.shape[0], 128),
            mib=60,
        )
        dkv = lax.psum_scatter(dkv, "ctx", scatter_dimension=0, tiled=True, axis_index_groups=teams)
        d_qkv = jnp.concatenate([dq, dkv], axis=1)
        (partial,) = call(partial_kernel, (shape(GROUP, D),), (here, d_qkv, w_qkv))
    if by_steps:
        (send,), (outer_chunk,), (inner_send, inner_keep) = run(
            here,
            send_job + ((partial,),),
            (finish, (parts_of(1, D // 8),), (outer_keep, outer_came)),
            (split_low, (parts_of(2 * TP + 2),) * 2, (inner_mine, inner_came)),
        )
        outer_came = to_ctx(outer_chunk, 4)
        inner_came = to_ctx(inner_send, 2)
    else:
        ((send,),) = run(here, send_job + ((partial,),))
    core = to_partner(send, 1)
    input_job = (
        input_kernel,
        (low(2, PIECE, D), low(2, PIECE, D)),
        (small, x_near, x_far, hidden_grad, partial, core, out_near, out_far),
    )
    small_shapes = (shape(1, OWN), shape(1, OWN), shape(8, H), shape(1, 1))
    sums_shape = shape(SUM_ROWS, D)
    pair_out = (low(SEQ_DEV, PIECE, D), shape(SEQ_DEV, PIECE, D))
    sum_args = (partial, normed, small, ffn_gain_grad, squares, table_part)

    if by_steps:
        going = scatter_tail(partial, core)
        across = to_partner(going, 2)
        qkv_send, qkv_mine = call(
            qkv_halves_kernel,
            (parts_of(12),) * 2,
            (here, normed, after(d_qkv, going)),
            scratch=(pltpu.VMEM((3, OWN, D), F32),),
        )
        qkv_came = to_ctx(qkv_send, 1)
        inner_keep, across = lax.optimization_barrier((after(inner_keep, qkv_send), across))
        (inner_send, inner_keep), (outer_pair,) = run(
            here,
            (split_high, (parts_of(TP + 1),) * 2, (inner_keep, inner_came)),
            (join_high, (parts_of(2, D // 8),), (outer_chunk, outer_came)),
        )
        inner_came = to_ctx(inner_send, 4)
        outer_came = to_ctx(outer_pair, 2)
        ((in_near, in_far),) = run(
            here, (input_job[0], input_job[1], input_job[2] + (after(across, inner_keep),))
        )
        home_near, home_far = from_home(in_near, in_far)
        ((qkv_send, qkv_keep),) = run(
            here, (split_low, (parts_of(6),) * 2, (after(qkv_mine, in_near), qkv_came))
        )
        qkv_came = to_ctx(qkv_send, 2)
        (sums,) = call(sums_kernel, (sums_shape,), (here, after(partial, qkv_send)) + sum_args[1:])
        inner_blocks, (outer_half,) = run(
            here,
            (
                inner_finish,
                (parts_of(2),) + (parts_of(1 + 1),) * 3,
                (after(inner_keep, qkv_keep), inner_came, sums),
            ),
            (join_low, (parts_of(4, D // 8),), (outer_pair, outer_came)),
        )
        inner_blocks = group_blocks(inner_blocks)
        outer_came = to_ctx(outer_half, 1)
        ((qkv_send, qkv_keep),) = run(
            here, (split_high, (parts_of(3),) * 2, (after(qkv_keep, outer_half), qkv_came))
        )
        qkv_came = to_ctx(qkv_send, 4)
        ((inner_chunk, sums),) = run(
            here,
            (
                inner_collect,
                (parts_of(TP + 1 + 1), sums_shape),
                (after(inner_blocks[0], qkv_keep, home_far),) + inner_blocks[1:] + (sums,),
            ),
        )
        inner_came = to_ctx(inner_chunk, 4)
        (qkv_blocks,) = run(
            here, (qkv_finish, (low(3, DEPTH, COLS),) * 4, (after(qkv_keep, inner_chunk), qkv_came))
        )
        qkv_blocks = group_blocks(qkv_blocks)
        (inner_pair, sums), (w_outer_grad,) = run(
            here,
            (
                inner_high,
                (parts_of(2 * TP + 2 + 1), sums_shape),
                (after(inner_chunk, qkv_blocks[0]), inner_came, sums),
            ),
            (outer_rows, (shape(D, D),), (outer_half, outer_came)),
        )
        inner_came = to_ctx(inner_pair, 2)
        ((qkv_chunk,),) = run(
            here, (qkv_collect, (parts_of(3),), (after(qkv_blocks[0], inner_pair),) + qkv_blocks[1:])
        )
        qkv_came = to_ctx(qkv_chunk, 4)
        ((inner_half, sums),) = run(
            here,
            (
                inner_low,
                (parts_of(4 * TP + 4 + 1), sums_shape),
                (after(inner_pair, qkv_chunk), inner_came, sums),
            ),
        )
        inner_came = to_ctx(inner_half, 1)
        ((qkv_pair,),) = run(here, (qkv_high, (parts_of(6),), (after(qkv_chunk, inner_half), qkv_came)))
        qkv_came = to_ctx(qkv_pair, 2)
        ((qkv_half,),) = run(here, (qkv_low, (parts_of(12),), (qkv_pair, qkv_came)))
        qkv_came = to_ctx(qkv_half, 1)
        ((w_inner_grad, w_out_grad, my_attn_gain, my_ffn_gain, my_rows, loss_value),) = run(
            here,
            (
                inner_rows,
                (shape(OWN, TP * D), shape(OWN, D)) + small_shapes,
                (info, after(inner_half, qkv_half), inner_came, sums),
            ),
        )
        (layer_out, input_grad), (w_query_grad, w_key_grad, w_value_grad) = run(
            here,
            (pair_kernel, pair_out, (home_near, home_far)),
            (qkv_rows, (shape(OWN, D),) * 3, (after(qkv_half, w_out_grad), qkv_came)),
        )
    else:
        across = to_partner(scatter_tail(partial, core), 2)
        ((in_near, in_far),) = run(here, (input_job[0], input_job[1], input_job[2] + (across,)))
        ((layer_out, input_grad),) = run(here, (pair_kernel, pair_out, from_home(in_near, in_far)))
        (sums,) = call(sums_kernel, (sums_shape,), (here,) + sum_args)
        (hidden_all,) = call(join_kernel, (low(GROUP, D),), (here,) + up_pieces)
        my_attn_gain, my_ffn_gain, my_rows, loss_value = call(
            small_out_kernel, small_shapes, (here, info, lax.psum(sums, AXES))
        )

        def summed(parts):
            return lax.psum_scatter(parts, "ctx", scatter_dimension=0)

        def inner_to_rows(chunk):
            return swap_blocks(chunk, "wsh").transpose(1, 0, 2).reshape(depth, TP * D)

        def attn_to_rows(chunk):
            blocks = chunk[:3].reshape(3, depth, TP, COLS).transpose(2, 0, 1, 3)
            mine = swap_blocks(blocks, "wsh").transpose(1, 2, 0, 3).reshape(3, depth, D)
            return jnp.concatenate([mine, chunk[3:]])

        (attn_wgrad,) = call(
            attention_grads_kernel, (low(4, OWN, D),), (here, normed, d_qkv, attn_t, hidden_all)
        )
        outer_full = lax.all_gather(summed(outer_wgrad.reshape(n_ctx, D // n_ctx, D)), "ctx")
        inner_parts = inner_wgrad.reshape(TP, n_ctx, depth, D).transpose(1, 0, 2, 3)
        inner_full = lax.all_gather(inner_to_rows(summed(inner_parts)), "ctx")
        attn_parts = attn_wgrad.reshape(4, n_ctx, depth, D).transpose(1, 0, 2, 3)
        attn_full = lax.all_gather(attn_to_rows(summed(attn_parts)), "ctx")
        w_outer_grad = outer_full.reshape(D, D).astype(F32)
        w_inner_grad = inner_full.reshape(OWN, TP * D).astype(F32)
        w_query_grad, w_key_grad, w_value_grad, w_out_grad = (
            attn_full[:, m].reshape(OWN, D).astype(F32) for m in range(4)
        )

    return (
        layer_out,
        loss_value.reshape(()),
        input_grad,
        my_attn_gain.reshape(-1),
        w_query_grad,
        w_key_grad,
        w_value_grad,
        w_out_grad,
        my_rows,
        my_ffn_gain.reshape(-1),
        w_inner_grad,
        w_outer_grad,
    )


def solution(mesh):
    rows = P("wsh", None)
    tokens = P("wsh", "ctx", None)
    return jax.shard_map(
        on_device,
        mesh=mesh,
        in_specs=(tokens, tokens, P("wsh"), P("wsh"), rows, rows, rows, rows, rows, P("wsh"), rows, rows),
        out_specs=(tokens, P(), tokens, P("wsh"), rows, rows, rows, rows, rows, P("wsh"), rows, rows),
        check_vma=False,
    )
```

```python
import functools

import jax
import jax.numpy as jnp
from jax import lax
from jax.experimental import pallas as pl
from jax.experimental.pallas import tpu as pltpu
from jax.sharding import PartitionSpec as P

D = 768
H = 12
DH = 64
BUCKETS = 32
SEQ_DEV = 2
PIECE = 128
TP = 4
HEADS = H // TP
COLS = HEADS * DH
OWN = D // TP
ROWS = SEQ_DEV * PIECE
GROUP = ROWS * TP
DEPTH = OWN // 8
START_MIB = 60
EPS = 1e-06
NEG_FILL = -1e30
BUCKET_EDGES = (12, 16, 23, 32, 46, 64, 91)
AXES = ("ctx", "wsh")
ORDER = (0, 2, 1, 3)

ME, X, Z, SEQ_OWNER, SEQ_BIT, QUERY_BLOCKS = range(6)
KEY_BLOCKS = QUERY_BLOCKS + 8

BF16 = jnp.bfloat16
F32 = jnp.float32
NT = (((1,), (1,)), ((), ()))
TN = (((0,), (0,)), ((), ()))
NN = (((1,), (0,)), ((), ()))


def dot(left, right, dims=NN):
    return lax.dot_general(left, right, dims, preferred_element_type=F32)


def swapped(index):
    return (index & 1) * 2 + (index >> 1)


def seq_routes(n_ctx):
    spread = n_ctx // (SEQ_DEV * TP)
    same, cross = [], []
    for c in range(n_ctx):
        for w in range(TP):
            pair = c // 2
            for b in range(2):
                home = (2 * swapped(w) + b) * spread + pair // TP
                route = (c * TP + w, home * TP + swapped(pair % TP))
                (same if b == c % 2 else cross).append(route)
    return same, cross


def backwards(routes):
    return [(there, here) for here, there in routes]


def to_partner(value, offset):
    return lax.ppermute(value, "wsh", [(i, i ^ offset) for i in range(TP)])


def to_ctx(value, offset):
    n_ctx = lax.axis_size("ctx")
    return lax.ppermute(value, "ctx", [(i, i ^ offset) for i in range(n_ctx)])


def swap_blocks(blocks, axis, groups=None):
    return lax.all_to_all(blocks, axis, 0, 0, tiled=True, axis_index_groups=groups)


def pick(stack, index):
    return lax.dynamic_index_in_dim(stack, index, 0, keepdims=False)


def after(value, *earlier):
    return lax.optimization_barrier((value,) + earlier)[0]


def bucket_index(offset):
    distance = jnp.abs(offset)
    far_bucket = 8 + sum(((distance >= edge).astype(jnp.int32) for edge in BUCKET_EDGES))
    near_or_far = jnp.where(distance < 8, distance, far_bucket)
    return near_or_far + jnp.where(offset > 0, 16, 0)


def gelu_and_slope(values):
    cumulative = 0.5 * (1.0 + lax.erf(values * 0.7071067811865476))
    density = jnp.exp(-0.5 * values * values) * 0.3989422804014327
    return values * cumulative, cumulative + values * density


def inverse_rms(values):
    return lax.rsqrt(jnp.mean(values * values, axis=-1, keepdims=True) + EPS)


def norm_back(values, gain, grad):
    scale = inverse_rms(values)
    unit = values * scale
    scaled = gain * grad
    back = scale * (scaled - unit * jnp.mean(scaled * unit, axis=-1, keepdims=True))
    return back, jnp.sum(grad * unit, axis=0, keepdims=True)


def repeat(count, unroll, body, carry):
    if unroll:
        for index in range(count):
            carry = body(index, carry)
        return carry
    return lax.fori_loop(0, count, body, carry)


def vmem():
    return pl.BlockSpec(memory_space=pltpu.VMEM)


def smem():
    return pl.BlockSpec(memory_space=pltpu.SMEM)


def shape(*dims, dtype=F32):
    return jax.ShapeDtypeStruct(dims, dtype)


def hbm():
    return pl.BlockSpec(memory_space=pl.ANY)


def name_of(body):
    return (body.func if isinstance(body, functools.partial) else body).__name__


def run(here, *jobs, scratch=(), mib=10, weight=1):
    args = [a for _, _, given in jobs for a in given]
    outs = [o for _, made, _ in jobs for o in made]

    def bodies(here, *refs):
        ins, rest = refs[: len(args)], refs[len(args) :]
        made, extra = rest[: len(outs)], rest[len(outs) :]
        i = o = 0
        for body, shapes, given in jobs:
            body(here, *ins[i : i + len(given)], *made[o : o + len(shapes)], *extra)
            i, o = i + len(given), o + len(shapes)

    bodies.__name__ = "_".join(name_of(body) for body, _, _ in jobs)
    results = list(call(bodies, outs, [here] + args, scratch, mib, weight=weight))
    return [tuple(results.pop(0) for _ in made) for _, made, _ in jobs]


def call(body, outs, args, scratch=(), mib=10, in_hbm=0, weight=1):
    return pl.pallas_call(
        body,
        name=name_of(body),
        out_shape=tuple(outs),
        in_specs=[smem()] + [hbm()] * in_hbm + [vmem()] * (len(args) - 1 - in_hbm),
        out_specs=(vmem(),) * len(outs),
        scratch_shapes=tuple(scratch),
        compiler_params=pltpu.CompilerParams(vmem_limit_bytes=mib * 2**20),
        cost_estimate=pl.CostEstimate(flops=int(2e9 * weight), bytes_accessed=int(2**23 * weight), transcendentals=0),
    )(*args)


def start_kernel(
    here, x_hbm, wq_hbm, wk_hbm, wv_hbm, gain_a_hbm, gain_f_hbm, table_hbm, lengths_hbm, *refs
):
    halves, outs, small_ref = refs[:2], refs[2:6], refs[6]
    weights, (gain_a_ref, gain_f_ref, table_ref, lengths_ref), sems = refs[7:10], refs[10:14], refs[14]
    moves = [(x_hbm.at[here[X]], halves[0]), (x_hbm.at[1 - here[X]], halves[1])]
    moves += list(zip((wq_hbm, wk_hbm, wv_hbm), weights))
    moves += [(gain_a_hbm, gain_a_ref), (gain_f_hbm, gain_f_ref), (table_hbm, table_ref), (lengths_hbm, lengths_ref)]
    copies = [pltpu.make_async_copy(src, dst, sems.at[i]) for i, (src, dst) in enumerate(moves)]
    for copy in copies:
        copy.start()
    small_ref[...] = jnp.zeros(small_ref.shape, F32)
    for copy in copies:
        copy.wait()
    small_ref[0:1, :OWN] = gain_a_ref[...].astype(F32).reshape(1, OWN)
    small_ref[1:2, :OWN] = gain_f_ref[...].astype(F32).reshape(1, OWN)
    lengths = lengths_ref[...].reshape(1, SEQ_DEV)
    high = lengths >> 7
    small_ref[2:3, :SEQ_DEV] = high.astype(F32)
    small_ref[3:4, :SEQ_DEV] = (lengths - high * 128).astype(F32)
    small_ref[8:16, :H] = table_ref[...].astype(F32)
    for k in range(TP):

        @pl.when(here[ME] == k)
        def _():
            for r in range(TP):
                for m, ref in enumerate(weights):
                    outs[r][:OWN, m * COLS : (m + 1) * COLS] = ref[:, (k ^ r) * COLS : (k ^ r) * COLS + COLS]

    for out in outs:
        out[OWN:] = small_ref[...].astype(BF16)


def inner_blocks_kernel(here, inner_ref, teacher_ref, near_ref, far_ref, own_ref, core_ref, across_ref):
    near_ref[...] = teacher_ref[here[X]]
    far_ref[...] = teacher_ref[1 - here[X]]

    def lanes(r):
        return pl.ds(pl.multiple_of((here[ME] ^ r) * D, D), D)

    own_ref[...] = inner_ref[:, lanes(0)]
    core_ref[...] = inner_ref[:, lanes(1)]
    rows = across_ref.shape[1]
    for i in range(2):
        across_ref[i] = inner_ref[pl.ds(pl.multiple_of(here[X] * rows, rows), rows), lanes(2 + i)]


def inner_rows_kernel(here, own_ref, core_ref, y_ref, x_ref, core_y_ref, core_x_ref, out_ref):
    rows = y_ref.shape[1]
    me, x = here[ME], here[X]
    out_ref[pl.ds(pl.multiple_of(me * OWN, OWN), OWN)] = own_ref[...]
    out_ref[pl.ds(pl.multiple_of((me ^ 1) * OWN, OWN), OWN)] = core_ref[...]
    for r, ref, half in ((2, y_ref, x), (2, x_ref, 1 - x), (3, core_y_ref, x), (3, core_x_ref, 1 - x)):
        start = (me ^ r) * OWN + half * rows
        out_ref[pl.ds(pl.multiple_of(start, rows), rows)] = ref[r - 2]


def gain_row(small_ref, row):
    return jnp.concatenate([small_ref[i, row : row + 1, :OWN] for i in range(TP)], axis=1)


def bias_kernel(longest, here, small_a, small_b, small_c, small_d, small_ref, info_ref, bias_ref):
    for r, ref in enumerate((small_a, small_b, small_c, small_d)):
        small_ref[here[ME] ^ r] = ref[OWN:].astype(F32)
    pair = lax.broadcasted_iota(jnp.int32, (1, SEQ_DEV), 1)
    length = jnp.zeros((1, 1), F32)
    count = jnp.zeros((1, 1), F32)
    for i in range(TP):
        lengths = small_ref[i, 2:3, :SEQ_DEV] * 128.0 + small_ref[i, 3:4, :SEQ_DEV]
        mine = (pair == here[SEQ_BIT]) & (here[SEQ_OWNER] == i)
        length = length + jnp.sum(jnp.where(mine, lengths, 0.0), axis=1, keepdims=True)
        count = count + jnp.sum(jnp.minimum(lengths, longest), axis=1, keepdims=True)
    info_ref[0:1, :] = jnp.broadcast_to(length, (1, 128))
    info_ref[1:2, :] = jnp.broadcast_to(count, (1, 128))
    table = jnp.concatenate([small_ref[i, 8:16, :] for i in range(TP)], axis=0)
    lane = lax.broadcasted_iota(jnp.int32, table.shape, 1)
    apart = lax.broadcasted_iota(jnp.int32, (PIECE, PIECE), 0) - lax.broadcasted_iota(
        jnp.int32, (PIECE, PIECE), 1
    )
    for head in range(HEADS):
        values = jnp.sum(jnp.where(lane == here[ME] * HEADS + head, table, 0.0), axis=1, keepdims=True)
        for tile in range(5):
            low, high = ((15, 16), (1, 16), (0, 32), (17, 32), (31, 32))[tile]
            ids = bucket_index(apart + (tile - 2) * PIECE)
            total = jnp.broadcast_to(values[low : low + 1], (PIECE, PIECE))
            for b in range(low + 1, high):
                total = jnp.where(ids == b, values[b : b + 1], total)
            bias_ref[head, tile] = total


def block_bias(bias_ref, here, head, key_block, query_block, blocks):
    tiles = []
    for i in range(blocks):
        apart = here[KEY_BLOCKS + key_block] - here[QUERY_BLOCKS + query_block + i]
        tiles.append(bias_ref[head, jnp.clip(apart, -2, 2) + 2])
    return tiles[0] if blocks == 1 else jnp.concatenate(tiles, axis=1)


def attend(chunk, offsets, here, q_ref, kv_ref, info_ref, bias_ref, attn_ref, lse_ref, s_ref, p_ref):
    key_blocks = kv_ref.shape[0] // PIECE
    length = info_ref[0:1, 0:1]
    k_off, v_off = offsets
    blocks = chunk // PIECE
    unroll = key_blocks <= 8
    key_iota = lax.broadcasted_iota(jnp.int32, (PIECE, 1), 0)
    for head in range(HEADS):
        lanes = slice(head * DH, head * DH + DH)
        key_part = kv_ref[:, k_off + head * DH : k_off + head * DH + DH]
        value_part = kv_ref[:, v_off + head * DH : v_off + head * DH + DH]

        def for_queries(q_chunk, carry):
            rows = pl.ds(pl.multiple_of(q_chunk * chunk, chunk), chunk)
            s_ref[...] = dot(key_part, q_ref[rows, lanes], NT)

            def score(index, top):
                at = pl.ds(pl.multiple_of(index * PIECE, PIECE), PIECE)
                tile = s_ref[at, :] + block_bias(bias_ref, here, head, index, q_chunk * blocks, blocks)
                ok = (here[KEY_BLOCKS + index] * PIECE + key_iota).astype(F32) < length
                tile = jnp.where(ok, tile, NEG_FILL)
                s_ref[at, :] = tile
                return jnp.maximum(top, jnp.max(tile, axis=0, keepdims=True))

            top = repeat(key_blocks, unroll, score, jnp.full((1, chunk), NEG_FILL, F32))

            def weigh(index, total):
                at = pl.ds(pl.multiple_of(index * PIECE, PIECE), PIECE)
                weight = jnp.exp(s_ref[at, :] - top)
                p_ref[at, :] = weight.astype(BF16)
                return total + jnp.sum(weight, axis=0, keepdims=True)

            total = repeat(key_blocks, unroll, weigh, jnp.zeros((1, chunk), F32))
            attn_ref[lanes, rows] = dot(value_part, p_ref[...], TN) / total
            lse_ref[head : head + 1, rows] = top + jnp.log(total)
            return carry

        repeat(GROUP // chunk, unroll, for_queries, 0)


def send_kernel(here, partial_ref, send_ref, *_):
    send_ref[...] = partial_ref[2 * ROWS :].astype(BF16)


def stack_rows(here, pieces, out_ref):
    for r, piece in enumerate(pieces):
        out_ref[pl.ds(pl.multiple_of((here[ME] ^ r) * OWN, OWN), OWN)] = piece[:OWN]


def project(here, small_ref, pieces, w_ref, normed_ref, qkv_ref):
    gain = gain_row(small_ref, 0)
    for i, piece in enumerate(pieces):
        values = piece[...].astype(F32)
        normed_ref[i * PIECE : (i + 1) * PIECE] = (values * inverse_rms(values) * gain).astype(BF16)
    qkv_ref[...] = dot(normed_ref[...], w_ref[...]).astype(BF16)


def project_kernel(here, small_ref, *refs):
    project(here, small_ref, refs[:8], *refs[8:])


def attention_kernel(chunk, offsets, here, q_ref, kv_ref, info_ref, bias_ref, out_w_ref, *refs):
    attn_ref, lse_ref, partial_ref, s_ref, p_ref = refs
    attend(chunk, offsets, here, q_ref, kv_ref, info_ref, bias_ref, attn_ref, lse_ref, s_ref, p_ref)
    partial_ref[...] = dot(attn_ref[...].astype(BF16), out_w_ref[...], TN)


def front_kernel(here, small_ref, *refs):
    pieces, (w_ref, info_ref, bias_ref, out_w_ref), (normed_ref, qkv_ref) = refs[:8], refs[8:12], refs[12:14]
    project(here, small_ref, pieces, w_ref, normed_ref, qkv_ref)
    attention_kernel(GROUP, (COLS, 2 * COLS), here, qkv_ref, qkv_ref, info_ref, bias_ref, out_w_ref, *refs[14:])


def attend_back(
    chunk, offsets, here, q_ref, kv_ref, info_ref, bias_ref, out_w_ref, pieces, attn_ref, lse_ref,
    tile_ref, s_ref, dp_ref, p_ref, ds_ref, do_ref, outdot_ref, dqt_ref, dkv_ref,
):
    key_blocks = kv_ref.shape[0] // PIECE
    length = info_ref[0:1, 0:1]
    k_off, v_off = offsets
    blocks = chunk // PIECE
    unroll = key_blocks <= 8
    key_iota = lax.broadcasted_iota(jnp.int32, (PIECE, 1), 0)
    for i, piece in enumerate(pieces):
        at = slice(i * ROWS, (i + 1) * ROWS)
        do_ref[at] = dot(piece[...], out_w_ref[...], NT).astype(BF16)
        do_t = dot(out_w_ref[...], piece[...], NT).astype(BF16).astype(F32) * attn_ref[:, at]
        for head in range(HEADS):
            outdot_ref[head : head + 1, at] = jnp.sum(do_t[head * DH : head * DH + DH], axis=0, keepdims=True)
    tile_ref[...] = jnp.zeros_like(tile_ref)
    dkv_ref[...] = jnp.zeros_like(dkv_ref)
    for head in range(HEADS):
        lanes = slice(head * DH, head * DH + DH)
        v_lanes = slice(COLS + head * DH, COLS + head * DH + DH)
        key_part = kv_ref[:, k_off + head * DH : k_off + head * DH + DH]
        value_part = kv_ref[:, v_off + head * DH : v_off + head * DH + DH]

        def for_queries(q_chunk, carry):
            rows = pl.ds(pl.multiple_of(q_chunk * chunk, chunk), chunk)
            query_part = q_ref[rows, lanes]
            do_part = do_ref[rows, lanes]
            s_ref[...] = dot(key_part, query_part, NT)
            dp_ref[...] = dot(value_part, do_part, NT)
            lse = lse_ref[head : head + 1, rows]
            outdot = outdot_ref[head : head + 1, rows]

            def step(index, carry):
                at = pl.ds(pl.multiple_of(index * PIECE, PIECE), PIECE)
                tile = s_ref[at, :] + block_bias(bias_ref, here, head, index, q_chunk * blocks, blocks)
                ok = (here[KEY_BLOCKS + index] * PIECE + key_iota).astype(F32) < length
                prob = jnp.exp(jnp.where(ok, tile, NEG_FILL) - lse)
                p_ref[at, :] = prob.astype(BF16)
                grad = prob * (dp_ref[at, :] - outdot)
                ds_ref[at, :] = grad.astype(BF16)
                for i in range(blocks):
                    apart = here[KEY_BLOCKS + index] - here[QUERY_BLOCKS + q_chunk * blocks + i]
                    which = jnp.clip(apart, -2, 2) + 2
                    tile_ref[head, which] += grad[:, i * PIECE : (i + 1) * PIECE]
                return carry

            repeat(key_blocks, unroll, step, 0)
            dkv_ref[:, lanes] += dot(ds_ref[...], query_part)
            dkv_ref[:, v_lanes] += dot(p_ref[...], do_part)
            dqt_ref[lanes, rows] = dot(key_part, ds_ref[...], TN)
            return carry

        repeat(GROUP // chunk, unroll, for_queries, 0)


def bucket_sums(tile_ref, head):
    apart = lax.broadcasted_iota(jnp.int32, (PIECE, PIECE), 0) - lax.broadcasted_iota(
        jnp.int32, (PIECE, PIECE), 1
    )
    bucket = lax.broadcasted_iota(jnp.int32, (BUCKETS, 128), 0)
    table = jnp.zeros((BUCKETS, 128), F32)
    for which in range(5):
        tile = tile_ref[head, which]
        low, high = ((15, 16), (1, 16), (0, 32), (17, 32), (31, 32))[which]
        ids = bucket_index(apart + (which - 2) * PIECE)
        for b in range(low, high):
            chosen = tile if high == low + 1 else jnp.where(ids == b, tile, 0.0)
            table = table + jnp.where(bucket == b, jnp.sum(chosen, axis=0, keepdims=True), 0.0)
    return table


def back_scratch(keys, chunk):
    return (
        pltpu.VMEM((keys, chunk), F32),
        pltpu.VMEM((keys, chunk), F32),
        pltpu.VMEM((keys, chunk), BF16),
        pltpu.VMEM((keys, chunk), BF16),
        pltpu.VMEM((GROUP, COLS), BF16),
        pltpu.VMEM((8, GROUP), F32),
        pltpu.VMEM((COLS, GROUP), F32),
        pltpu.VMEM((keys, 2 * COLS), F32),
    )


def join_kernel(here, *refs):
    for i, piece in enumerate(refs[:4]):
        refs[4][i * ROWS : (i + 1) * ROWS] = piece[...]


def attention_back_kernel(chunk, offsets, here, q_ref, kv_ref, info_ref, bias_ref, out_w_ref, attn_ref, lse_ref, *refs):
    pieces, (dq_ref, dkv_low_ref, tile_ref), scratch = refs[:4], refs[4:7], refs[7:]
    attend_back(
        chunk, offsets, here, q_ref, kv_ref, info_ref, bias_ref, out_w_ref, pieces, attn_ref, lse_ref, tile_ref,
        *scratch,
    )
    dq_ref[...] = scratch[6][...].T.astype(BF16)
    dkv_low_ref[...] = scratch[7][...].astype(BF16)


def back_kernel(here, qkv_ref, info_ref, bias_ref, out_w_ref, attn_ref, lse_ref, w_ref, *refs):
    pieces, (d_qkv_ref, tile_ref, partial_ref), scratch = refs[:4], refs[4:7], refs[7:]
    attend_back(
        256, (COLS, 2 * COLS), here, qkv_ref, qkv_ref, info_ref, bias_ref, out_w_ref, pieces, attn_ref, lse_ref,
        tile_ref, *scratch,
    )
    d_qkv_ref[:, :COLS] = scratch[6][...].T.astype(BF16)
    d_qkv_ref[:, COLS:] = scratch[7][...].astype(BF16)
    partial_ref[...] = dot(d_qkv_ref[...], w_ref[...], NT)


def partial_kernel(here, d_ref, w_ref, partial_ref):
    partial_ref[...] = dot(d_ref[...], w_ref[...], NT)


def hidden_kernel(here, small_ref, near_ref, far_ref, keep_ref, core_ref, y_ref, hidden_ref, low_ref):
    rows = jnp.concatenate([near_ref[...], far_ref[...]], axis=0).astype(F32)
    hidden = rows + (keep_ref[:ROWS] + core_ref[:ROWS].astype(F32) + y_ref[...].astype(F32))
    hidden_ref[...] = hidden
    low_ref[...] = (hidden * inverse_rms(hidden) * gain_row(small_ref, 1)).astype(BF16)


def tail_kernel(here, keep_ref, core_ref, out_ref):
    first = 0 if keep_ref.shape[0] == ROWS else ROWS
    kept = keep_ref[first : first + ROWS]
    out_ref[...] = (kept + core_ref[core_ref.shape[0] - ROWS :].astype(F32)).astype(BF16)


def pair_kernel(here, near_ref, far_ref, layer_ref, grad_ref):
    for place, ref in ((here[X], near_ref), (1 - here[X], far_ref)):
        layer_ref[place] = ref[0]
        grad_ref[place] = ref[1].astype(F32)


def sums_kernel(here, partial_ref, normed_ref, small_ref, ffn_gain_ref, squares_ref, tile_ref, out_ref):
    out_ref[...] = jnp.zeros(out_ref.shape, F32)
    products = jnp.sum(partial_ref[...] * normed_ref[...].astype(F32), axis=0, keepdims=True)
    out_ref[0:1] = products / gain_row(small_ref, 0)
    out_ref[1:2] = ffn_gain_ref[...]
    out_ref[2:3] = squares_ref[...]
    lane = lax.broadcasted_iota(jnp.int32, (BUCKETS, 128), 1)
    table = jnp.zeros((BUCKETS, 128), F32)
    for head in range(HEADS):
        values = jnp.sum(bucket_sums(tile_ref, head), axis=1, keepdims=True)
        table = table + jnp.where(lane == here[ME] * HEADS + head, values, 0.0)
    for i in range(TP):
        out_ref[8:16, i * 128 : (i + 1) * 128] = table[i * 8 : (i + 1) * 8]


def small_out(here, info_ref, total, attn_gain_ref, ffn_gain_ref, rows_ref, loss_ref):
    for k in range(TP):

        @pl.when(here[ME] == k)
        def _():
            attn_gain_ref[...] = total[0:1, k * OWN : (k + 1) * OWN]
            ffn_gain_ref[...] = total[1:2, k * OWN : (k + 1) * OWN]
            rows_ref[...] = total[8:16, k * 128 : k * 128 + H]

    loss_ref[...] = jnp.sum(total[2:3], axis=1, keepdims=True) / (info_ref[1:2, 0:1] * D)


def small_out_kernel(here, info_ref, total_ref, *outs):
    small_out(here, info_ref, total_ref[...], *outs)


def rows_kernel(here, a_ref, b_ref, c_ref, d_ref, out_ref):
    stack_rows(here, (a_ref, b_ref, c_ref, d_ref), out_ref)


def ffn_body(values, in_ref, outer_ref, active_ref, slope_ref, keep_ref, send_ref):
    for i, ref in enumerate(values):
        rows = slice(i * ROWS, (i + 1) * ROWS)
        active, slope = gelu_and_slope(dot(ref[...], in_ref[...]))
        active_ref[rows] = active.astype(BF16)
        slope_ref[rows] = slope.astype(BF16)
    partial = dot(active_ref[...], outer_ref[...])
    keep_ref[...] = partial[:ROWS]
    send_ref[...] = partial[ROWS:].astype(BF16)


def ffn_kernel(here, own_ref, core_ref, in_ref, outer_ref, *outs):
    ffn_body((own_ref, core_ref), in_ref, outer_ref, *outs)


def loss_kernel(
    tokens, here, hidden_ref, keep_ref, core_ref, y_ref, near_ref, far_ref, info_ref,
    out_near_ref, out_far_ref, grad_ref, low_ref, square_ref,
):
    length = info_ref[0:1, 0:1]
    factor = tokens / info_ref[1:2, 0:1]
    result = hidden_ref[...] + (keep_ref[...] + core_ref[...].astype(F32) + y_ref[...].astype(F32))
    spot = lax.broadcasted_iota(jnp.int32, (PIECE, 1), 0)
    total = jnp.zeros((1, D), F32)
    for i, (teacher, out) in enumerate(((near_ref, out_near_ref), (far_ref, out_far_ref))):
        rows = slice(i * PIECE, (i + 1) * PIECE)
        part = result[rows]
        out[...] = part.astype(BF16)
        valid = ((here[QUERY_BLOCKS + i] * PIECE + spot).astype(F32) < length).astype(F32)
        deviation = (part - teacher[...].astype(F32)) * valid
        total = total + jnp.sum(deviation * deviation, axis=0, keepdims=True)
        grad = deviation * factor
        grad_ref[rows] = grad
        low_ref[rows] = grad.astype(BF16)
    square_ref[...] = total


def ffn_back_kernel(here, own_ref, core_ref, slope_ref, in_ref, outer_ref, inner_ref, keep_ref, send_ref):
    for i, ref in enumerate((own_ref, core_ref)):
        rows = slice(i * ROWS, (i + 1) * ROWS)
        grad = dot(ref[...], outer_ref[...], NT)
        inner_ref[rows] = (slope_ref[rows].astype(F32) * grad).astype(BF16)
    partial = dot(inner_ref[...], in_ref[...], NT)
    keep_ref[...] = partial[:ROWS]
    send_ref[...] = partial[ROWS:].astype(BF16)


def inner_sum(refs):
    inputs, inner = refs[:4], refs[4:6]
    at = [slice(0, ROWS), slice(ROWS, 2 * ROWS)] * 2
    return sum(dot(inputs[i][...], inner[i // 2][at[i]], TN) for i in range(4))


def outer_half(active_ref, own_ref, core_ref):
    return dot(active_ref[:ROWS], own_ref[...], TN) + dot(active_ref[ROWS:], core_ref[...], TN)


def outer_own_kernel(here, active_ref, own_ref, core_ref, out_ref):
    out_ref[...] = outer_half(active_ref, own_ref, core_ref)


def outer_kernel(here, part_ref, active_ref, own_ref, core_ref, out_ref):
    out_ref[...] = (part_ref[...] + outer_half(active_ref, own_ref, core_ref)).astype(BF16)


def outer_halves_kernel(here, part_ref, active_ref, own_ref, core_ref, send, mine, total_ref):
    total_ref[...] = part_ref[...] + outer_half(active_ref, own_ref, core_ref)
    quarter = D // 8
    for x, out in ((1 - here[X], send), (here[X], mine)):
        for z in range(4):
            start = pl.multiple_of((4 * x + z) * quarter, quarter)
            out[z] = total_ref[pl.ds(start, quarter)].astype(BF16)


def inner_kernel(here, *refs):
    refs[6][...] = inner_sum(refs).astype(BF16)


def inner_halves_kernel(here, *refs):
    send, mine, total_ref = refs[6:]
    total_ref[...] = inner_sum(refs)
    for x, out in ((1 - here[X], send), (here[X], mine)):
        for z in range(4):
            for w in range(TP):
                start = pl.multiple_of(w * OWN + (4 * x + z) * DEPTH, 8)
                out[z * TP + w] = total_ref[pl.ds(start, DEPTH)].astype(BF16)


def hidden_back_kernel(
    here, small_ref, hidden_ref, result_grad_ref, keep_ref, core_ref, y_ref, grad_ref, low_ref, gain_grad_ref
):
    upper = keep_ref[...] + core_ref[...].astype(F32) + y_ref[...].astype(F32)
    back, gain_grad_ref[...] = norm_back(hidden_ref[...], gain_row(small_ref, 1), upper)
    grad = result_grad_ref[...] + back
    grad_ref[...] = grad
    low_ref[...] = grad.astype(BF16)


def qkv_grads(normed_ref, d_qkv_ref, put):
    d_qkv = dot(normed_ref[...], d_qkv_ref[...], TN)
    for m in range(3):
        for i in range(TP):
            block = d_qkv[i * OWN : (i + 1) * OWN, m * COLS : (m + 1) * COLS]
            put(m, slice(i * COLS, (i + 1) * COLS), block)


def attention_grads_kernel(here, normed_ref, d_qkv_ref, attn_ref, up_ref, out_ref):
    def put(m, lanes, block):
        out_ref[m, :, lanes] = block.astype(BF16)

    qkv_grads(normed_ref, d_qkv_ref, put)
    out_ref[3] = dot(attn_ref[...].astype(BF16), up_ref[...]).astype(BF16)


SUM_ROWS = 16


def added(ref, other, index):
    return ref[index].astype(F32) + other[index].astype(F32)


def split_low(here, mine, came, send, keep):
    per = mine.shape[0] // 4
    low = here[Z] & 1
    for high in range(2):
        for i in range(per):
            at = high * per + i
            send[at] = added(mine, came, (2 * high + 1 - low) * per + i).astype(BF16)
            keep[at] = added(mine, came, (2 * high + low) * per + i).astype(BF16)


def split_high(here, mine, came, send, keep, *_):
    per = mine.shape[0] // 2
    high = here[Z] >> 1
    for i in range(per):
        send[i] = added(mine, came, (1 - high) * per + i).astype(BF16)
        keep[i] = added(mine, came, high * per + i).astype(BF16)


def finish(here, mine, came, chunk):
    for i in range(mine.shape[0]):
        chunk[i] = added(mine, came, i).astype(BF16)


def join_high(here, mine, came, pair, per=1):
    high = here[Z] >> 1
    for i in range(per):
        pair[high * per + i] = mine[i]
        pair[(1 - high) * per + i] = came[i]


def join_low(here, mine, came, half, per=1):
    low = here[Z] & 1
    for high in range(2):
        for i in range(per):
            half[(2 * high + low) * per + i] = mine[high * per + i]
            half[(2 * high + 1 - low) * per + i] = came[high * per + i]


def outer_rows(here, half, came, out):
    rows = half.shape[1]
    for x, ref in ((here[X], half), (1 - here[X], came)):
        for z in range(4):
            out[pl.ds(pl.multiple_of((4 * x + z) * rows, 8), rows)] = ref[z].astype(F32)


def send_sums(total, send):
    last = send.shape[0] - 1
    high = total.astype(BF16)
    low = (total - high.astype(F32)).astype(BF16)
    send[last, :8] = high[:8]
    send[last, 8:16] = low[:8]
    send[last, 16:, : TP * 128] = high[8:, : TP * 128]


def sums_of(came):
    last = came.shape[0] - 1
    top = came[last, :8].astype(F32) + came[last, 8:16].astype(F32)
    return jnp.concatenate([top, came[last, 16:].astype(F32)], axis=0)


def out_grads(here, attn_ref, a_ref, b_ref, c_ref, d_ref, send_ref, mine_ref, send, mine, total_ref):
    total = None
    for i, ref in enumerate((a_ref, b_ref, c_ref, d_ref)):
        part = dot(attn_ref[:, i * ROWS : (i + 1) * ROWS].astype(BF16), ref[...])
        total = part if total is None else total + part
    total_ref[...] = total
    for x, ref, out in ((1 - here[X], send_ref, send), (here[X], mine_ref, mine)):
        for z in range(4):
            for w in range(TP):
                out[z * (TP + 1) + w] = ref[z * TP + w]
            start = pl.multiple_of((4 * x + z) * DEPTH, 8)
            out[z * (TP + 1) + TP] = total_ref[pl.ds(start, DEPTH)].astype(BF16)


def inner_finish(here, mine, came, sums, own, *others):
    own[0] = added(mine, came, here[ME]).astype(BF16)
    own[1] = added(mine, came, TP).astype(BF16)
    for r, other in enumerate(others):
        other[0] = added(mine, came, here[ME] ^ (r + 1)).astype(BF16)
        send_sums(sums[...], other)


def inner_collect(here, own, a_ref, b_ref, c_ref, sums, chunk, total):
    for r, ref in enumerate((own, a_ref, b_ref, c_ref)):
        chunk[here[ME] ^ r] = ref[0]
    chunk[TP] = own[1]
    value = sums[...]
    for ref in (a_ref, b_ref, c_ref):
        value = value + sums_of(ref)
    total[...] = value
    send_sums(value, chunk)


def inner_high(here, chunk, came, sums, pair, total):
    join_high(here, chunk, came, pair, TP + 1)
    total[...] = sums[...] + sums_of(came)
    send_sums(total[...], pair)


def inner_low(here, pair, came, sums, half, total):
    join_low(here, pair, came, half, TP + 1)
    total[...] = sums[...] + sums_of(came)
    send_sums(total[...], half)


def inner_rows(here, info_ref, half, came, sums, inner_out, out_out, *small):
    for x, ref in ((here[X], half), (1 - here[X], came)):
        for z in range(4):
            rows = pl.ds(pl.multiple_of((4 * x + z) * DEPTH, 8), DEPTH)
            for w in range(TP):
                inner_out[rows, w * D : (w + 1) * D] = ref[z * (TP + 1) + w].astype(F32)
            out_out[rows] = ref[z * (TP + 1) + TP].astype(F32)
    small_out(here, info_ref, sums[...] + sums_of(came), *small)


def qkv_halves_kernel(here, normed_ref, d_qkv_ref, send, mine, total_ref):
    def put(m, lanes, block):
        total_ref[m, :, lanes] = block

    qkv_grads(normed_ref, d_qkv_ref, put)
    for x, out in ((1 - here[X], send), (here[X], mine)):
        for z in range(4):
            start = pl.multiple_of((4 * x + z) * DEPTH, 8)
            for m in range(3):
                out[z * 3 + m] = total_ref[m, pl.ds(start, DEPTH), :].astype(BF16)


def qkv_finish(here, mine, came, *outs):
    for k in range(TP):

        @pl.when(here[ME] == k)
        def _():
            for m in range(3):
                values = added(mine, came, m).astype(BF16)
                for r, out in enumerate(outs):
                    out[m] = values[:, (k ^ r) * COLS : (k ^ r) * COLS + COLS]


def qkv_collect(here, own, a_ref, b_ref, c_ref, chunk):
    for k in range(TP):

        @pl.when(here[ME] == k)
        def _():
            for m in range(3):
                for r, ref in enumerate((own, a_ref, b_ref, c_ref)):
                    chunk[m, :, (k ^ r) * COLS : (k ^ r) * COLS + COLS] = ref[m]


def qkv_high(here, chunk, came, pair):
    join_high(here, chunk, came, pair, 3)


def qkv_low(here, pair, came, half):
    join_low(here, pair, came, half, 3)


def qkv_rows(here, half, came, *outs):
    for x, ref in ((here[X], half), (1 - here[X], came)):
        for z in range(4):
            for m, out in enumerate(outs):
                out[pl.ds(pl.multiple_of((4 * x + z) * DEPTH, 8), DEPTH)] = ref[z * 3 + m].astype(F32)


def input_kernel(
    here, small_ref, near_ref, far_ref, hidden_grad_ref, keep_ref, core_ref, layer_near_ref, layer_far_ref, y_ref,
    out_near_ref, out_far_ref,
):
    values = jnp.concatenate([near_ref[...], far_ref[...]], axis=0).astype(F32)
    upper = keep_ref[:ROWS] + core_ref[:ROWS].astype(F32) + y_ref[...].astype(F32)
    back, _ = norm_back(values, gain_row(small_ref, 0), upper)
    grad = (hidden_grad_ref[...] + back).astype(BF16)
    out_near_ref[0] = layer_near_ref[...]
    out_near_ref[1] = grad[:PIECE]
    out_far_ref[0] = layer_far_ref[...]
    out_far_ref[1] = grad[PIECE:]


def on_device(
    inputs, teacher, seq_lengths, gain_attn, w_query, w_key, w_value, w_out, bias_table, gain_ffn, w_inner, w_outer
):
    n_ctx = lax.axis_size("ctx")
    spread = n_ctx // (SEQ_DEV * TP)
    me = lax.axis_index("wsh")
    ctx_me = lax.axis_index("ctx")
    parity = ctx_me & 1
    token_total = ROWS * n_ctx * TP
    same, cross = seq_routes(n_ctx)
    home = ctx_me // spread
    stretch = ctx_me % spread
    seq_bit = home & 1
    by_steps = n_ctx == 8

    def to_home(pair):
        return lax.ppermute(pair[0], AXES, same), lax.ppermute(pair[1], AXES, cross)

    def from_home(near, far):
        near = lax.ppermute(near, AXES, backwards(same))
        far = lax.ppermute(far, AXES, backwards(cross))
        return near, far

    def block_places(stretch_index):
        return [
            TP * 2 * stretch_index + 2 * swapped(me ^ r) + (seq_bit ^ e) for r in ORDER for e in (0, 1)
        ]

    query_blocks = block_places(stretch)
    key_blocks = [p for i in range(spread) for p in block_places(i)] if spread > 1 else query_blocks

    scalars = [me, parity, (ctx_me >> 1) & 3, swapped(home >> 1), seq_bit] + query_blocks + key_blocks
    here = jnp.stack([jnp.asarray(v, jnp.int32) for v in scalars])

    low = functools.partial(shape, dtype=BF16)
    x_here, x_there, *qkv_blocks = call(
        start_kernel,
        (low(PIECE, D),) * 2 + (low(OWN + 16, 3 * COLS),) * 4,
        (here, inputs, w_query, w_key, w_value, gain_attn, gain_ffn, bias_table, seq_lengths),
        scratch=(pltpu.VMEM((16, 3 * COLS), F32),) + (pltpu.VMEM((OWN, D), BF16),) * 3
        + (pltpu.VMEM((OWN,), BF16),) * 2 + (pltpu.VMEM((8, H), BF16), pltpu.VMEM((SEQ_DEV,), jnp.int32))
        + (pltpu.SemaphoreType.DMA((9,)),),
        mib=START_MIB,
        in_hbm=8,
    )
    x_near, x_far = to_home((x_here, x_there))

    def group_blocks(values):
        return (values[0],) + tuple(to_partner(values[r], r) for r in (1, 2, 3))

    w_qkv_pieces = group_blocks(qkv_blocks)
    (small, info, bias), (w_qkv,) = run(
        here,
        (
            functools.partial(bias_kernel, float(n_ctx * PIECE)),
            (shape(TP, 16, 3 * COLS), shape(8, 128), shape(HEADS, 5, PIECE, PIECE)),
            w_qkv_pieces,
        ),
        (rows_kernel, (low(D, 3 * COLS),), w_qkv_pieces),
    )
    x_own = (x_near, x_far)
    *teacher_halves, in_own, in_core, in_across = call(
        inner_blocks_kernel,
        (low(PIECE, D),) * 2 + (low(OWN, D),) * 2 + (low(2, OWN // 2, D),),
        (here, after(w_inner, w_qkv), teacher),
    )
    x_y = tuple(to_partner(v, 2) for v in x_own)
    x_y = tuple(after(v, w_qkv) for v in x_y)
    pieces = x_own + x_y + tuple(to_partner(v, 1) for v in x_own + x_y)
    attn_shapes = (shape(COLS, GROUP), shape(8, GROUP), shape(GROUP, D))
    send_job = (send_kernel, (low(2 * ROWS, D),))
    proj_shapes = (low(GROUP, D), low(GROUP, 3 * COLS))

    def attn_scratch(keys, chunk):
        return (pltpu.VMEM((keys, chunk), F32), pltpu.VMEM((keys, chunk), BF16))

    if spread == 1:
        normed, qkv, attn_t, lse, partial = call(
            front_kernel,
            proj_shapes + attn_shapes,
            (here, small) + pieces + (w_qkv, info, bias, w_out),
            scratch=attn_scratch(GROUP, GROUP),
            mib=14,
        )
    else:
        teams = [[s * spread + i for i in range(spread)] for s in range(SEQ_DEV * TP)]
        normed, qkv = call(project_kernel, proj_shapes, (here, small) + pieces + (w_qkv,))
        kv = lax.all_gather(qkv[:, COLS:], "ctx", axis=0, tiled=True, axis_index_groups=teams)
        q = qkv[:, :COLS]
        attn_t, lse, partial = call(
            functools.partial(attention_kernel, 128, (0, COLS)),
            attn_shapes,
            (here, q, kv, info, bias, w_out),
            scratch=attn_scratch(kv.shape[0], 128),
            mib=56,
        )

    def scatter_tail(keep_y, from_core):
        return call(tail_kernel, (low(ROWS, D),), (here, keep_y, from_core))[0]

    from_y = to_partner(after(in_across, *x_y), 2)
    teacher_near, teacher_far = to_home([after(v, *x_y) for v in teacher_halves])
    partial, from_y, teacher_near, teacher_far = lax.optimization_barrier((partial, from_y, teacher_near, teacher_far))
    ((send,),) = run(here, send_job + ((partial,),))
    core = to_partner(send, 1)
    from_x = to_ctx(after(from_y, send), 1)
    in_core = to_partner(after(in_core, send), 1)
    going = scatter_tail(partial, core)
    across = to_partner(going, 2)
    hidden, ffn_low = call(
        hidden_kernel,
        (shape(ROWS, D), low(ROWS, D)),
        (here, small, x_near, x_far, partial, core, across),
    )
    core_y, core_x = to_partner(after(from_y, send), 1), to_partner(after(from_x, ffn_low), 1)
    (w_in,) = call(
        inner_rows_kernel, (low(D, D),), (here, after(in_own, ffn_low), in_core, from_y, from_x, core_y, core_x)
    )

    def gathered(value):
        from_y = to_partner(value, 2)
        return to_partner(value, 1), from_y

    def both_halves(first_call, second_call, value):
        from_core, from_y = gathered(value)
        first, done = first_call((value, from_core))
        core_y = to_partner(after(from_y, done), 1)
        second = second_call((from_y, core_y))
        core_own = to_partner(first[-1], 1)
        going = scatter_tail(second[-2], to_partner(second[-1], 1))
        across = to_partner(going, 2)
        return (value, from_core, from_y, core_y), first, second, (first[-2], core_own, across), going

    half = low(2 * ROWS, D)
    piece_shapes = (shape(ROWS, D), low(ROWS, D))
    def ffn(values):
        return call(ffn_kernel, (half, half) + piece_shapes, (here,) + values + (w_in, w_outer))

    def ffn_first(values):
        outs = ffn(values)
        return outs, outs[-1]

    ffn_all, (active_a, slope_a, *_), (active_b, slope_b, *_), parts, _ = both_halves(ffn_first, ffn, ffn_low)
    out_near, out_far, result_grad, result_low, squares = call(
        functools.partial(loss_kernel, float(token_total)),
        (low(PIECE, D), low(PIECE, D), shape(ROWS, D), low(ROWS, D), shape(1, D)),
        (here, hidden) + parts + (teacher_near, teacher_far, info),
    )

    depth = OWN // n_ctx

    def parts_of(count, rows=DEPTH):
        return low(count, rows, D)

    def ffn_back(values, slope):
        return call(ffn_back_kernel, (half,) + piece_shapes, (here,) + values + (slope, w_in, w_outer))

    def ffn_back_first(values):
        outs = ffn_back(values, slope_a)
        (part,) = call(
            outer_own_kernel, (shape(D, D),), (here, after(active_a, outs[-1])) + values, mib=12
        )
        grads.append(part)
        return outs, part

    def ffn_back_second(values):
        args = (here, grads[0], active_b) + values
        if by_steps:
            outs = (parts_of(4, D // 8),) * 2
            grads[:] = call(outer_halves_kernel, outs, args, scratch=(pltpu.VMEM((D, D), F32),), mib=14)
        else:
            grads[:] = call(outer_kernel, (low(D, D),), args, mib=12)
        return ffn_back((after(values[0], grads[0]), values[1]), slope_b)

    grads = []
    result_all, (inner_a, *_), (inner_b, *_), parts, going = both_halves(
        ffn_back_first, ffn_back_second, result_low
    )
    inner_args = (here,) + ffn_all + (inner_a, after(inner_b, going))
    ahead = []
    if by_steps:
        outer_send, outer_mine = grads
        outer_came = to_ctx(outer_send, 1)
        inner_send, inner_mine = call(
            inner_halves_kernel, (parts_of(4 * TP),) * 2, inner_args, scratch=(pltpu.VMEM((D, D), F32),), mib=14
        )
        ordered = inner_send
        ahead.append((split_low, (parts_of(2, D // 8),) * 2, (outer_mine, outer_came)))
    else:
        (outer_wgrad,) = grads
        (inner_wgrad,) = call(inner_kernel, (low(D, D),), inner_args, mib=14)
        ordered = inner_wgrad
    ((hidden_grad, hidden_low, ffn_gain_grad),) = run(
        here,
        (
            hidden_back_kernel,
            (shape(ROWS, D), low(ROWS, D), shape(1, D)),
            (small, after(hidden, ordered), result_grad) + parts,
        ),
    )
    from_core, from_y = gathered(hidden_low)
    if by_steps:
        body, outs, args = ahead[0]
        ((outer_send, outer_keep),) = run(here, (body, outs, (after(args[0], hidden_low),) + args[1:]))
        outer_came = to_ctx(outer_send, 2)
        from_y = after(from_y, outer_came)
    up_pieces = (hidden_low, from_y, from_core, to_partner(from_y, 1))
    table_shape = shape(HEADS, 5, PIECE, PIECE)
    if by_steps:
        (inner_send, inner_mine), (outer_send, outer_keep) = run(
            here,
            (
                out_grads,
                (parts_of(4 * TP + 4),) * 2,
                (attn_t,) + up_pieces + (inner_send, inner_mine),
            ),
            (split_high, (parts_of(1, D // 8),) * 2, (outer_keep, outer_came)),
            scratch=(pltpu.VMEM((OWN, D), F32),),
        )
        inner_came = to_ctx(inner_send, 1)
        outer_came = to_ctx(outer_send, 4)
        up_pieces = (after(hidden_low, outer_keep),) + up_pieces[1:]
    if spread == 1:
        d_qkv, table_part, partial = call(
            back_kernel,
            (proj_shapes[1], table_shape, shape(GROUP, D)),
            (here, qkv, info, bias, w_out, attn_t, lse, w_qkv) + up_pieces,
            scratch=back_scratch(GROUP, 256),
            mib=20,
        )
    else:
        dq, dkv, table_part = call(
            functools.partial(attention_back_kernel, 128, (0, COLS)),
            (low(GROUP, COLS), low(kv.shape[0], 2 * COLS), table_shape),
            (here, q, kv, info, bias, w_out, attn_t, lse) + up_pieces,
            scratch=back_scratch(kv.shape[0], 128),
            mib=60,
        )
        dkv = lax.psum_scatter(dkv, "ctx", scatter_dimension=0, tiled=True, axis_index_groups=teams)
        d_qkv = jnp.concatenate([dq, dkv], axis=1)
        (partial,) = call(partial_kernel, (shape(GROUP, D),), (here, d_qkv, w_qkv))
    if by_steps:
        (send,), (outer_chunk,), (inner_send, inner_keep) = run(
            here,
            send_job + ((partial,),),
            (finish, (parts_of(1, D // 8),), (outer_keep, outer_came)),
            (split_low, (parts_of(2 * TP + 2),) * 2, (inner_mine, inner_came)),
        )
        outer_came = to_ctx(outer_chunk, 4)
        inner_came = to_ctx(inner_send, 2)
    else:
        ((send,),) = run(here, send_job + ((partial,),))
    core = to_partner(send, 1)
    input_job = (
        input_kernel,
        (low(2, PIECE, D), low(2, PIECE, D)),
        (small, x_near, x_far, hidden_grad, partial, core, out_near, out_far),
    )
    small_shapes = (shape(1, OWN), shape(1, OWN), shape(8, H), shape(1, 1))
    sums_shape = shape(SUM_ROWS, D)
    pair_out = (low(SEQ_DEV, PIECE, D), shape(SEQ_DEV, PIECE, D))
    sum_args = (partial, normed, small, ffn_gain_grad, squares, table_part)

    if by_steps:
        going = scatter_tail(partial, core)
        across = to_partner(going, 2)
        qkv_send, qkv_mine = call(
            qkv_halves_kernel,
            (parts_of(12),) * 2,
            (here, normed, after(d_qkv, going)),
            scratch=(pltpu.VMEM((3, OWN, D), F32),),
        )
        qkv_came = to_ctx(qkv_send, 1)
        inner_keep, across = lax.optimization_barrier((after(inner_keep, qkv_send), across))
        (inner_send, inner_keep), (outer_pair,) = run(
            here,
            (split_high, (parts_of(TP + 1),) * 2, (inner_keep, inner_came)),
            (join_high, (parts_of(2, D // 8),), (outer_chunk, outer_came)),
        )
        inner_came = to_ctx(inner_send, 4)
        outer_came = to_ctx(outer_pair, 2)
        ((in_near, in_far),) = run(
            here, (input_job[0], input_job[1], input_job[2] + (after(across, inner_keep),))
        )
        home_near, home_far = from_home(in_near, in_far)
        ((qkv_send, qkv_keep),) = run(
            here, (split_low, (parts_of(6),) * 2, (after(qkv_mine, in_near), qkv_came))
        )
        qkv_came = to_ctx(qkv_send, 2)
        (sums,) = call(sums_kernel, (sums_shape,), (here, after(partial, qkv_send)) + sum_args[1:])
        inner_blocks, (outer_half,) = run(
            here,
            (
                inner_finish,
                (parts_of(2),) + (parts_of(1 + 1),) * 3,
                (after(inner_keep, qkv_keep), inner_came, sums),
            ),
            (join_low, (parts_of(4, D // 8),), (outer_pair, outer_came)),
        )
        inner_blocks = group_blocks(inner_blocks)
        outer_came = to_ctx(outer_half, 1)
        ((qkv_send, qkv_keep),) = run(
            here, (split_high, (parts_of(3),) * 2, (after(qkv_keep, outer_half), qkv_came))
        )
        qkv_came = to_ctx(qkv_send, 4)
        ((inner_chunk, sums),) = run(
            here,
            (
                inner_collect,
                (parts_of(TP + 1 + 1), sums_shape),
                (after(inner_blocks[0], qkv_keep),) + inner_blocks[1:] + (sums,),
            ),
        )
        inner_came = to_ctx(inner_chunk, 4)
        (qkv_blocks,) = run(
            here, (qkv_finish, (low(3, DEPTH, COLS),) * 4, (after(qkv_keep, inner_chunk), qkv_came))
        )
        qkv_blocks = group_blocks(qkv_blocks)
        (inner_pair, sums), (w_outer_grad,) = run(
            here,
            (
                inner_high,
                (parts_of(2 * TP + 2 + 1), sums_shape),
                (after(inner_chunk, qkv_blocks[0], home_far), inner_came, sums),
            ),
            (outer_rows, (shape(D, D),), (outer_half, outer_came)),
        )
        inner_came = to_ctx(inner_pair, 2)
        ((qkv_chunk,),) = run(
            here, (qkv_collect, (parts_of(3),), (after(qkv_blocks[0], inner_pair),) + qkv_blocks[1:])
        )
        qkv_came = to_ctx(qkv_chunk, 4)
        ((inner_half, sums),) = run(
            here,
            (
                inner_low,
                (parts_of(4 * TP + 4 + 1), sums_shape),
                (after(inner_pair, qkv_chunk), inner_came, sums),
            ),
        )
        inner_came = to_ctx(inner_half, 1)
        ((qkv_pair,),) = run(here, (qkv_high, (parts_of(6),), (after(qkv_chunk, inner_half), qkv_came)))
        qkv_came = to_ctx(qkv_pair, 2)
        ((qkv_half,),) = run(here, (qkv_low, (parts_of(12),), (qkv_pair, qkv_came)))
        qkv_came = to_ctx(qkv_half, 1)
        ((w_inner_grad, w_out_grad, my_attn_gain, my_ffn_gain, my_rows, loss_value),) = run(
            here,
            (
                inner_rows,
                (shape(OWN, TP * D), shape(OWN, D)) + small_shapes,
                (info, after(inner_half, qkv_half), inner_came, sums),
            ),
        )
        (layer_out, input_grad), (w_query_grad, w_key_grad, w_value_grad) = run(
            here,
            (pair_kernel, pair_out, (home_near, home_far)),
            (qkv_rows, (shape(OWN, D),) * 3, (after(qkv_half, w_out_grad), qkv_came)),
        )
    else:
        across = to_partner(scatter_tail(partial, core), 2)
        ((in_near, in_far),) = run(here, (input_job[0], input_job[1], input_job[2] + (across,)))
        ((layer_out, input_grad),) = run(here, (pair_kernel, pair_out, from_home(in_near, in_far)))
        (sums,) = call(sums_kernel, (sums_shape,), (here,) + sum_args)
        (hidden_all,) = call(join_kernel, (low(GROUP, D),), (here,) + up_pieces)
        my_attn_gain, my_ffn_gain, my_rows, loss_value = call(
            small_out_kernel, small_shapes, (here, info, lax.psum(sums, AXES))
        )

        def summed(parts):
            return lax.psum_scatter(parts, "ctx", scatter_dimension=0)

        def inner_to_rows(chunk):
            return swap_blocks(chunk, "wsh").transpose(1, 0, 2).reshape(depth, TP * D)

        def attn_to_rows(chunk):
            blocks = chunk[:3].reshape(3, depth, TP, COLS).transpose(2, 0, 1, 3)
            mine = swap_blocks(blocks, "wsh").transpose(1, 2, 0, 3).reshape(3, depth, D)
            return jnp.concatenate([mine, chunk[3:]])

        (attn_wgrad,) = call(
            attention_grads_kernel, (low(4, OWN, D),), (here, normed, d_qkv, attn_t, hidden_all)
        )
        outer_full = lax.all_gather(summed(outer_wgrad.reshape(n_ctx, D // n_ctx, D)), "ctx")
        inner_parts = inner_wgrad.reshape(TP, n_ctx, depth, D).transpose(1, 0, 2, 3)
        inner_full = lax.all_gather(inner_to_rows(summed(inner_parts)), "ctx")
        attn_parts = attn_wgrad.reshape(4, n_ctx, depth, D).transpose(1, 0, 2, 3)
        attn_full = lax.all_gather(attn_to_rows(summed(attn_parts)), "ctx")
        w_outer_grad = outer_full.reshape(D, D).astype(F32)
        w_inner_grad = inner_full.reshape(OWN, TP * D).astype(F32)
        w_query_grad, w_key_grad, w_value_grad, w_out_grad = (
            attn_full[:, m].reshape(OWN, D).astype(F32) for m in range(4)
        )

    return (
        layer_out,
        loss_value.reshape(()),
        input_grad,
        my_attn_gain.reshape(-1),
        w_query_grad,
        w_key_grad,
        w_value_grad,
        w_out_grad,
        my_rows,
        my_ffn_gain.reshape(-1),
        w_inner_grad,
        w_outer_grad,
    )


def solution(mesh):
    rows = P("wsh", None)
    tokens = P("wsh", "ctx", None)
    return jax.shard_map(
        on_device,
        mesh=mesh,
        in_specs=(tokens, tokens, P("wsh"), P("wsh"), rows, rows, rows, rows, rows, P("wsh"), rows, rows),
        out_specs=(tokens, P(), tokens, P("wsh"), rows, rows, rows, rows, rows, P("wsh"), rows, rows),
        check_vma=False,
    )
```
